32 devices in a mesh: rve: 2 (over x), sub: 16 (over z, y, core).
Axes of the slice: x: 2, y: 2, z: 4, core: 2. Of those that a mesh axis runs over, the one named last changes fastest.
Arguments:
- condensed: float32 [49152, 1536], P(('rve', 'sub')), parts along dimension 0, may hold values from -0.15625 to 0.15625
- eigen_loads: float32 [49152, 128], P(('rve', 'sub')), parts along dimension 0, may hold values from -6 to 6
- coarse_inverse: float32 [1536, 768], P(('rve', 'sub')), parts along dimension 0, may hold values from -0.21875 to 0.21875
- face_rows: int32 [16, 2, 128], P('sub'), may hold values from 0 to 1535, as said below
- primal_rows: int32 [16, 96], P('sub'), may hold values from 0 to 1535, as said below
- primal_slot: int32 [16, 96], P('sub'), may hold values from 0 to 95, each once within a row
Outputs:
- displaced: float32 [49152, 128], P(('rve', 'sub')), parts along dimension 0
- multipliers: float32 [4096, 128], P(('rve', 'sub')), parts along dimension 0
The draws below stay inside these ranges and needn't reach their ends.
There are 2 independent parts, one for each index of `rve`. The reference program is written for one: setup_inputs(seed, part) draws one part's arguments, and reference() takes and returns one part's arrays. A program takes and returns all parts, laid end to end along the dimension named above; an argument that names none is the same for every part. Nothing has to cross between parts.
Inputs may be any that keep to these rules, and one draw needn't show every extreme that they name: `face_rows`: in each subdomain the 128 left-face rows, the 128 right-face rows and the 96 primal rows in primal_rows are all distinct. `primal_rows`: distinct from that subdomain's face rows.
All inputs are finite; a program needn't handle non-finite values.
Results may differ from the reference program's by a relative error of at most 0.0001.
Values sent between devices are 32-bit elements; how exact they have to be, the bound alone decides.
A program may use at most 64 MiB of HBM per device.

```python
import jax
import jax.numpy as jnp
from jax import lax

B = 1536
PR = 96
IF = 128
COLS = 128
ITERS = 3
PC = 48
SUBS = 16
NC = 768


def layout_rows(key):
    keys = jax.random.split(jax.random.fold_in(key, 11), SUBS)
    return jax.vmap(lambda item: jax.random.permutation(item, B))(keys)


def draw_face_rows(key, part):
    perms = layout_rows(key)
    return perms[:, :2 * IF].reshape(SUBS, 2, IF).astype(jnp.int32)


def draw_primal_rows(key, part):
    perms = layout_rows(key)
    return perms[:, 2 * IF:2 * IF + PR].astype(jnp.int32)


def level_of(own_key, extent, cuts, smallest, largest):
    factor_of = 1.0
    for position, parts in cuts:
        draws = jax.random.uniform(jax.random.fold_in(jax.random.fold_in(own_key, 6), position), (parts,), jnp.float32, smallest / len(cuts), largest / len(cuts))
        factor_of = factor_of * jnp.repeat(jnp.exp(draws), extent[position] // parts).reshape((-1,) + (1,) * (len(extent) - 1 - position))
    return factor_of


def normal_values(own_key, dims, spread, bound, cuts=(), held_as=jnp.bfloat16):
    level = level_of(own_key, dims, cuts, -0.22, 0.18) if cuts else 1.0
    array = jax.random.normal(own_key, dims, jnp.float32) * spread * level
    return jnp.minimum(jnp.maximum(array, -bound), bound).astype(held_as)


def setup_inputs(seed: int = 0, part: int = 0) -> dict:
    key_list = jax.random.split(jax.random.key(seed), 7)
    part_splits = jax.random.split(jax.random.fold_in(key_list[6], part), 7)
    return {
        "condensed": normal_values(part_splits[0], (SUBS * B, B), B ** -0.5, 0.15625, ((0, 16),), jnp.float32),
        "eigen_loads": normal_values(part_splits[1], (SUBS * B, COLS), 1.0, 6.0, ((0, 16),), jnp.float32),
        "coarse_inverse": normal_values(part_splits[2], (NC, NC), NC ** -0.5, 0.21875, ((0, 16),), jnp.float32),
        "face_rows": draw_face_rows(jax.random.fold_in(key_list[6], 71), part),
        "primal_rows": draw_primal_rows(jax.random.fold_in(key_list[6], 71), part),
        "primal_slot": jax.vmap(lambda own: jax.random.permutation(own, PR))(jax.random.split(key_list[5], SUBS)).reshape((SUBS, PR)).astype(jnp.int32),
    }


DAMPING = 0.5


def add_faces(loads, right_rows, left_rows, right_term, left_term):
    return loads.at[right_rows].add(-right_term).at[left_rows].add(left_term)


def place_slots(values, slots):
    return jnp.zeros((PR, values.shape[1]), jnp.float32).at[slots].set(values)


def reference(condensed, eigen_loads, coarse_inverse, face_rows, primal_rows, primal_slot):
    blocks = condensed.reshape(SUBS, B, B)
    loads_all = eigen_loads.reshape(SUBS, B, COLS)
    left_rows = face_rows[:, 0, :]
    right_rows = face_rows[:, 1, :]
    prolong = jnp.take_along_axis(blocks, primal_rows[:, None, :], 2)
    multipliers = jnp.zeros((SUBS, IF, COLS), jnp.float32)
    displaced = loads_all
    for step in range(ITERS):
        previous = jnp.roll(multipliers, 1, axis=0)
        loads = jax.vmap(add_faces)(loads_all, right_rows, left_rows, multipliers, previous)
        displaced = jnp.einsum("sij,sjc->sic", blocks, loads, precision=lax.Precision.HIGHEST)
        picked = jnp.take_along_axis(displaced, primal_rows[:, :, None], 1)
        slotted = jax.vmap(place_slots)(picked, primal_slot)
        assembled = slotted[:, :PC] + jnp.roll(slotted[:, PC:], 1, axis=0)
        coarse_sol = jnp.dot(coarse_inverse, assembled.reshape(NC, COLS), precision=lax.Precision.HIGHEST, preferred_element_type=jnp.float32).reshape(SUBS, PC, COLS)
        paired = jnp.concatenate([coarse_sol, jnp.roll(coarse_sol, -1, axis=0)], axis=1)
        gathered = jnp.take_along_axis(paired, primal_slot[:, :, None], 1)
        displaced = displaced - jnp.einsum("sij,sjc->sic", prolong, gathered, precision=lax.Precision.HIGHEST)
        right_vals = jnp.take_along_axis(displaced, right_rows[:, :, None], 1)
        left_vals = jnp.take_along_axis(displaced, left_rows[:, :, None], 1)
        multipliers = multipliers + DAMPING * (right_vals - jnp.roll(left_vals, -1, axis=0))
    return displaced.reshape(SUBS * B, COLS), multipliers.reshape(SUBS * IF, COLS)
```

```python
import functools

import jax
import jax.numpy as jnp
from jax import lax
from jax.experimental import pallas as pl
from jax.experimental.pallas import tpu as pltpu
from jax.sharding import PartitionSpec as P

ITERS = 3
DAMPING = 0.5
VMEM_LIMIT = 67043328
MESH = pl.DeviceIdType.MESH
F32 = jnp.float32
BF16 = jnp.bfloat16
LANES = 128
PLANE_LIMIT = 60 * 1024 * 1024


def grid_of(count):
    chips = count // 2
    inner = 1
    while (2 * inner) ** 2 <= chips and chips % (2 * inner) == 0:
        inner *= 2
    return chips // inner, inner


def flipped(index, mask, count):
    if count & (count - 1):
        return lax.rem(index + count - mask, count)
    out = 0
    bit = 1
    while bit < count:
        own = lax.rem(index // bit, 2)
        out = out + bit * ((1 - own) if mask & bit else own)
        bit *= 2
    return out


def returned(index, mask, count):
    if count & (count - 1):
        return lax.rem(index + mask, count)
    return flipped(index, mask, count)


def split(value):
    high = value.astype(BF16)
    return high, (value - high.astype(F32)).astype(BF16)


def product(high, low, value):
    value_high, value_low = split(value)
    return product_parts(high, low, value_high, value_low)


def product_parts(high, low, value_high, value_low):
    width = value_high.shape[1]
    both = jnp.dot(high, jnp.concatenate([value_high, value_low], axis=1), preferred_element_type=F32)
    return both[:, :width] + both[:, width:] + jnp.dot(low, value_high, preferred_element_type=F32)


def kernel(
    count, primal, width, face_s, prim_s, face_hbm, prim_hbm, slot_hbm, k_hbm, f_hbm, cinv_hbm, pre_ref, kph_ref, kpl_ref, q_ref, lam_ref,
    face_v, prim_v, slot_v, f_ref, cinv_ref, in_sem, k_ref, kh_ref, kl_ref, e_ref, fh_ref, fl_ref, ks_ref, first_ref, ah_ref, al_ref, cols_ref, ch_ref, cl_ref,
    gat_ref, r_ref, send_r, send_l, got_r, got_l, send_ar, send_al, got_ar, got_al,
    k_sem, send_sem, block_sem, face_sem, cinv_send, cinv_recv, a_send, a_recv,
):
    outer, inner = grid_of(count)
    order, columns = f_ref.shape
    owned = primal // 2
    tile = order // k_sem.shape[0]
    padded = e_ref.shape[1]
    me = lax.axis_index("sub")
    core = lax.rem(me, 2)
    y = lax.rem(me // 2, inner)
    z = me // (2 * inner)

    def at(z_, y_, core_):
        return (z_ * inner + y_) * 2 + core_

    def around(steps):
        return lax.rem(me + (steps + count), count)

    def k_copy(c):
        rows = pl.ds(c * tile, tile)
        return pltpu.make_async_copy(k_hbm.at[rows, :], k_ref.at[rows, :], k_sem.at[c])

    held = [
        pltpu.make_async_copy(src, dst, in_sem.at[i])
        for i, (src, dst) in enumerate((
            (f_hbm, f_ref), (cinv_hbm, cinv_ref), (face_hbm, face_v), (prim_hbm, prim_v), (slot_hbm, slot_v)
        ))
    ]
    for copy in held:
        copy.start()
    for c in range(k_sem.shape[0]):
        k_copy(c).start()

    outer_peers = [at(flipped(z, m, outer), y, core) for m in range(1, outer)]
    outer_back = [returned(z, m, outer) for m in range(1, outer)]
    inner_peers = [at(z, flipped(y, m, inner), core) for m in range(1, inner)]
    partner = at(z, y, 1 - core)
    ring = [around(d) for d in (-1, 1)]

    barrier = pltpu.get_barrier_semaphore()
    greeted = outer_peers + inner_peers + [partner] + ring
    if outer & (outer - 1):
        greeted = greeted + [at(b, y, core) for b in outer_back]
    for peer in greeted:
        pl.semaphore_signal(barrier, inc=1, device_id={"sub": peer}, device_id_type=MESH)

    def remote(src, dst, ssem, rsem, peer):
        return pltpu.make_async_remote_copy(
            src_ref=src, dst_ref=dst, send_sem=ssem, recv_sem=rsem, device_id={"sub": peer}, device_id_type=MESH
        )

    cinv_copies = [
        remote(cinv_ref, cols_ref.at[slot], cinv_send.at[slot], cinv_recv.at[slot], around(d))
        for slot, d in ((0, 1), (1, -1))
    ]
    passed_on = remote(cols_ref.at[1], cols_ref.at[2], cinv_send.at[2], cinv_recv.at[2], around(-1))

    for copy in held:
        copy.wait()

    square = (primal, primal)
    eye = lax.broadcasted_iota(jnp.int32, square, 0) == lax.broadcasted_iota(jnp.int32, square, 1)
    prim_col = jnp.sum(jnp.where(eye, prim_v[...].astype(F32), 0.0), axis=1, keepdims=True)
    slot_col = jnp.sum(jnp.where(eye, slot_v[...].astype(F32), 0.0), axis=1, keepdims=True)
    corner_width = padded - 2 * width
    lane = lax.broadcasted_iota(jnp.int32, (primal, corner_width), 1).astype(F32)
    ordered = jnp.sum(jnp.where(slot_col == lane, prim_col + 1.0, 0.0), axis=0, keepdims=True) - 1.0
    ordering = jnp.where(lax.broadcasted_iota(jnp.int32, square, 0) == slot_v[...], 1.0, 0.0).astype(BF16)

    fh, fl = split(f_ref[...])
    fh_ref[...] = fh
    fl_ref[...] = fl

    def stream(first_tile, last_tile):
        @pl.loop(first_tile, last_tile)
        def _(c):
            k_copy(c).wait()
            rows = pl.ds(pl.multiple_of(c * tile, tile), tile)
            high, low = split(k_ref[rows, :])
            kh_ref[rows, :] = high
            kl_ref[rows, :] = low
            pre_ref[rows, :] = product_parts(high, low, fh_ref[...], fl_ref[...])

    half = 1
    stream(0, half)
    pl.semaphore_wait(barrier, len(greeted))
    for copy in cinv_copies:
        copy.start()
    stream(half, order // tile)

    used = 2 * width + primal

    def picked(to_ref, from_ref):
        def rows_of(start, size, row_at):
            @pl.loop(0, size // 8)
            def _(i):
                base = pl.multiple_of(i * 8, 8)
                for j in range(8):
                    to_ref[pl.ds(start + base + j, 1), :] = from_ref[pl.ds(row_at(base + j), 1), :]

        rows_of(0, width, lambda i: face_s[0, 1, i])
        rows_of(width, width, lambda i: face_s[0, 0, i])
        rows_of(2 * width, primal, lambda i: prim_s[0, i])

    def in_order(value):
        high, low = split(value)
        half_width = value.shape[1]
        both = jnp.dot(ordering, jnp.concatenate([high, low], axis=1), preferred_element_type=F32)
        return both[:, :half_width] + both[:, half_width:]

    picked(first_ref, pre_ref)
    empty = jnp.zeros((padded - used, columns), F32)
    first = jnp.concatenate([first_ref[:2 * width], in_order(first_ref[2 * width:used]), empty], axis=0)

    def one_hot_columns():
        right_ids, left_ids = face_v[0, 1:2, :], face_v[0, 0:1, :]
        ordered_ids = ordered.astype(jnp.int32)

        @pl.loop(0, order // tile)
        def _(c):
            rows = pl.ds(pl.multiple_of(c * tile, tile), tile)
            near = lax.broadcasted_iota(jnp.int32, (tile, width), 0) + c * tile
            e_ref[rows, :width] = jnp.where(near == right_ids, 1.0, 0.0).astype(BF16)
            e_ref[rows, width:2 * width] = jnp.where(near == left_ids, 1.0, 0.0).astype(BF16)
            near = lax.broadcasted_iota(jnp.int32, (tile, corner_width), 0) + c * tile
            e_ref[rows, 2 * width:] = jnp.where(near == ordered_ids, 1.0, 0.0).astype(BF16)

    def finish_a():
        one_hot_columns()
        if padded > used:
            ks_ref[used:, :] = jnp.zeros((padded - used, order), F32)
        picked(ks_ref, k_ref)
        high, low = split(ks_ref[...])
        parts = []
        for part, out in ((high, ah_ref), (low, al_ref)):
            found = jnp.dot(part, e_ref[...], preferred_element_type=F32)
            out[:2 * width, :] = found[:2 * width].astype(BF16)
            out[2 * width:used, :] = jnp.dot(
                ordering, found[2 * width:used].astype(BF16), preferred_element_type=F32
            ).astype(BF16)
            if padded > used:
                out[used:, :] = jnp.zeros((padded - used, padded), BF16)
            parts.append(found[:2 * width, 2 * width:])
        corner = parts[0] + parts[1]
        send_ar[...] = corner[:width]
        send_al[...] = corner[width:]

    def primal_columns():
        picks = e_ref[:, 2 * width:]

        @pl.loop(0, order // tile)
        def _(c):
            rows = pl.ds(pl.multiple_of(c * tile, tile), tile)
            kph_ref[rows, :] = jnp.dot(kh_ref[rows, :], picks, preferred_element_type=F32).astype(BF16)
            kpl_ref[rows, :] = jnp.dot(kl_ref[rows, :], picks, preferred_element_type=F32).astype(BF16)

    def uncorrected(changes):
        high, low = split(changes)
        spread = jnp.dot(e_ref[:, :2 * width], jnp.concatenate([high, low], axis=1), preferred_element_type=F32)
        loads = f_ref[...] + (spread[:, :columns] + spread[:, columns:])
        high, low = split(loads)
        fh_ref[...] = high
        fl_ref[...] = low

        @pl.loop(0, order // tile)
        def _(c):
            rows = pl.ds(pl.multiple_of(c * tile, tile), tile)
            pre_ref[rows, :] = product_parts(kh_ref[rows, :], kl_ref[rows, :], fh_ref[...], fl_ref[...])

    a_copies = [
        remote(send_al, got_al, a_send.at[0], a_recv.at[0], around(-1)),
        remote(send_ar, got_ar, a_send.at[1], a_recv.at[1], around(1)),
    ]

    lam = jnp.zeros((width, columns), F32)
    lam_before = jnp.zeros((width, columns), F32)
    values = first
    changes = None
    for step in range(ITERS):
        if step:
            changes = jnp.concatenate([-lam, lam_before], axis=0)
            values = first + product(ah_ref[:, :2 * width], al_ref[:, :2 * width], changes)
        gat = gat_ref.at[step]
        gat_ref[step, me] = values[2 * width:2 * width + primal]
        send_r[step] = values[:width]
        send_l[step] = values[width:2 * width]
        started = []

        def forward(block, peer, part):
            rows = gat.at[block, pl.ds(part * owned, owned)]
            copy = remote(rows, rows, send_sem.at[step, len(started)], block_sem.at[step, block, part], peer)
            copy.start()
            started.append(copy)

        def arrived(block, part):
            rows = gat.at[block, pl.ds(part * owned, owned)]
            remote(rows, rows, send_sem.at[step, 0], block_sem.at[step, block, part], partner).wait_recv()

        for part in range(2):
            for peer in reversed(outer_peers):
                forward(me, peer, part)
            for peer in inner_peers:
                forward(me, peer, part)
            forward(me, partner, part)
        faces = [
            remote(send_l.at[step], got_l.at[step], face_sem.at[0, step, 0], face_sem.at[1, step, 0], around(-1)),
            remote(send_r.at[step], got_r.at[step], face_sem.at[0, step, 1], face_sem.at[1, step, 1], around(1)),
        ]
        for copy in faces:
            copy.start()

        if step == 0:
            cinv_copies[1].wait_recv()
            passed_on.start()
            finish_a()
            for copy in a_copies:
                copy.start()
        if step == 1:
            primal_columns()
        if step == ITERS - 1:
            uncorrected(changes)

        for part in range(2):
            for source in outer_back:
                block = at(source, y, core)
                arrived(block, part)
                for peer in inner_peers:
                    forward(block, peer, part)
                forward(block, partner, part)
        if step == 0:
            cinv_copies[0].wait()
            cinv_copies[1].wait_send()
            passed_on.wait()
            for slot, part in enumerate((cols_ref.at[0], cinv_ref, cols_ref.at[1], cols_ref.at[2])):
                high, low = split(part[...])
                ch_ref[slot * owned:(slot + 1) * owned, :] = high
                cl_ref[slot * owned:(slot + 1) * owned, :] = low
        for part in range(2):
            for m in range(1, inner):
                for source in [z] + outer_back:
                    block = at(source, returned(y, m, inner), core)
                    arrived(block, part)
                    forward(block, partner, part)
        for part in range(2):
            for source in [z] + outer_back:
                for m in range(inner):
                    arrived(at(source, y if m == 0 else returned(y, m, inner), 1 - core), part)

        for s in range(count):
            r_ref[s * owned:(s + 1) * owned, :] = (
                gat_ref[step, s, :owned, :] + gat_ref[step, (s - 1) % count, owned:, :]
            )
        coarse = product(ch_ref[...], cl_ref[...], r_ref[...])
        fill = jnp.zeros((padded - 2 * width - primal, columns), F32)

        def steps_of(slot):
            return jnp.concatenate([coarse[slot * owned:(slot + 2) * owned], fill], axis=0)

        q_before, q_own, q_after = steps_of(0), steps_of(1), steps_of(2)
        own = product(ah_ref[:2 * width, 2 * width:], al_ref[:2 * width, 2 * width:], q_own)
        if step == 0:
            for copy in a_copies:
                copy.wait()
        for copy in faces:
            copy.wait()
        after = product(*split(got_al[...]), q_after)
        lam = lam + DAMPING * ((values[:width] - own[:width]) - (got_l[step] - after))
        if step + 1 < ITERS:
            before = product(*split(got_ar[...]), q_before)
            lam_before = lam_before + DAMPING * ((got_r[step] - before) - (values[width:2 * width] - own[width:]))
        else:
            lam_ref[...] = lam
            q_ref[...] = q_own
        for copy in started:
            copy.wait_send()


def finish(pre_ref, kph_ref, kpl_ref, q_ref, lam_ref, u_ref, lam_out):
    u_ref[...] = pre_ref[...] - product(kph_ref[...], kpl_ref[...], q_ref[...])
    lam_out[...] = lam_ref[...]


NT = (((1,), (1,)), ((), ()))
NN = (((1,), (0,)), ((), ()))


def tall(x, high, low, dims):
    x_high, x_low = split(x)
    count = x.shape[0]
    both = lax.dot_general(jnp.concatenate([x_high, x_low], axis=0), high, dims, preferred_element_type=F32)
    return both[:count] + both[count:] + lax.dot_general(x_high, low, dims, preferred_element_type=F32)


def lanes_of(count):
    return -(-count // LANES) * LANES


def plane_kernel(
    count, primal, width, face_hbm, prim_hbm, slot_hbm, k_hbm, f_hbm, cinv_hbm, pre_ref, kph_ref, kpl_ref, q_ref, lam_ref,
    face_s, prim_s, face_v, prim_v, slot_v, f_ref, k_ref, kh_ref, kl_ref, e_ref, fh_ref, fl_ref, ks_ref,
    own_c, own_b, c_in, b_in, cinv_ref, cqh_ref, cql_ref, ac_ref, ap_ref, ar_ref, before_ref, after_ref,
    ach_ref, acl_ref, aph_ref, apl_ref, arh_ref, arl_ref, r_ref, face_out, face_in, x_out, x_in, q_out, q_in, lam_out, lam_in,
    in_sem, k_sem, c_sem, b_sem, cinv_send, cinv_recv, ac_send, ac_recv, ap_send, ap_recv, ar_send, ar_recv,
    halo_send, halo_recv, edge_sem, r_sem, face_sem, x_sem, q_sem, lam_sem,
):
    outer, inner = grid_of(count)
    plane = 2 * inner
    order, columns = f_ref.shape
    owned = primal // 2
    total = cinv_ref.shape[-1]
    tiles = k_sem.shape[0]
    tile = order // tiles
    share = columns // plane
    both = 2 * width
    wide = lanes_of(primal)
    span = r_ref.shape[-1]
    me = lax.axis_index("sub")
    mine = lax.rem(me, plane)
    z = me // plane
    core = lax.rem(me, 2)

    def at(z_, mine_):
        return z_ * plane + mine_

    partner = at(z, mine + 1 - 2 * core)
    across = [lax.rem(mine + 2 * m, plane) for m in range(1, inner)]
    across_peers = [at(z, other) for other in across]
    others = [lax.rem(mine + m, plane) for m in range(1, plane)]
    mates = [at(z, other) for other in others]
    beyond = [at(lax.rem(z + m, outer), mine) for m in range(1, outer)]
    after, before = beyond[0], beyond[-1]

    def remote(src, dst, ssem, rsem, peer):
        return pltpu.make_async_remote_copy(
            src_ref=src, dst_ref=dst, send_sem=ssem, recv_sem=rsem, device_id={"sub": peer}, device_id_type=MESH
        )

    def send(src, dst, ssem, rsem, peer):
        remote(src, dst, ssem, rsem, peer).start()

    def arrived(ref, rsem):
        remote(ref, ref, r_sem.at[0, 0], rsem, partner).wait_recv()

    def sent(ref, ssem):
        remote(ref, ref, ssem, r_sem.at[0, 1], partner).wait_send()

    ints = [
        pltpu.make_async_copy(src, dst, in_sem.at[i])
        for i, (src, dst) in enumerate((
            (face_hbm, face_s), (prim_hbm, prim_s), (face_hbm, face_v), (prim_hbm, prim_v), (slot_hbm, slot_v)
        ))
    ]
    cinv_copy = pltpu.make_async_copy(cinv_hbm, cinv_ref.at[mine + 1], in_sem.at[5])
    f_copy = pltpu.make_async_copy(f_hbm, f_ref, in_sem.at[6])

    def k_copy(c):
        rows = pl.ds(c * tile, tile)
        return pltpu.make_async_copy(k_hbm.at[rows, :], k_ref.at[rows, :], k_sem.at[c])

    for copy in ints + [cinv_copy, f_copy]:
        copy.start()
    for c in range(tiles):
        k_copy(c).start()

    barrier = pltpu.get_barrier_semaphore()
    for peer in mates + beyond:
        pl.semaphore_signal(barrier, inc=1, device_id={"sub": peer}, device_id_type=MESH)

    with jax.named_scope("P_ints"):
        for copy in ints:
            copy.wait()
    square = (primal, primal)
    eye = lax.broadcasted_iota(jnp.int32, square, 0) == lax.broadcasted_iota(jnp.int32, square, 1)
    prim_col = jnp.sum(jnp.where(eye, prim_v[...].astype(F32), 0.0), axis=1, keepdims=True)
    slot_col = jnp.sum(jnp.where(eye, slot_v[...].astype(F32), 0.0), axis=1, keepdims=True)
    lane = lax.broadcasted_iota(jnp.int32, (primal, wide), 1).astype(F32)
    ordered = jnp.sum(jnp.where(slot_col == lane, prim_col + 1.0, 0.0), axis=0, keepdims=True) - 1.0
    ordering = jnp.where(lax.broadcasted_iota(jnp.int32, (wide, primal), 0) == slot_v[...], 1.0, 0.0).astype(BF16)

    def in_order(value):
        high, low = split(value)
        size = value.shape[1]
        pair = jnp.dot(ordering, jnp.concatenate([high, low], axis=1), preferred_element_type=F32)
        return pair[:, :size] + pair[:, size:]

    def one_hot_columns():
        right_ids, left_ids = face_v[0, 1:2, :], face_v[0, 0:1, :]
        ordered_ids = ordered.astype(jnp.int32)

        @pl.loop(0, tiles)
        def _(c):
            rows = pl.ds(pl.multiple_of(c * tile, tile), tile)
            near = lax.broadcasted_iota(jnp.int32, (tile, width), 0) + c * tile
            e_ref[rows, :width] = jnp.where(near == right_ids, 1.0, 0.0).astype(BF16)
            e_ref[rows, width:both] = jnp.where(near == left_ids, 1.0, 0.0).astype(BF16)
            near = lax.broadcasted_iota(jnp.int32, (tile, wide), 0) + c * tile
            e_ref[rows, both:] = jnp.where(near == ordered_ids, 1.0, 0.0).astype(BF16)

    def spread(buf, ssem, rsem, own):
        for peer in across_peers + [partner]:
            send(buf.at[own], buf.at[own], ssem, rsem.at[own], peer)

    def relay(buf, ssem, rsem, shift=0):
        for other in across:
            block = other + shift
            arrived(buf.at[block], rsem.at[block])
            send(buf.at[block], buf.at[block], ssem, rsem.at[block], partner)

    def settle(buf, rsem, shift=0):
        for other in [mine] + across:
            block = other + 1 - 2 * core + shift
            arrived(buf.at[block], rsem.at[block])

    with jax.named_scope("P_onehot"):
        one_hot_columns()
    with jax.named_scope("P_barrier"):
        pl.semaphore_wait(barrier, len(mates + beyond))
        cinv_copy.wait()
    spread(cinv_ref, cinv_send, cinv_recv, mine + 1)

    with jax.named_scope("P_f"):
        f_copy.wait()
        high, low = split(f_ref[...])
        fh_ref[...] = high
        fl_ref[...] = low

    def halve(first_tile, last_tile):
        @pl.loop(first_tile, last_tile)
        def _(c):
            rows = pl.ds(pl.multiple_of(c * tile, tile), tile)
            high, low = split(k_ref[rows, :])
            kh_ref[rows, :] = high
            kl_ref[rows, :] = low

    with jax.named_scope("P_kwait"):
        for c in range(tiles):
            k_copy(c).wait()

    def picked(start, size, row_at):
        @pl.loop(0, size // 8)
        def _(i):
            base = pl.multiple_of(i * 8, 8)
            for j in range(8):
                ks_ref[pl.ds(start + base + j, 1), :] = k_ref[pl.ds(row_at(base + j), 1), :]

    def first(rows):
        high, low = split(ks_ref[rows, :])
        return product_parts(high, low, fh_ref[...], fl_ref[...])

    with jax.named_scope("P_first"):
        picked(both, primal, lambda i: prim_s[0, i])
        own_c[...] = in_order(first(slice(both, both + primal))).T.reshape(own_c.shape)
        for other, peer in zip(others, mates):
            send(own_c.at[other], c_in.at[mine], c_sem.at[0], c_sem.at[1], peer)
        c_in[mine] = own_c[mine]
    with jax.named_scope("P_firstb"):
        picked(0, width, lambda i: face_s[0, 1, i])
        picked(width, width, lambda i: face_s[0, 0, i])
        loads = first(slice(0, both))
        own_b[:, :, :width] = loads[:width].T.reshape(plane, share, width)
        own_b[:, :, width:] = loads[width:].T.reshape(plane, share, width)
        for other, peer in zip(others, mates):
            send(own_b.at[other], b_in.at[mine], b_sem.at[0], b_sem.at[1], peer)
        b_in[mine] = own_b[mine]
    def assembled(parts):
        sums = None
        for i, part in enumerate(parts):
            part = jnp.concatenate([part, jnp.zeros((share, span - wide), F32)], axis=1)
            part = pltpu.roll(part, owned * i, 1) if i else part
            sums = part if sums is None else sums + part
        return sums

    def publish(step, parts):
        r_ref[step, z] = assembled(parts)
        for peer in reversed(beyond):
            rows = r_ref.at[step, z]
            send(rows, rows, r_sem.at[step, 0], r_sem.at[step, 1], peer)

    def faces(step, last_right, first_left):
        face_out[step, 0] = first_left
        send(face_out.at[step, 0], face_in.at[step, 0], face_sem.at[step, 0], face_sem.at[step, 1], before)
        if step + 1 < ITERS:
            face_out[step, 1] = last_right
            send(face_out.at[step, 1], face_in.at[step, 1], face_sem.at[step, 0], face_sem.at[step, 1], after)

    def face_part(ref, step):
        return ref.at[step] if step + 1 < ITERS else ref.at[step, pl.ds(0, 1)]

    def columns_of(rows, picks):
        high, low = split(ks_ref[rows, :])
        return jnp.dot(high, picks, preferred_element_type=F32) + jnp.dot(low, picks, preferred_element_type=F32)

    def primal_columns(first_tile, last_tile):
        picks = e_ref[:, both:]

        @pl.loop(first_tile, last_tile)
        def _(c):
            rows = pl.ds(pl.multiple_of(c * tile, tile), tile)
            kph_ref[rows, :] = jnp.dot(kh_ref[rows, :], picks, preferred_element_type=F32).astype(BF16)
            kpl_ref[rows, :] = jnp.dot(kl_ref[rows, :], picks, preferred_element_type=F32).astype(BF16)

    def coarse_rows(blocks):
        for b in blocks:
            high, low = split(cinv_ref[b])
            for pair, half in ((b, 0), (b - 1, 1)):
                if 0 <= pair < plane + 2:
                    start = pair * wide + half * owned
                    cqh_ref[start:start + owned, :] = high
                    cql_ref[start:start + owned, :] = low

    def halves_of(refs, src):
        for i in range(plane):
            for ref, part in zip(refs, split(src[i])):
                ref[i, :primal, :] = part
                ref[i, primal:, :] = jnp.zeros((wide - primal, both), BF16)

    with jax.named_scope("P_ac"):
        found = columns_of(slice(0, both), e_ref[:, both:])
        ac_ref[mine, :, :width] = found[:width].T[:primal]
        ac_ref[mine, :, width:] = found[width:].T[:primal]
        spread(ac_ref, ac_send, ac_recv, mine)
    with jax.named_scope("P_relayc"):
        relay(cinv_ref, cinv_send, cinv_recv, 1)
    with jax.named_scope("P_cwait"):
        arrived(c_in.at[pl.ds(0, plane - 1)], c_sem.at[1])
    publish(0, [c_in[i] for i in range(plane)])
    with jax.named_scope("P_ap"):
        ap_ref[mine] = in_order(columns_of(slice(both, both + primal), e_ref[:, :both]))[:primal]
        spread(ap_ref, ap_send, ap_recv, mine)
    with jax.named_scope("P_halo"):
        settle(cinv_ref, cinv_recv, 1)
        halves = owned // 2
        near = cinv_ref.at[0, pl.ds(core * halves, halves)]
        far = cinv_ref.at[plane + 1 + core]
        send(cinv_ref.at[1 + core], far, halo_send.at[0], halo_recv.at[0], before)
        send(cinv_ref.at[plane, pl.ds(core * halves, halves)], near, halo_send.at[1], halo_recv.at[1], after)
    with jax.named_scope("P_bwait"):
        arrived(b_in.at[pl.ds(0, plane - 1)], b_sem.at[1])
    faces(0, b_in[plane - 1, :, :width], b_in[0, :, width:])

    urgent = jnp.where(mine == 0, 1, 0)

    def spread_half(half):
        for peer in across_peers + [partner]:
            rows = ar_ref.at[mine, half]
            send(rows, rows, ar_send, ar_recv.at[mine, half], peer)

    def relay_half(flip):
        for other in across:
            half = jnp.where(other == 0, 1 - flip, flip)
            rows = ar_ref.at[other, half]
            arrived(rows, ar_recv.at[other, half])
            send(rows, rows, ar_send, ar_recv.at[other, half], partner)

    def settle_half(flip):
        for other in [mine] + across:
            block = other + 1 - 2 * core
            half = jnp.where(block == 0, 1 - flip, flip)
            arrived(ar_ref.at[block, half], ar_recv.at[block, half])

    with jax.named_scope("P_ar"):
        found = columns_of(slice(0, both), e_ref[:, :both])
        ar_ref[mine, 0] = found[:width]
        ar_ref[mine, 1] = found[width:]
    with jax.named_scope("P_halve"):
        halve(0, tiles)
    with jax.named_scope("P_cq"):
        for ref in (cqh_ref, cql_ref):
            for pair in range(plane + 2):
                ref[pair * wide + primal:(pair + 1) * wide, :] = jnp.zeros((wide - primal, total), BF16)
        coarse_rows(range(1, plane + 1))
    with jax.named_scope("P_relayac"):
        relay(ac_ref, ac_send, ac_recv)
        spread_half(urgent)
    with jax.named_scope("P_settleac"):
        settle(ac_ref, ac_recv)
        send(ac_ref.at[plane - 1, :, pl.ds(0, width)], before_ref, edge_sem.at[0], edge_sem.at[1], after)
        send(ac_ref.at[0, :, pl.ds(width, width)], after_ref, edge_sem.at[0], edge_sem.at[2], before)
        halves_of((ach_ref, acl_ref), ac_ref)
    with jax.named_scope("P_halo2"):
        arrived(far, halo_recv.at[0])
        send(far, far, halo_send.at[0], halo_recv.at[2], partner)
        arrived(near, halo_recv.at[1])
        send(near, near, halo_send.at[1], halo_recv.at[3], partner)
    with jax.named_scope("P_relayap"):
        relay(ap_ref, ap_send, ap_recv)
        spread_half(1 - urgent)
    half_tiles = tiles // 2
    with jax.named_scope("P_halo3"):
        other_near = cinv_ref.at[0, pl.ds((1 - core) * halves, halves)]
        other_far = cinv_ref.at[plane + 2 - core]
        arrived(other_far, halo_recv.at[2])
        arrived(other_near, halo_recv.at[3])
        coarse_rows([0, plane + 1, plane + 2])

    def uncorrected(first_tile, last_tile):
        @pl.loop(first_tile, last_tile)
        def _(c):
            rows = pl.ds(pl.multiple_of(c * tile, tile), tile)
            pre_ref[rows, :] = product_parts(kh_ref[rows, :], kl_ref[rows, :], fh_ref[...], fl_ref[...])

    def changed_loads():
        high, low = split(x_in[...].reshape(columns, both))
        moved = lax.dot_general(
            e_ref[:, :both], jnp.concatenate([high, low], axis=0), NT, preferred_element_type=F32
        )
        high, low = split(f_ref[...] + (moved[:, :columns] + moved[:, columns:]))
        fh_ref[...] = high
        fl_ref[...] = low

    def padded(value):
        return jnp.concatenate([value, jnp.zeros((wide - primal, value.shape[1]), F32)], axis=0)

    lam = [jnp.zeros((share, width), F32)] * (plane + 1)
    values = [b_in[i] for i in range(plane)]
    edges = None
    for step in range(ITERS):
        if step == ITERS - 1:
            with jax.named_scope("P_xwait"):
                arrived(x_in.at[pl.ds(0, plane - 1)], x_sem.at[1])
                changed_loads()
            with jax.named_scope("P_uncorr0"):
                uncorrected(0, half_tiles)
        with jax.named_scope(f"P_rwait{step}"):
            arrived(r_ref.at[step, pl.ds(0, outer - 1)], r_sem.at[step, 1])
        with jax.named_scope(f"P_coarse{step}"):
            sums = None
            for i in range(outer):
                part = jnp.concatenate([r_ref[step, i], jnp.zeros((share, total - span), F32)], axis=1)
                part = pltpu.roll(part, plane * owned * i, 1) if i else part
                sums = part if sums is None else sums + part
            coarse = tall(sums, cqh_ref[...], cql_ref[...], NT)
            steps = [coarse[:, i * wide:(i + 1) * wide] for i in range(plane + 2)]
            if step == ITERS - 1:
                for i in range(plane):
                    q_out[i] = steps[i + 1]
                for other, peer in zip(others, mates):
                    send(q_out.at[other], q_in.at[mine], q_sem.at[0], q_sem.at[1], peer)
                q_in[mine] = q_out[mine]
        if edges is None:
            with jax.named_scope("P_edge"):
                arrived(before_ref, edge_sem.at[1])
                arrived(after_ref, edge_sem.at[2])
                edges = [split(padded(ref[...])) for ref in (before_ref, after_ref)]
        with jax.named_scope(f"P_faces{step}"):
            arrived(face_part(face_in, step), face_sem.at[step, 1])
        with jax.named_scope(f"P_update{step}"):
            moved = [values[i] - tall(steps[i + 1], ach_ref[i], acl_ref[i], NN) for i in range(plane)]
            right = [part[:, :width] for part in moved]
            left = [part[:, width:] for part in moved]
            left.append(face_in[step, 0] - tall(steps[plane + 1], *edges[1], NN))
            lam_next = [lam[i + 1] + DAMPING * (right[i] - left[i + 1]) for i in range(plane)]
            if step + 1 < ITERS:
                ahead = face_in[step, 1] - tall(steps[0], *edges[0], NN)
                lam_next = [lam[0] + DAMPING * (ahead - left[0])] + lam_next
            else:
                for i in range(plane):
                    lam_out[i] = lam_next[i]
                for other, peer in zip(others, mates):
                    send(lam_out.at[other], lam_in.at[mine], lam_sem.at[0], lam_sem.at[1], peer)
                lam_in[mine] = lam_out[mine]
                break
            lam = lam_next
            if step == 0:
                with jax.named_scope("P_settleap"):
                    settle(ap_ref, ap_recv)
                    halves_of((aph_ref, apl_ref), ap_ref)
            changes = [jnp.concatenate([-lam[i + 1], lam[i]], axis=1) for i in range(plane)]
            publish(step + 1, [
                c_in[i] + tall(changes[i], aph_ref[i], apl_ref[i], NT) for i in range(plane)
            ])
            if step == ITERS - 2:
                for i in range(plane):
                    x_out[i] = changes[i]
                for other, peer in zip(others, mates):
                    send(x_out.at[other], x_in.at[mine], x_sem.at[0], x_sem.at[1], peer)
                x_in[mine] = x_out[mine]
        if step == 0:
            with jax.named_scope("P_relayr0"):
                relay_half(0)
                settle_half(0)
                for i, half in ((plane - 1, 0), (0, 1)):
                    rows = slice(half * width, (half + 1) * width)
                    for ref, part in zip((arh_ref, arl_ref), split(ar_ref[i, half])):
                        ref[i, rows] = part
            with jax.named_scope("P_facevalues"):
                last_right = tall(changes[-1], arh_ref[plane - 1, :width], arl_ref[plane - 1, :width], NT)
                first_left = tall(changes[0], arh_ref[0, width:], arl_ref[0, width:], NT)
                faces(1, b_in[plane - 1, :, :width] + last_right, b_in[0, :, width:] + first_left)
            with jax.named_scope("P_primcol"):
                primal_columns(0, half_tiles)
            with jax.named_scope("P_relayr1"):
                relay_half(1)
            with jax.named_scope("P_primcol"):
                primal_columns(half_tiles, tiles)
            with jax.named_scope("P_settler1"):
                settle_half(1)
                for i in range(plane):
                    for half in range(2):
                        if (i, half) not in ((plane - 1, 0), (0, 1)):
                            rows = slice(half * width, (half + 1) * width)
                            for ref, part in zip((arh_ref, arl_ref), split(ar_ref[i, half])):
                                ref[i, rows] = part
        with jax.named_scope(f"P_values{step}"):
            values = [b_in[i] + tall(changes[i], arh_ref[i], arl_ref[i], NT) for i in range(plane)]
            if step:
                faces(step + 1, values[plane - 1][:, :width], values[0][:, width:])

    with jax.named_scope("P_uncorr1"):
        uncorrected(half_tiles, tiles)
    with jax.named_scope("P_qwait"):
        arrived(q_in.at[pl.ds(0, plane - 1)], q_sem.at[1])
        q_ref[...] = q_in[...].reshape(q_ref.shape)
    with jax.named_scope("P_lamwait"):
        arrived(lam_in.at[pl.ds(0, plane - 1)], lam_sem.at[1])
        lam_ref[...] = lam_in[...].reshape(lam_ref.shape)
    with jax.named_scope("P_sent"):
        others_part = pl.ds(0, plane - 1)
        sent(own_c.at[others_part], c_sem.at[0])
        sent(own_b.at[others_part], b_sem.at[0])
        sent(cinv_ref.at[others_part], cinv_send)
        for ref, sem in ((ac_ref, ac_send), (ap_ref, ap_send), (ar_ref, ar_send)):
            sent(ref.at[others_part], sem)
        sent(cinv_ref.at[pl.ds(0, 2)], halo_send.at[0])
        sent(cinv_ref.at[0], halo_send.at[1])
        sent(ac_ref.at[0], edge_sem.at[0])
        for step in range(ITERS):
            sent(r_ref.at[step, pl.ds(0, outer - 1)], r_sem.at[step, 0])
            sent(face_part(face_out, step), face_sem.at[step, 0])
        sent(x_out.at[others_part], x_sem.at[0])
        sent(q_out.at[others_part], q_sem.at[0])
        sent(lam_out.at[others_part], lam_sem.at[0])


def plane_finish(pre_ref, kph_ref, kpl_ref, q_ref, lam_ref, u_ref, lam_out):
    high, low = split(q_ref[...])
    columns = high.shape[0]
    both = lax.dot_general(kph_ref[...], jnp.concatenate([high, low], axis=0), NT, preferred_element_type=F32)
    both = both[:, :columns] + both[:, columns:]
    u_ref[...] = pre_ref[...] - (both + lax.dot_general(kpl_ref[...], high, NT, preferred_element_type=F32))
    lam_out[...] = lam_ref[...].T


def size_of(buffers):
    return sum((4 if kind == F32 else 2) * functools.reduce(lambda a, b: a * b, size) for size, kind in buffers)


def plane_scratch(count, order, columns, owned, total, width, primal):
    outer, inner = grid_of(count)
    plane = 2 * inner
    both = 2 * width
    wide = lanes_of(primal)
    span = lanes_of((plane + 1) * owned)
    share = columns // plane
    pairs = (plane + 2) * wide
    return plane, [
        ((order, columns), F32),
        ((order, order), F32),
        ((order, order), BF16),
        ((order, order), BF16),
        ((order, both + wide), BF16),
        ((order, columns), BF16),
        ((order, columns), BF16),
        ((both + primal, order), F32),
        ((plane, share, wide), F32),
        ((plane, share, both), F32),
        ((plane, share, wide), F32),
        ((plane, share, both), F32),
        ((plane + 3, owned, total), F32),
        ((pairs, total), BF16),
        ((pairs, total), BF16),
        ((plane, primal, both), F32),
        ((plane, primal, both), F32),
        ((plane, 2, width, both), F32),
        ((primal, width), F32),
        ((primal, width), F32),
        ((plane, wide, both), BF16),
        ((plane, wide, both), BF16),
        ((plane, wide, both), BF16),
        ((plane, wide, both), BF16),
        ((plane, both, both), BF16),
        ((plane, both, both), BF16),
        ((ITERS, outer, share, span), F32),
        ((ITERS, 2, share, width), F32),
        ((ITERS, 2, share, width), F32),
        ((plane, share, both), F32),
        ((plane, share, both), F32),
        ((plane, share, wide), F32),
        ((plane, share, wide), F32),
        ((plane, share, width), F32),
        ((plane, share, width), F32),
    ]


def planar(condensed, eigen_loads, coarse_inverse, face_rows, primal_rows, primal_slot):
    count = lax.axis_size("sub")
    order, columns = eigen_loads.shape
    owned, total = coarse_inverse.shape
    width = face_rows.shape[2]
    primal = primal_rows.shape[1]
    outer, inner = grid_of(count)
    tile = 256 if order % 256 == 0 else order
    tiles = order // tile
    plane, buffers = plane_scratch(count, order, columns, owned, total, width, primal)
    needed = size_of(buffers)
    wide = lanes_of(primal)
    dma = pltpu.SemaphoreType.DMA
    vmem = pl.BlockSpec(memory_space=pltpu.VMEM)
    shape = jax.ShapeDtypeStruct
    held = [
        pltpu.with_memory_space_constraint(value, pltpu.HBM)
        for value in (face_rows, primal_rows, primal_slot, condensed, eigen_loads, coarse_inverse)
    ]
    parts = pl.pallas_call(
        functools.partial(plane_kernel, count, primal, width),
        out_shape=(
            shape((order, columns), F32),
            shape((order, wide), BF16),
            shape((order, wide), BF16),
            shape((columns, wide), F32),
            shape((columns, width), F32),
        ),
        in_specs=[pl.BlockSpec(memory_space=pltpu.HBM)] * 6,
        out_specs=(vmem,) * 5,
        scratch_shapes=[
            pltpu.SMEM(face_rows.shape, jnp.int32),
            pltpu.SMEM(primal_rows.shape, jnp.int32),
            pltpu.VMEM(face_rows.shape, jnp.int32),
            pltpu.VMEM(primal_rows.shape, jnp.int32),
            pltpu.VMEM(primal_slot.shape, jnp.int32),
        ] + [pltpu.VMEM(size, kind) for size, kind in buffers] + [
            dma((7,)),
            dma((tiles,)),
            dma((2,)),
            dma((2,)),
            dma(()),
            dma((plane + 1,)),
            dma(()),
            dma((plane,)),
            dma(()),
            dma((plane,)),
            dma(()),
            dma((plane, 2)),
            dma((2,)),
            dma((4,)),
            dma((3,)),
            dma((ITERS, 2)),
            dma((ITERS, 2)),
            dma((2,)),
            dma((2,)),
            dma((2,)),
        ],
        compiler_params=pltpu.CompilerParams(
            collective_id=0, has_side_effects=True, vmem_limit_bytes=min(PLANE_LIMIT, needed + needed // 3)
        ),
    )(*held)
    return pl.pallas_call(
        plane_finish,
        out_shape=(shape((order, columns), F32), shape((width, columns), F32)),
        in_specs=[vmem] * 5,
        out_specs=(vmem, vmem),
        compiler_params=pltpu.CompilerParams(vmem_limit_bytes=4 * order * columns * 8),
    )(*parts)


def fits_plane(condensed, eigen_loads, coarse_inverse, face_rows, primal_rows, primal_slot):
    count = lax.axis_size("sub")
    order, columns = eigen_loads.shape
    owned, total = coarse_inverse.shape
    width = face_rows.shape[2]
    primal = primal_rows.shape[1]
    outer, inner = grid_of(count)
    plane = 2 * inner
    if outer < 2 or columns % (8 * plane) or total % LANES or width % LANES or owned % 16 or primal != 2 * owned:
        return False
    _, buffers = plane_scratch(count, order, columns, owned, total, width, primal)
    return size_of(buffers) <= PLANE_LIMIT * 3 // 4


def local(*values):
    return (planar if fits_plane(*values) else general)(*values)


def general(condensed, eigen_loads, coarse_inverse, face_rows, primal_rows, primal_slot):
    count = lax.axis_size("sub")
    order, columns = eigen_loads.shape
    owned, total = coarse_inverse.shape
    width = face_rows.shape[2]
    primal = primal_rows.shape[1]
    padded = 2 * width + -(-primal // LANES) * LANES
    outer, inner = grid_of(count)
    corner_width = padded - 2 * width
    tile = 256 if order % 256 == 0 else order
    sends = (outer - 1) + (inner - 1) * outer + outer * inner
    dma = pltpu.SemaphoreType.DMA
    vmem = pl.BlockSpec(memory_space=pltpu.VMEM)
    face = pltpu.VMEM((ITERS, width, columns), F32)
    corner = pltpu.VMEM((width, padded - 2 * width), F32)
    smem = pl.BlockSpec(memory_space=pltpu.SMEM)
    needed = 8 * order * (order + padded + 2 * columns) + 4 * padded * (order + columns + padded)
    needed += 4 * owned * total * 8 + 4 * columns * (ITERS * (count * primal + 4 * width) + total)
    needed += 4 * order * (columns + 2 * corner_width) + 4 * columns * (order + 8 * width)
    shape = jax.ShapeDtypeStruct
    held = [
        pltpu.with_memory_space_constraint(value, pltpu.HBM)
        for value in (face_rows, primal_rows, primal_slot, condensed, eigen_loads, coarse_inverse)
    ]
    parts = pl.pallas_call(
        functools.partial(kernel, count, primal, width),
        out_shape=(
            shape((order, columns), F32),
            shape((order, corner_width), BF16),
            shape((order, corner_width), BF16),
            shape((corner_width, columns), F32),
            shape((width, columns), F32),
        ),
        in_specs=[smem, smem] + [pl.BlockSpec(memory_space=pltpu.HBM)] * 6,
        out_specs=(vmem,) * 5,
        scratch_shapes=[
            pltpu.VMEM(face_rows.shape, jnp.int32),
            pltpu.VMEM(primal_rows.shape, jnp.int32),
            pltpu.VMEM(primal_slot.shape, jnp.int32),
            pltpu.VMEM((order, columns), F32),
            pltpu.VMEM((owned, total), F32),
            dma((5,)),
            pltpu.VMEM((order, order), F32),
            pltpu.VMEM((order, order), BF16),
            pltpu.VMEM((order, order), BF16),
            pltpu.VMEM((order, padded), BF16),
            pltpu.VMEM((order, columns), BF16),
            pltpu.VMEM((order, columns), BF16),
            pltpu.VMEM((padded, order), F32),
            pltpu.VMEM((padded, columns), F32),
            pltpu.VMEM((padded, padded), BF16),
            pltpu.VMEM((padded, padded), BF16),
            pltpu.VMEM((3, owned, total), F32),
            pltpu.VMEM((4 * owned, total), BF16),
            pltpu.VMEM((4 * owned, total), BF16),
            pltpu.VMEM((ITERS, count, primal, columns), F32),
            pltpu.VMEM((total, columns), F32),
            face, face, face, face,
            corner, corner, corner, corner,
            dma((order // tile,)),
            dma((ITERS, 2 * sends)),
            dma((ITERS, count, 2)),
            dma((2, ITERS, 2)),
            dma((3,)),
            dma((3,)),
            dma((2,)),
            dma((2,)),
        ],
        compiler_params=pltpu.CompilerParams(
            collective_id=0, has_side_effects=True, vmem_limit_bytes=min(VMEM_LIMIT, needed + needed // 4)
        ),
    )(face_rows, primal_rows, *held)
    return pl.pallas_call(
        finish,
        out_shape=(shape((order, columns), F32), shape((width, columns), F32)),
        in_specs=[vmem] * 5,
        out_specs=(vmem, vmem),
        compiler_params=pltpu.CompilerParams(vmem_limit_bytes=4 * order * columns * 8),
    )(*parts)


def solution(mesh):
    placed = (
        P(("rve", "sub"), None),
        P(("rve", "sub"), None),
        P(("rve", "sub"), None),
        P("sub", None, None),
        P("sub", None),
        P("sub", None),
    )
    return jax.shard_map(
        local,
        mesh=mesh,
        in_specs=placed,
        out_specs=(P(("rve", "sub"), None), P(("rve", "sub"), None)),
        check_vma=False,
    )
```

```python
import functools

import jax
import jax.numpy as jnp
from jax import lax
from jax.experimental import pallas as pl
from jax.experimental.pallas import tpu as pltpu
from jax.sharding import PartitionSpec as P

ITERS = 3
DAMPING = 0.5
VMEM_LIMIT = 67043328
MESH = pl.DeviceIdType.MESH
F32 = jnp.float32
BF16 = jnp.bfloat16
LANES = 128
PLANE_LIMIT = 60 * 1024 * 1024


def grid_of(count):
    chips = count // 2
    inner = 1
    while (2 * inner) ** 2 <= chips and chips % (2 * inner) == 0:
        inner *= 2
    return chips // inner, inner


def flipped(index, mask, count):
    if count & (count - 1):
        return lax.rem(index + count - mask, count)
    out = 0
    bit = 1
    while bit < count:
        own = lax.rem(index // bit, 2)
        out = out + bit * ((1 - own) if mask & bit else own)
        bit *= 2
    return out


def returned(index, mask, count):
    if count & (count - 1):
        return lax.rem(index + mask, count)
    return flipped(index, mask, count)


def split(value):
    high = value.astype(BF16)
    return high, (value - high.astype(F32)).astype(BF16)


def product(high, low, value):
    value_high, value_low = split(value)
    return product_parts(high, low, value_high, value_low)


def product_parts(high, low, value_high, value_low):
    width = value_high.shape[1]
    both = jnp.dot(high, jnp.concatenate([value_high, value_low], axis=1), preferred_element_type=F32)
    return both[:, :width] + both[:, width:] + jnp.dot(low, value_high, preferred_element_type=F32)


def kernel(
    count, primal, width, face_s, prim_s, face_hbm, prim_hbm, slot_hbm, k_hbm, f_hbm, cinv_hbm, pre_ref, kph_ref, kpl_ref, q_ref, lam_ref,
    face_v, prim_v, slot_v, f_ref, cinv_ref, in_sem, k_ref, kh_ref, kl_ref, e_ref, fh_ref, fl_ref, ks_ref, first_ref, ah_ref, al_ref, cols_ref, ch_ref, cl_ref,
    gat_ref, r_ref, send_r, send_l, got_r, got_l, send_ar, send_al, got_ar, got_al,
    k_sem, send_sem, block_sem, face_sem, cinv_send, cinv_recv, a_send, a_recv,
):
    outer, inner = grid_of(count)
    order, columns = f_ref.shape
    owned = primal // 2
    tile = order // k_sem.shape[0]
    padded = e_ref.shape[1]
    me = lax.axis_index("sub")
    core = lax.rem(me, 2)
    y = lax.rem(me // 2, inner)
    z = me // (2 * inner)

    def at(z_, y_, core_):
        return (z_ * inner + y_) * 2 + core_

    def around(steps):
        return lax.rem(me + (steps + count), count)

    def k_copy(c):
        rows = pl.ds(c * tile, tile)
        return pltpu.make_async_copy(k_hbm.at[rows, :], k_ref.at[rows, :], k_sem.at[c])

    held = [
        pltpu.make_async_copy(src, dst, in_sem.at[i])
        for i, (src, dst) in enumerate((
            (f_hbm, f_ref), (cinv_hbm, cinv_ref), (face_hbm, face_v), (prim_hbm, prim_v), (slot_hbm, slot_v)
        ))
    ]
    for copy in held:
        copy.start()
    for c in range(k_sem.shape[0]):
        k_copy(c).start()

    outer_peers = [at(flipped(z, m, outer), y, core) for m in range(1, outer)]
    outer_back = [returned(z, m, outer) for m in range(1, outer)]
    inner_peers = [at(z, flipped(y, m, inner), core) for m in range(1, inner)]
    partner = at(z, y, 1 - core)
    ring = [around(d) for d in (-1, 1)]

    barrier = pltpu.get_barrier_semaphore()
    greeted = outer_peers + inner_peers + [partner] + ring
    if outer & (outer - 1):
        greeted = greeted + [at(b, y, core) for b in outer_back]
    for peer in greeted:
        pl.semaphore_signal(barrier, inc=1, device_id={"sub": peer}, device_id_type=MESH)

    def remote(src, dst, ssem, rsem, peer):
        return pltpu.make_async_remote_copy(
            src_ref=src, dst_ref=dst, send_sem=ssem, recv_sem=rsem, device_id={"sub": peer}, device_id_type=MESH
        )

    cinv_copies = [
        remote(cinv_ref, cols_ref.at[slot], cinv_send.at[slot], cinv_recv.at[slot], around(d))
        for slot, d in ((0, 1), (1, -1))
    ]
    passed_on = remote(cols_ref.at[1], cols_ref.at[2], cinv_send.at[2], cinv_recv.at[2], around(-1))

    for copy in held:
        copy.wait()

    square = (primal, primal)
    eye = lax.broadcasted_iota(jnp.int32, square, 0) == lax.broadcasted_iota(jnp.int32, square, 1)
    prim_col = jnp.sum(jnp.where(eye, prim_v[...].astype(F32), 0.0), axis=1, keepdims=True)
    slot_col = jnp.sum(jnp.where(eye, slot_v[...].astype(F32), 0.0), axis=1, keepdims=True)
    corner_width = padded - 2 * width
    lane = lax.broadcasted_iota(jnp.int32, (primal, corner_width), 1).astype(F32)
    ordered = jnp.sum(jnp.where(slot_col == lane, prim_col + 1.0, 0.0), axis=0, keepdims=True) - 1.0
    ordering = jnp.where(lax.broadcasted_iota(jnp.int32, square, 0) == slot_v[...], 1.0, 0.0).astype(BF16)

    fh, fl = split(f_ref[...])
    fh_ref[...] = fh
    fl_ref[...] = fl

    def stream(first_tile, last_tile):
        @pl.loop(first_tile, last_tile)
        def _(c):
            k_copy(c).wait()
            rows = pl.ds(pl.multiple_of(c * tile, tile), tile)
            high, low = split(k_ref[rows, :])
            kh_ref[rows, :] = high
            kl_ref[rows, :] = low
            pre_ref[rows, :] = product_parts(high, low, fh_ref[...], fl_ref[...])

    half = 1
    stream(0, half)
    pl.semaphore_wait(barrier, len(greeted))
    for copy in cinv_copies:
        copy.start()
    stream(half, order // tile)

    used = 2 * width + primal

    def picked(to_ref, from_ref):
        def rows_of(start, size, row_at):
            @pl.loop(0, size // 8)
            def _(i):
                base = pl.multiple_of(i * 8, 8)
                for j in range(8):
                    to_ref[pl.ds(start + base + j, 1), :] = from_ref[pl.ds(row_at(base + j), 1), :]

        rows_of(0, width, lambda i: face_s[0, 1, i])
        rows_of(width, width, lambda i: face_s[0, 0, i])
        rows_of(2 * width, primal, lambda i: prim_s[0, i])

    def in_order(value):
        high, low = split(value)
        half_width = value.shape[1]
        both = jnp.dot(ordering, jnp.concatenate([high, low], axis=1), preferred_element_type=F32)
        return both[:, :half_width] + both[:, half_width:]

    picked(first_ref, pre_ref)
    empty = jnp.zeros((padded - used, columns), F32)
    first = jnp.concatenate([first_ref[:2 * width], in_order(first_ref[2 * width:used]), empty], axis=0)

    def one_hot_columns():
        right_ids, left_ids = face_v[0, 1:2, :], face_v[0, 0:1, :]
        ordered_ids = ordered.astype(jnp.int32)

        @pl.loop(0, order // tile)
        def _(c):
            rows = pl.ds(pl.multiple_of(c * tile, tile), tile)
            near = lax.broadcasted_iota(jnp.int32, (tile, width), 0) + c * tile
            e_ref[rows, :width] = jnp.where(near == right_ids, 1.0, 0.0).astype(BF16)
            e_ref[rows, width:2 * width] = jnp.where(near == left_ids, 1.0, 0.0).astype(BF16)
            near = lax.broadcasted_iota(jnp.int32, (tile, corner_width), 0) + c * tile
            e_ref[rows, 2 * width:] = jnp.where(near == ordered_ids, 1.0, 0.0).astype(BF16)

    def finish_a():
        one_hot_columns()
        if padded > used:
            ks_ref[used:, :] = jnp.zeros((padded - used, order), F32)
        picked(ks_ref, k_ref)
        high, low = split(ks_ref[...])
        parts = []
        for part, out in ((high, ah_ref), (low, al_ref)):
            found = jnp.dot(part, e_ref[...], preferred_element_type=F32)
            out[:2 * width, :] = found[:2 * width].astype(BF16)
            out[2 * width:used, :] = jnp.dot(
                ordering, found[2 * width:used].astype(BF16), preferred_element_type=F32
            ).astype(BF16)
            if padded > used:
                out[used:, :] = jnp.zeros((padded - used, padded), BF16)
            parts.append(found[:2 * width, 2 * width:])
        corner = parts[0] + parts[1]
        send_ar[...] = corner[:width]
        send_al[...] = corner[width:]

    def primal_columns():
        picks = e_ref[:, 2 * width:]

        @pl.loop(0, order // tile)
        def _(c):
            rows = pl.ds(pl.multiple_of(c * tile, tile), tile)
            kph_ref[rows, :] = jnp.dot(kh_ref[rows, :], picks, preferred_element_type=F32).astype(BF16)
            kpl_ref[rows, :] = jnp.dot(kl_ref[rows, :], picks, preferred_element_type=F32).astype(BF16)

    def uncorrected(changes):
        high, low = split(changes)
        spread = jnp.dot(e_ref[:, :2 * width], jnp.concatenate([high, low], axis=1), preferred_element_type=F32)
        loads = f_ref[...] + (spread[:, :columns] + spread[:, columns:])
        high, low = split(loads)
        fh_ref[...] = high
        fl_ref[...] = low

        @pl.loop(0, order // tile)
        def _(c):
            rows = pl.ds(pl.multiple_of(c * tile, tile), tile)
            pre_ref[rows, :] = product_parts(kh_ref[rows, :], kl_ref[rows, :], fh_ref[...], fl_ref[...])

    a_copies = [
        remote(send_al, got_al, a_send.at[0], a_recv.at[0], around(-1)),
        remote(send_ar, got_ar, a_send.at[1], a_recv.at[1], around(1)),
    ]

    lam = jnp.zeros((width, columns), F32)
    lam_before = jnp.zeros((width, columns), F32)
    values = first
    changes = None
    for step in range(ITERS):
        if step:
            changes = jnp.concatenate([-lam, lam_before], axis=0)
            values = first + product(ah_ref[:, :2 * width], al_ref[:, :2 * width], changes)
        gat = gat_ref.at[step]
        gat_ref[step, me] = values[2 * width:2 * width + primal]
        send_r[step] = values[:width]
        send_l[step] = values[width:2 * width]
        started = []

        def forward(block, peer, part):
            rows = gat.at[block, pl.ds(part * owned, owned)]
            copy = remote(rows, rows, send_sem.at[step, len(started)], block_sem.at[step, block, part], peer)
            copy.start()
            started.append(copy)

        def arrived(block, part):
            rows = gat.at[block, pl.ds(part * owned, owned)]
            remote(rows, rows, send_sem.at[step, 0], block_sem.at[step, block, part], partner).wait_recv()

        for part in range(2):
            for peer in reversed(outer_peers):
                forward(me, peer, part)
            for peer in inner_peers:
                forward(me, peer, part)
            forward(me, partner, part)
        faces = [
            remote(send_l.at[step], got_l.at[step], face_sem.at[0, step, 0], face_sem.at[1, step, 0], around(-1)),
            remote(send_r.at[step], got_r.at[step], face_sem.at[0, step, 1], face_sem.at[1, step, 1], around(1)),
        ]
        for copy in faces:
            copy.start()

        if step == 0:
            cinv_copies[1].wait_recv()
            passed_on.start()
            finish_a()
            for copy in a_copies:
                copy.start()
        if step == 1:
            primal_columns()
        if step == ITERS - 1:
            uncorrected(changes)

        for part in range(2):
            for source in outer_back:
                block = at(source, y, core)
                arrived(block, part)
                for peer in inner_peers:
                    forward(block, peer, part)
                forward(block, partner, part)
        if step == 0:
            cinv_copies[0].wait()
            cinv_copies[1].wait_send()
            passed_on.wait()
            for slot, part in enumerate((cols_ref.at[0], cinv_ref, cols_ref.at[1], cols_ref.at[2])):
                high, low = split(part[...])
                ch_ref[slot * owned:(slot + 1) * owned, :] = high
                cl_ref[slot * owned:(slot + 1) * owned, :] = low
        for part in range(2):
            for m in range(1, inner):
                for source in [z] + outer_back:
                    block = at(source, returned(y, m, inner), core)
                    arrived(block, part)
                    forward(block, partner, part)
        for part in range(2):
            for source in [z] + outer_back:
                for m in range(inner):
                    arrived(at(source, y if m == 0 else returned(y, m, inner), 1 - core), part)

        for s in range(count):
            r_ref[s * owned:(s + 1) * owned, :] = (
                gat_ref[step, s, :owned, :] + gat_ref[step, (s - 1) % count, owned:, :]
            )
        coarse = product(ch_ref[...], cl_ref[...], r_ref[...])
        fill = jnp.zeros((padded - 2 * width - primal, columns), F32)

        def steps_of(slot):
            return jnp.concatenate([coarse[slot * owned:(slot + 2) * owned], fill], axis=0)

        q_before, q_own, q_after = steps_of(0), steps_of(1), steps_of(2)
        own = product(ah_ref[:2 * width, 2 * width:], al_ref[:2 * width, 2 * width:], q_own)
        if step == 0:
            for copy in a_copies:
                copy.wait()
        for copy in faces:
            copy.wait()
        after = product(*split(got_al[...]), q_after)
        lam = lam + DAMPING * ((values[:width] - own[:width]) - (got_l[step] - after))
        if step + 1 < ITERS:
            before = product(*split(got_ar[...]), q_before)
            lam_before = lam_before + DAMPING * ((got_r[step] - before) - (values[width:2 * width] - own[width:]))
        else:
            lam_ref[...] = lam
            q_ref[...] = q_own
        for copy in started:
            copy.wait_send()


def finish(pre_ref, kph_ref, kpl_ref, q_ref, lam_ref, u_ref, lam_out):
    u_ref[...] = pre_ref[...] - product(kph_ref[...], kpl_ref[...], q_ref[...])
    lam_out[...] = lam_ref[...]


NT = (((1,), (1,)), ((), ()))
NN = (((1,), (0,)), ((), ()))


def tall(x, high, low, dims):
    x_high, x_low = split(x)
    count = x.shape[0]
    both = lax.dot_general(jnp.concatenate([x_high, x_low], axis=0), high, dims, preferred_element_type=F32)
    return both[:count] + both[count:] + lax.dot_general(x_high, low, dims, preferred_element_type=F32)


def lanes_of(count):
    return -(-count // LANES) * LANES


def plane_kernel(
    count, primal, width, face_hbm, prim_hbm, slot_hbm, k_hbm, f_hbm, cinv_hbm, pre_ref, kph_ref, kpl_ref, q_ref, lam_ref,
    face_s, prim_s, face_v, prim_v, slot_v, f_ref, k_ref, kh_ref, kl_ref, e_ref, fh_ref, fl_ref, ks_ref,
    own_c, own_b, c_in, b_in, cinv_ref, cqh_ref, cql_ref, ac_ref, ap_ref, ar_ref, edge_ref,
    ach_ref, acl_ref, aph_ref, apl_ref, arh_ref, arl_ref, r_ref, face_out, face_in, x_out, x_in, q_out, q_in, lam_out, lam_in,
    in_sem, k_sem, c_sem, b_sem, cinv_send, cinv_recv, ac_send, ac_recv, ap_send, ap_recv, ar_send, ar_recv,
    halo_send, halo_recv, edge_sem, r_sem, face_sem, x_sem, q_sem, lam_sem,
):
    outer, inner = grid_of(count)
    plane = 2 * inner
    order, columns = f_ref.shape
    owned = primal // 2
    total = cinv_ref.shape[-1]
    tiles = k_sem.shape[0]
    tile = order // tiles
    share = columns // plane
    both = 2 * width
    wide = lanes_of(primal)
    span = r_ref.shape[-1]
    me = lax.axis_index("sub")
    mine = lax.rem(me, plane)
    z = me // plane
    core = lax.rem(me, 2)

    def at(z_, mine_):
        return z_ * plane + mine_

    partner = at(z, mine + 1 - 2 * core)
    across = [lax.rem(mine + 2 * m, plane) for m in range(1, inner)]
    across_peers = [at(z, other) for other in across]
    others = [lax.rem(mine + m, plane) for m in range(1, plane)]
    mates = [at(z, other) for other in others]
    beyond = [at(lax.rem(z + m, outer), mine) for m in range(1, outer)]
    after, before = beyond[0], beyond[-1]
    far_first = beyond[::-1]
    if outer == 4:
        end = lax.rem(z + 1, outer) < 2
        mirror, skip, twin = outer - 1 - z, lax.rem(z + 2, outer), z + 1 - 2 * lax.rem(z, 2)
        far_first = [at(place, mine) for place in (jnp.where(end, mirror, skip), jnp.where(end, skip, mirror), twin)]

    def remote(src, dst, ssem, rsem, peer):
        return pltpu.make_async_remote_copy(
            src_ref=src, dst_ref=dst, send_sem=ssem, recv_sem=rsem, device_id={"sub": peer}, device_id_type=MESH
        )

    def send(src, dst, ssem, rsem, peer):
        remote(src, dst, ssem, rsem, peer).start()

    def arrived(ref, rsem):
        remote(ref, ref, r_sem.at[0, 0], rsem, partner).wait_recv()

    def sent(ref, ssem):
        remote(ref, ref, ssem, r_sem.at[0, 1], partner).wait_send()

    ints = [
        pltpu.make_async_copy(src, dst, in_sem.at[i])
        for i, (src, dst) in enumerate((
            (face_hbm, face_s), (prim_hbm, prim_s), (face_hbm, face_v), (prim_hbm, prim_v), (slot_hbm, slot_v)
        ))
    ]
    cinv_copy = pltpu.make_async_copy(cinv_hbm, cinv_ref.at[mine + 1], in_sem.at[5])
    f_copy = pltpu.make_async_copy(f_hbm, f_ref, in_sem.at[6])

    def k_copy(c):
        rows = pl.ds(c * tile, tile)
        return pltpu.make_async_copy(k_hbm.at[rows, :], k_ref.at[rows, :], k_sem.at[c])

    for copy in ints + [cinv_copy, f_copy]:
        copy.start()
    for c in range(tiles):
        k_copy(c).start()

    barrier = pltpu.get_barrier_semaphore()
    for peer in mates + beyond:
        pl.semaphore_signal(barrier, inc=1, device_id={"sub": peer}, device_id_type=MESH)

    with jax.named_scope("P_ints"):
        for copy in ints:
            copy.wait()
    square = (primal, primal)
    eye = lax.broadcasted_iota(jnp.int32, square, 0) == lax.broadcasted_iota(jnp.int32, square, 1)
    prim_col = jnp.sum(jnp.where(eye, prim_v[...].astype(F32), 0.0), axis=1, keepdims=True)
    slot_col = jnp.sum(jnp.where(eye, slot_v[...].astype(F32), 0.0), axis=1, keepdims=True)
    lane = lax.broadcasted_iota(jnp.int32, (primal, wide), 1).astype(F32)
    ordered = jnp.sum(jnp.where(slot_col == lane, prim_col + 1.0, 0.0), axis=0, keepdims=True) - 1.0
    ordering = jnp.where(lax.broadcasted_iota(jnp.int32, (wide, primal), 0) == slot_v[...], 1.0, 0.0).astype(BF16)

    def in_order(value):
        high, low = split(value)
        size = value.shape[1]
        pair = jnp.dot(ordering, jnp.concatenate([high, low], axis=1), preferred_element_type=F32)
        return pair[:, :size] + pair[:, size:]

    def one_hot_columns():
        right_ids, left_ids = face_v[0, 1:2, :], face_v[0, 0:1, :]
        ordered_ids = ordered.astype(jnp.int32)

        @pl.loop(0, tiles)
        def _(c):
            rows = pl.ds(pl.multiple_of(c * tile, tile), tile)
            near = lax.broadcasted_iota(jnp.int32, (tile, width), 0) + c * tile
            e_ref[rows, :width] = jnp.where(near == right_ids, 1.0, 0.0).astype(BF16)
            e_ref[rows, width:both] = jnp.where(near == left_ids, 1.0, 0.0).astype(BF16)
            near = lax.broadcasted_iota(jnp.int32, (tile, wide), 0) + c * tile
            e_ref[rows, both:] = jnp.where(near == ordered_ids, 1.0, 0.0).astype(BF16)

    def spread(buf, ssem, rsem, own):
        for peer in across_peers + [partner]:
            send(buf.at[own], buf.at[own], ssem, rsem.at[own], peer)

    def relay(buf, ssem, rsem):
        for other in across:
            arrived(buf.at[other], rsem.at[other])
            send(buf.at[other], buf.at[other], ssem, rsem.at[other], partner)

    def settle(buf, rsem):
        for other in [mine] + across:
            block = other + 1 - 2 * core
            arrived(buf.at[block], rsem.at[block])

    with jax.named_scope("P_onehot"):
        one_hot_columns()
    with jax.named_scope("P_barrier"):
        pl.semaphore_wait(barrier, len(mates + beyond))
        cinv_copy.wait()
    halves = owned // 2

    def piece(block, half):
        return cinv_ref.at[block, pl.ds(half * halves, halves)]

    def send_far(half):
        send(piece(1 + core, half), piece(plane + 1 + core, half), halo_send.at[0], halo_recv.at[0, half], before)

    def send_near(half):
        send(piece(plane, half), piece(0, half), halo_send.at[1], halo_recv.at[1, half], after)

    def spread_coarse(half):
        for peer in across_peers + [partner]:
            rows = piece(mine + 1, half)
            send(rows, rows, cinv_send, cinv_recv.at[mine + 1, half], peer)

    def relay_coarse(half):
        for other in across:
            rows = piece(other + 1, half)
            arrived(rows, cinv_recv.at[other + 1, half])
            send(rows, rows, cinv_send, cinv_recv.at[other + 1, half], partner)
        pl.when(mine >= 2)(functools.partial(send_far, half))
        pl.when(mine == 1)(functools.partial(send_near, half))

    def settle_coarse():
        for half in range(2):
            for other in [mine] + across:
                block = other + 2 - 2 * core
                arrived(piece(block, half), cinv_recv.at[block, half])

    def last_edge():
        send(ac_ref.at[plane - 1, :, pl.ds(0, width)], edge_ref.at[0], edge_sem.at[0], edge_sem.at[1], after)

    def first_edge():
        send(ac_ref.at[0, :, pl.ds(width, width)], edge_ref.at[1], edge_sem.at[0], edge_sem.at[1], before)

    spread_coarse(0)
    for half in range(2):
        pl.when(mine < 2)(functools.partial(send_far, half))
        pl.when(mine == plane - 1)(functools.partial(send_near, half))
    with jax.named_scope("P_f"):
        f_copy.wait()
        high, low = split(f_ref[...])
        fh_ref[...] = high
        fl_ref[...] = low

    def halve(first_tile, last_tile):
        @pl.loop(first_tile, last_tile)
        def _(c):
            rows = pl.ds(pl.multiple_of(c * tile, tile), tile)
            high, low = split(k_ref[rows, :])
            kh_ref[rows, :] = high
            kl_ref[rows, :] = low

    with jax.named_scope("P_kwait"):
        for c in range(tiles):
            k_copy(c).wait()

    def picked(start, size, row_at):
        @pl.loop(0, size // 8)
        def _(i):
            base = pl.multiple_of(i * 8, 8)
            for j in range(8):
                ks_ref[pl.ds(start + base + j, 1), :] = k_ref[pl.ds(row_at(base + j), 1), :]

    def first(rows):
        high, low = split(ks_ref[rows, :])
        return product_parts(high, low, fh_ref[...], fl_ref[...])

    def columns_of(rows, picks):
        high, low = split(ks_ref[rows, :])
        return jnp.dot(high, picks, preferred_element_type=F32) + jnp.dot(low, picks, preferred_element_type=F32)

    def give(out, into, sems):
        for other, peer in zip(others, mates):
            send(out.at[other], into.at[mine], sems.at[0], sems.at[1], peer)
        into[mine] = out[mine]

    def taken(into, sems):
        arrived(into.at[pl.ds(0, plane - 1)], sems.at[1])

    def assembled(parts):
        sums = None
        for i, part in enumerate(parts):
            part = jnp.concatenate([part, jnp.zeros((share, span - wide), F32)], axis=1)
            part = pltpu.roll(part, owned * i, 1) if i else part
            sums = part if sums is None else sums + part
        return sums

    def publish(step, parts):
        r_ref[step, z] = assembled(parts)
        for peer in far_first:
            rows = r_ref.at[step, z]
            send(rows, rows, r_sem.at[step, 0], r_sem.at[step, 1], peer)

    def faces(step, last_right, first_left):
        face_out[step, 0] = first_left
        send(face_out.at[step, 0], face_in.at[step, 0], face_sem.at[step, 0], face_sem.at[step, 1], before)
        if step + 1 < ITERS:
            face_out[step, 1] = last_right
            send(face_out.at[step, 1], face_in.at[step, 1], face_sem.at[step, 0], face_sem.at[step, 1], after)

    def face_part(ref, step):
        return ref.at[step] if step + 1 < ITERS else ref.at[step, pl.ds(0, 1)]

    urgent = jnp.where(mine == 0, 1, 0)

    def spread_half(half):
        for peer in across_peers + [partner]:
            rows = ar_ref.at[mine, half]
            send(rows, rows, ar_send, ar_recv.at[mine, half], peer)

    def relay_half(flip):
        for other in across:
            half = jnp.where(other == 0, 1 - flip, flip)
            rows = ar_ref.at[other, half]
            arrived(rows, ar_recv.at[other, half])
            send(rows, rows, ar_send, ar_recv.at[other, half], partner)

    def settle_half(flip):
        for other in [mine] + across:
            block = other + 1 - 2 * core
            half = jnp.where(block == 0, 1 - flip, flip)
            arrived(ar_ref.at[block, half], ar_recv.at[block, half])

    with jax.named_scope("P_first"):
        picked(both, primal, lambda i: prim_s[0, i])
        own_c[...] = in_order(first(slice(both, both + primal))).T.reshape(own_c.shape)
        give(own_c, c_in, c_sem)
    spread_coarse(1)
    with jax.named_scope("P_pick"):
        picked(0, width, lambda i: face_s[0, 1, i])
        picked(width, width, lambda i: face_s[0, 0, i])
    with jax.named_scope("P_ac"):
        found = columns_of(slice(0, both), e_ref[:, both:])
        ac_ref[mine, :, :width] = found[:width].T[:primal]
        ac_ref[mine, :, width:] = found[width:].T[:primal]
        spread(ac_ref, ac_send, ac_recv, mine)
    with jax.named_scope("P_relayc0"):
        relay_coarse(0)
    with jax.named_scope("P_cwait"):
        taken(c_in, c_sem)
    publish(0, [c_in[i] for i in range(plane)])
    pl.when(mine == plane - 1)(last_edge)
    pl.when(mine == 0)(first_edge)
    with jax.named_scope("P_firstb"):
        loads = first(slice(0, both))
        own_b[:, :, :width] = loads[:width].T.reshape(plane, share, width)
        own_b[:, :, width:] = loads[width:].T.reshape(plane, share, width)
        give(own_b, b_in, b_sem)
    with jax.named_scope("P_relayc1"):
        relay_coarse(1)
    with jax.named_scope("P_ap"):
        ap_ref[mine] = in_order(columns_of(slice(both, both + primal), e_ref[:, :both]))[:primal]
        spread(ap_ref, ap_send, ap_recv, mine)
    with jax.named_scope("P_ar"):
        found = columns_of(slice(0, both), e_ref[:, :both])
        ar_ref[mine, 0] = found[:width]
        ar_ref[mine, 1] = found[width:]
        spread_half(urgent)
        spread_half(1 - urgent)
    with jax.named_scope("P_relayac"):
        relay(ac_ref, ac_send, ac_recv)
    pl.when(mine == 1)(last_edge)
    pl.when(mine == 2)(first_edge)
    with jax.named_scope("P_bwait"):
        taken(b_in, b_sem)
    faces(0, b_in[plane - 1, :, :width], b_in[0, :, width:])
    with jax.named_scope("P_halve"):
        halve(0, tiles)

    def primal_columns(first_tile, last_tile):
        picks = e_ref[:, both:]

        @pl.loop(first_tile, last_tile)
        def _(c):
            rows = pl.ds(pl.multiple_of(c * tile, tile), tile)
            kph_ref[rows, :] = jnp.dot(kh_ref[rows, :], picks, preferred_element_type=F32).astype(BF16)
            kpl_ref[rows, :] = jnp.dot(kl_ref[rows, :], picks, preferred_element_type=F32).astype(BF16)

    def coarse_rows(first_block, last_block):
        for b in range(first_block, last_block):
            for ref, part in zip((cqh_ref, cql_ref), split(cinv_ref[b])):
                ref[b * owned:(b + 1) * owned, :] = part

    def halves_of(refs, src):
        for i in range(plane):
            for ref, part in zip(refs, split(src[i])):
                ref[i, :primal, :] = part
                ref[i, primal:, :] = jnp.zeros((wide - primal, both), BF16)

    early = tiles // 3
    with jax.named_scope("P_halo"):
        settle_coarse()
        far = cinv_ref.at[plane + 1 + core]
        near = cinv_ref.at[0]
        for half in range(2):
            arrived(piece(plane + 1 + core, half), halo_recv.at[0, half])
        send(far, far, halo_send.at[0], halo_recv.at[2, 0], partner)

        @pl.when(core == 1)
        def _():
            for half in range(2):
                arrived(piece(0, half), halo_recv.at[1, half])
            send(near, near, halo_send.at[1], halo_recv.at[2, 1], partner)

    with jax.named_scope("P_cq"):
        rest = (plane + 3) * owned
        for ref in (cqh_ref, cql_ref):
            ref[rest:, :] = jnp.zeros((ref.shape[0] - rest, total), BF16)
        coarse_rows(1, plane + 1)
    with jax.named_scope("P_settleac"):
        settle(ac_ref, ac_recv)
        halves_of((ach_ref, acl_ref), ac_ref)
    with jax.named_scope("P_relayap"):
        relay(ap_ref, ap_send, ap_recv)
    with jax.named_scope("P_halo2"):
        arrived(cinv_ref.at[plane + 2 - core], halo_recv.at[2, 0])

        @pl.when(core == 0)
        def _():
            arrived(near, halo_recv.at[2, 1])

        coarse_rows(0, 1)
        coarse_rows(plane + 1, plane + 3)
    with jax.named_scope("P_edge0"):
        rows = edge_ref.at[1 - core]
        arrived(rows, edge_sem.at[1])
        send(rows, rows, edge_sem.at[3], edge_sem.at[2], partner)

    def uncorrected(first_tile, last_tile):
        @pl.loop(first_tile, last_tile)
        def _(c):
            rows = pl.ds(pl.multiple_of(c * tile, tile), tile)
            pre_ref[rows, :] = product_parts(kh_ref[rows, :], kl_ref[rows, :], fh_ref[...], fl_ref[...])

    def changed_loads():
        high, low = split(x_in[...].reshape(columns, both))
        moved = lax.dot_general(
            e_ref[:, :both], jnp.concatenate([high, low], axis=0), NT, preferred_element_type=F32
        )
        high, low = split(f_ref[...] + (moved[:, :columns] + moved[:, columns:]))
        fh_ref[...] = high
        fl_ref[...] = low

    def padded(value):
        return jnp.concatenate([value, jnp.zeros((wide - primal, value.shape[1]), F32)], axis=0)

    lam = [jnp.zeros((share, width), F32)] * (plane + 1)
    values = [b_in[i] for i in range(plane)]
    edges = None
    for step in range(ITERS):
        if step == ITERS - 1:
            with jax.named_scope("P_primcol1"):
                primal_columns(tiles - early, tiles)
            with jax.named_scope("P_xwait"):
                arrived(x_in.at[pl.ds(0, plane - 1)], x_sem.at[1])
                changed_loads()
            with jax.named_scope("P_uncorr0"):
                uncorrected(0, early)
        with jax.named_scope(f"P_rwait{step}"):
            arrived(r_ref.at[step, pl.ds(0, outer - 1)], r_sem.at[step, 1])
        with jax.named_scope(f"P_coarse{step}"):
            sums = None
            for i in range(outer):
                part = jnp.concatenate([r_ref[step, i], jnp.zeros((share, total - span), F32)], axis=1)
                part = pltpu.roll(part, plane * owned * i, 1) if i else part
                sums = part if sums is None else sums + part
            coarse = tall(sums, cqh_ref[...], cql_ref[...], NT)
            steps = [coarse[:, :wide]]
            for i in range(1, plane + 2):
                steps.append(pltpu.roll(coarse, coarse.shape[1] - owned * i, 1)[:, :wide])
            if step == ITERS - 1:
                for i in range(plane):
                    q_out[i] = steps[i + 1]
                for other, peer in zip(others, mates):
                    send(q_out.at[other], q_in.at[mine], q_sem.at[0], q_sem.at[1], peer)
                q_in[mine] = q_out[mine]
        if edges is None:
            with jax.named_scope("P_edge"):
                arrived(edge_ref.at[core], edge_sem.at[2])
                edges = [split(padded(edge_ref[i])) for i in range(2)]
        with jax.named_scope(f"P_faces{step}"):
            arrived(face_part(face_in, step), face_sem.at[step, 1])
        with jax.named_scope(f"P_update{step}"):
            moved = [values[i] - tall(steps[i + 1], ach_ref[i], acl_ref[i], NN) for i in range(plane)]
            right = [part[:, :width] for part in moved]
            left = [part[:, width:] for part in moved]
            left.append(face_in[step, 0] - tall(steps[plane + 1], *edges[1], NN))
            lam_next = [lam[i + 1] + DAMPING * (right[i] - left[i + 1]) for i in range(plane)]
            if step + 1 < ITERS:
                ahead = face_in[step, 1] - tall(steps[0], *edges[0], NN)
                lam_next = [lam[0] + DAMPING * (ahead - left[0])] + lam_next
            else:
                for i in range(plane):
                    lam_out[i] = lam_next[i]
                for other, peer in zip(others, mates):
                    send(lam_out.at[other], lam_in.at[mine], lam_sem.at[0], lam_sem.at[1], peer)
                lam_in[mine] = lam_out[mine]
                break
            lam = lam_next
            if step == 0:
                with jax.named_scope("P_settleap"):
                    settle(ap_ref, ap_recv)
                    halves_of((aph_ref, apl_ref), ap_ref)
            changes = [jnp.concatenate([-lam[i + 1], lam[i]], axis=1) for i in range(plane)]
            publish(step + 1, [
                c_in[i] + tall(changes[i], aph_ref[i], apl_ref[i], NT) for i in range(plane)
            ])
            if step == ITERS - 2:
                for i in range(plane):
                    x_out[i] = changes[i]
                for other, peer in zip(others, mates):
                    send(x_out.at[other], x_in.at[mine], x_sem.at[0], x_sem.at[1], peer)
                x_in[mine] = x_out[mine]
        if step == 0:
            with jax.named_scope("P_relayr0"):
                relay_half(0)
                settle_half(0)
                for i, half in ((plane - 1, 0), (0, 1)):
                    rows = slice(half * width, (half + 1) * width)
                    for ref, part in zip((arh_ref, arl_ref), split(ar_ref[i, half])):
                        ref[i, rows] = part
            with jax.named_scope("P_facevalues"):
                last_right = tall(changes[-1], arh_ref[plane - 1, :width], arl_ref[plane - 1, :width], NT)
                first_left = tall(changes[0], arh_ref[0, width:], arl_ref[0, width:], NT)
                faces(1, b_in[plane - 1, :, :width] + last_right, b_in[0, :, width:] + first_left)
            with jax.named_scope("P_primcol0"):
                primal_columns(0, early)
            with jax.named_scope("P_relayr1"):
                relay_half(1)
            with jax.named_scope("P_primcol0"):
                primal_columns(early, tiles - early)
            with jax.named_scope("P_settler1"):
                settle_half(1)
                for i in range(plane):
                    for half in range(2):
                        if (i, half) not in ((plane - 1, 0), (0, 1)):
                            rows = slice(half * width, (half + 1) * width)
                            for ref, part in zip((arh_ref, arl_ref), split(ar_ref[i, half])):
                                ref[i, rows] = part
        with jax.named_scope(f"P_values{step}"):
            values = [b_in[i] + tall(changes[i], arh_ref[i], arl_ref[i], NT) for i in range(plane)]
            if step:
                faces(step + 1, values[plane - 1][:, :width], values[0][:, width:])

    with jax.named_scope("P_uncorr1"):
        uncorrected(early, tiles)
    with jax.named_scope("P_qwait"):
        arrived(q_in.at[pl.ds(0, plane - 1)], q_sem.at[1])
        q_ref[...] = q_in[...].reshape(q_ref.shape)
    with jax.named_scope("P_lamwait"):
        arrived(lam_in.at[pl.ds(0, plane - 1)], lam_sem.at[1])
        lam_ref[...] = lam_in[...].reshape(lam_ref.shape)
    with jax.named_scope("P_sent"):
        others_part = pl.ds(0, plane - 1)
        sent(own_c.at[others_part], c_sem.at[0])
        sent(own_b.at[others_part], b_sem.at[0])
        sent(cinv_ref.at[others_part], cinv_send)
        for ref, sem in ((ac_ref, ac_send), (ap_ref, ap_send), (ar_ref, ar_send)):
            sent(ref.at[others_part], sem)
        sent(cinv_ref.at[pl.ds(0, 2)], halo_send.at[0])

        @pl.when(core == 1)
        def _():
            sent(cinv_ref.at[pl.ds(0, 2)], halo_send.at[1])

        sent(edge_ref.at[0], edge_sem.at[0])
        sent(edge_ref.at[0], edge_sem.at[3])
        for step in range(ITERS):
            sent(r_ref.at[step, pl.ds(0, outer - 1)], r_sem.at[step, 0])
            sent(face_part(face_out, step), face_sem.at[step, 0])
        sent(x_out.at[others_part], x_sem.at[0])
        sent(q_out.at[others_part], q_sem.at[0])
        sent(lam_out.at[others_part], lam_sem.at[0])


def plane_finish(pre_ref, kph_ref, kpl_ref, q_ref, lam_ref, u_hbm, lam_hbm, u_ref, lam_out, sem):
    tiles = sem.shape[0] - 1
    tile = u_ref.shape[0] // tiles
    columns = q_ref.shape[0]
    lam_out[...] = lam_ref[...].T
    copies = [pltpu.make_async_copy(lam_out, lam_hbm, sem.at[tiles])]
    copies[0].start()
    high, low = split(q_ref[...])
    pair = jnp.concatenate([high, low], axis=0)
    for c in range(tiles):
        rows = pl.ds(c * tile, tile)
        both = lax.dot_general(kph_ref[rows, :], pair, NT, preferred_element_type=F32)
        both = both[:, :columns] + both[:, columns:]
        u_ref[rows, :] = pre_ref[rows, :] - (
            both + lax.dot_general(kpl_ref[rows, :], high, NT, preferred_element_type=F32)
        )
        copies.append(pltpu.make_async_copy(u_ref.at[rows, :], u_hbm.at[rows, :], sem.at[c]))
        copies[-1].start()
    for copy in copies:
        copy.wait()


def size_of(buffers):
    return sum((4 if kind == F32 else 2) * functools.reduce(lambda a, b: a * b, size) for size, kind in buffers)


def plane_scratch(count, order, columns, owned, total, width, primal):
    outer, inner = grid_of(count)
    plane = 2 * inner
    both = 2 * width
    wide = lanes_of(primal)
    span = lanes_of((plane + 1) * owned)
    share = columns // plane
    pairs = lanes_of((plane + 3) * owned)
    return plane, [
        ((order, columns), F32),
        ((order, order), F32),
        ((order, order), BF16),
        ((order, order), BF16),
        ((order, both + wide), BF16),
        ((order, columns), BF16),
        ((order, columns), BF16),
        ((both + primal, order), F32),
        ((plane, share, wide), F32),
        ((plane, share, both), F32),
        ((plane, share, wide), F32),
        ((plane, share, both), F32),
        ((plane + 3, owned, total), F32),
        ((pairs, total), BF16),
        ((pairs, total), BF16),
        ((plane, primal, both), F32),
        ((plane, primal, both), F32),
        ((plane, 2, width, both), F32),
        ((2, primal, width), F32),
        ((plane, wide, both), BF16),
        ((plane, wide, both), BF16),
        ((plane, wide, both), BF16),
        ((plane, wide, both), BF16),
        ((plane, both, both), BF16),
        ((plane, both, both), BF16),
        ((ITERS, outer, share, span), F32),
        ((ITERS, 2, share, width), F32),
        ((ITERS, 2, share, width), F32),
        ((plane, share, both), F32),
        ((plane, share, both), F32),
        ((plane, share, wide), F32),
        ((plane, share, wide), F32),
        ((plane, share, width), F32),
        ((plane, share, width), F32),
    ]


def planar(condensed, eigen_loads, coarse_inverse, face_rows, primal_rows, primal_slot):
    count = lax.axis_size("sub")
    order, columns = eigen_loads.shape
    owned, total = coarse_inverse.shape
    width = face_rows.shape[2]
    primal = primal_rows.shape[1]
    outer, inner = grid_of(count)
    tile = 256 if order % 256 == 0 else order
    tiles = order // tile
    pieces = tiles // 2 if tiles % 2 == 0 else 1
    plane, buffers = plane_scratch(count, order, columns, owned, total, width, primal)
    needed = size_of(buffers)
    wide = lanes_of(primal)
    dma = pltpu.SemaphoreType.DMA
    vmem = pl.BlockSpec(memory_space=pltpu.VMEM)
    shape = jax.ShapeDtypeStruct
    held = [
        pltpu.with_memory_space_constraint(value, pltpu.HBM)
        for value in (face_rows, primal_rows, primal_slot, condensed, eigen_loads, coarse_inverse)
    ]
    parts = pl.pallas_call(
        functools.partial(plane_kernel, count, primal, width),
        out_shape=(
            shape((order, columns), F32),
            shape((order, wide), BF16),
            shape((order, wide), BF16),
            shape((columns, wide), F32),
            shape((columns, width), F32),
        ),
        in_specs=[pl.BlockSpec(memory_space=pltpu.HBM)] * 6,
        out_specs=(vmem,) * 5,
        scratch_shapes=[
            pltpu.SMEM(face_rows.shape, jnp.int32),
            pltpu.SMEM(primal_rows.shape, jnp.int32),
            pltpu.VMEM(face_rows.shape, jnp.int32),
            pltpu.VMEM(primal_rows.shape, jnp.int32),
            pltpu.VMEM(primal_slot.shape, jnp.int32),
        ] + [pltpu.VMEM(size, kind) for size, kind in buffers] + [
            dma((7,)),
            dma((tiles,)),
            dma((2,)),
            dma((2,)),
            dma(()),
            dma((plane + 1, 2)),
            dma(()),
            dma((plane,)),
            dma(()),
            dma((plane,)),
            dma(()),
            dma((plane, 2)),
            dma((2,)),
            dma((3, 2)),
            dma((4,)),
            dma((ITERS, 2)),
            dma((ITERS, 2)),
            dma((2,)),
            dma((2,)),
            dma((2,)),
        ],
        compiler_params=pltpu.CompilerParams(
            collective_id=0, has_side_effects=True, vmem_limit_bytes=min(PLANE_LIMIT, needed + needed // 3)
        ),
    )(*held)
    return pl.pallas_call(
        plane_finish,
        out_shape=(shape((order, columns), F32), shape((width, columns), F32)),
        in_specs=[vmem] * 5,
        out_specs=(pl.BlockSpec(memory_space=pltpu.HBM),) * 2,
        scratch_shapes=[pltpu.VMEM((order, columns), F32), pltpu.VMEM((width, columns), F32), dma((pieces + 1,))],
        compiler_params=pltpu.CompilerParams(vmem_limit_bytes=4 * order * columns * 8),
    )(*parts)


def fits_plane(condensed, eigen_loads, coarse_inverse, face_rows, primal_rows, primal_slot):
    count = lax.axis_size("sub")
    order, columns = eigen_loads.shape
    owned, total = coarse_inverse.shape
    width = face_rows.shape[2]
    primal = primal_rows.shape[1]
    outer, inner = grid_of(count)
    plane = 2 * inner
    if outer < 2 or inner != 2 or columns % (8 * plane) or total % LANES or width % LANES or owned % 16 or primal != 2 * owned:
        return False
    _, buffers = plane_scratch(count, order, columns, owned, total, width, primal)
    return size_of(buffers) <= PLANE_LIMIT * 3 // 4


def local(*values):
    return (planar if fits_plane(*values) else general)(*values)


def general(condensed, eigen_loads, coarse_inverse, face_rows, primal_rows, primal_slot):
    count = lax.axis_size("sub")
    order, columns = eigen_loads.shape
    owned, total = coarse_inverse.shape
    width = face_rows.shape[2]
    primal = primal_rows.shape[1]
    padded = 2 * width + -(-primal // LANES) * LANES
    outer, inner = grid_of(count)
    corner_width = padded - 2 * width
    tile = 256 if order % 256 == 0 else order
    sends = (outer - 1) + (inner - 1) * outer + outer * inner
    dma = pltpu.SemaphoreType.DMA
    vmem = pl.BlockSpec(memory_space=pltpu.VMEM)
    face = pltpu.VMEM((ITERS, width, columns), F32)
    corner = pltpu.VMEM((width, padded - 2 * width), F32)
    smem = pl.BlockSpec(memory_space=pltpu.SMEM)
    needed = 8 * order * (order + padded + 2 * columns) + 4 * padded * (order + columns + padded)
    needed += 4 * owned * total * 8 + 4 * columns * (ITERS * (count * primal + 4 * width) + total)
    needed += 4 * order * (columns + 2 * corner_width) + 4 * columns * (order + 8 * width)
    shape = jax.ShapeDtypeStruct
    held = [
        pltpu.with_memory_space_constraint(value, pltpu.HBM)
        for value in (face_rows, primal_rows, primal_slot, condensed, eigen_loads, coarse_inverse)
    ]
    parts = pl.pallas_call(
        functools.partial(kernel, count, primal, width),
        out_shape=(
            shape((order, columns), F32),
            shape((order, corner_width), BF16),
            shape((order, corner_width), BF16),
            shape((corner_width, columns), F32),
            shape((width, columns), F32),
        ),
        in_specs=[smem, smem] + [pl.BlockSpec(memory_space=pltpu.HBM)] * 6,
        out_specs=(vmem,) * 5,
        scratch_shapes=[
            pltpu.VMEM(face_rows.shape, jnp.int32),
            pltpu.VMEM(primal_rows.shape, jnp.int32),
            pltpu.VMEM(primal_slot.shape, jnp.int32),
            pltpu.VMEM((order, columns), F32),
            pltpu.VMEM((owned, total), F32),
            dma((5,)),
            pltpu.VMEM((order, order), F32),
            pltpu.VMEM((order, order), BF16),
            pltpu.VMEM((order, order), BF16),
            pltpu.VMEM((order, padded), BF16),
            pltpu.VMEM((order, columns), BF16),
            pltpu.VMEM((order, columns), BF16),
            pltpu.VMEM((padded, order), F32),
            pltpu.VMEM((padded, columns), F32),
            pltpu.VMEM((padded, padded), BF16),
            pltpu.VMEM((padded, padded), BF16),
            pltpu.VMEM((3, owned, total), F32),
            pltpu.VMEM((4 * owned, total), BF16),
            pltpu.VMEM((4 * owned, total), BF16),
            pltpu.VMEM((ITERS, count, primal, columns), F32),
            pltpu.VMEM((total, columns), F32),
            face, face, face, face,
            corner, corner, corner, corner,
            dma((order // tile,)),
            dma((ITERS, 2 * sends)),
            dma((ITERS, count, 2)),
            dma((2, ITERS, 2)),
            dma((3,)),
            dma((3,)),
            dma((2,)),
            dma((2,)),
        ],
        compiler_params=pltpu.CompilerParams(
            collective_id=0, has_side_effects=True, vmem_limit_bytes=min(VMEM_LIMIT, needed + needed // 4)
        ),
    )(face_rows, primal_rows, *held)
    return pl.pallas_call(
        finish,
        out_shape=(shape((order, columns), F32), shape((width, columns), F32)),
        in_specs=[vmem] * 5,
        out_specs=(vmem, vmem),
        compiler_params=pltpu.CompilerParams(vmem_limit_bytes=4 * order * columns * 8),
    )(*parts)


def solution(mesh):
    placed = (
        P(("rve", "sub"), None),
        P(("rve", "sub"), None),
        P(("rve", "sub"), None),
        P("sub", None, None),
        P("sub", None),
        P("sub", None),
    )
    return jax.shard_map(
        local,
        mesh=mesh,
        in_specs=placed,
        out_specs=(P(("rve", "sub"), None), P(("rve", "sub"), None)),
        check_vma=False,
    )
```

```python
import functools

import jax
import jax.numpy as jnp
from jax import lax
from jax.experimental import pallas as pl
from jax.experimental.pallas import tpu as pltpu
from jax.sharding import PartitionSpec as P

ITERS = 3
DAMPING = 0.5
VMEM_LIMIT = 67043328
MESH = pl.DeviceIdType.MESH
F32 = jnp.float32
BF16 = jnp.bfloat16
LANES = 128
PLANE_LIMIT = 60 * 1024 * 1024


def grid_of(count):
    chips = count // 2
    inner = 1
    while (2 * inner) ** 2 <= chips and chips % (2 * inner) == 0:
        inner *= 2
    return chips // inner, inner


def flipped(index, mask, count):
    if count & (count - 1):
        return lax.rem(index + count - mask, count)
    out = 0
    bit = 1
    while bit < count:
        own = lax.rem(index // bit, 2)
        out = out + bit * ((1 - own) if mask & bit else own)
        bit *= 2
    return out


def returned(index, mask, count):
    if count & (count - 1):
        return lax.rem(index + mask, count)
    return flipped(index, mask, count)


def split(value):
    high = value.astype(BF16)
    return high, (value - high.astype(F32)).astype(BF16)


def product(high, low, value):
    value_high, value_low = split(value)
    return product_parts(high, low, value_high, value_low)


def product_parts(high, low, value_high, value_low):
    width = value_high.shape[1]
    both = jnp.dot(high, jnp.concatenate([value_high, value_low], axis=1), preferred_element_type=F32)
    return both[:, :width] + both[:, width:] + jnp.dot(low, value_high, preferred_element_type=F32)


def kernel(
    count, primal, width, face_s, prim_s, face_hbm, prim_hbm, slot_hbm, k_hbm, f_hbm, cinv_hbm, pre_ref, kph_ref, kpl_ref, q_ref, lam_ref,
    face_v, prim_v, slot_v, f_ref, cinv_ref, in_sem, k_ref, kh_ref, kl_ref, e_ref, fh_ref, fl_ref, ks_ref, first_ref, ah_ref, al_ref, cols_ref, ch_ref, cl_ref,
    gat_ref, r_ref, send_r, send_l, got_r, got_l, send_ar, send_al, got_ar, got_al,
    k_sem, send_sem, block_sem, face_sem, cinv_send, cinv_recv, a_send, a_recv,
):
    outer, inner = grid_of(count)
    order, columns = f_ref.shape
    owned = primal // 2
    tile = order // k_sem.shape[0]
    padded = e_ref.shape[1]
    me = lax.axis_index("sub")
    core = lax.rem(me, 2)
    y = lax.rem(me // 2, inner)
    z = me // (2 * inner)

    def at(z_, y_, core_):
        return (z_ * inner + y_) * 2 + core_

    def around(steps):
        return lax.rem(me + (steps + count), count)

    def k_copy(c):
        rows = pl.ds(c * tile, tile)
        return pltpu.make_async_copy(k_hbm.at[rows, :], k_ref.at[rows, :], k_sem.at[c])

    held = [
        pltpu.make_async_copy(src, dst, in_sem.at[i])
        for i, (src, dst) in enumerate((
            (f_hbm, f_ref), (cinv_hbm, cinv_ref), (face_hbm, face_v), (prim_hbm, prim_v), (slot_hbm, slot_v)
        ))
    ]
    for copy in held:
        copy.start()
    for c in range(k_sem.shape[0]):
        k_copy(c).start()

    outer_peers = [at(flipped(z, m, outer), y, core) for m in range(1, outer)]
    outer_back = [returned(z, m, outer) for m in range(1, outer)]
    inner_peers = [at(z, flipped(y, m, inner), core) for m in range(1, inner)]
    partner = at(z, y, 1 - core)
    ring = [around(d) for d in (-1, 1)]

    barrier = pltpu.get_barrier_semaphore()
    greeted = outer_peers + inner_peers + [partner] + ring
    if outer & (outer - 1):
        greeted = greeted + [at(b, y, core) for b in outer_back]
    for peer in greeted:
        pl.semaphore_signal(barrier, inc=1, device_id={"sub": peer}, device_id_type=MESH)

    def remote(src, dst, ssem, rsem, peer):
        return pltpu.make_async_remote_copy(
            src_ref=src, dst_ref=dst, send_sem=ssem, recv_sem=rsem, device_id={"sub": peer}, device_id_type=MESH
        )

    cinv_copies = [
        remote(cinv_ref, cols_ref.at[slot], cinv_send.at[slot], cinv_recv.at[slot], around(d))
        for slot, d in ((0, 1), (1, -1))
    ]
    passed_on = remote(cols_ref.at[1], cols_ref.at[2], cinv_send.at[2], cinv_recv.at[2], around(-1))

    for copy in held:
        copy.wait()

    square = (primal, primal)
    eye = lax.broadcasted_iota(jnp.int32, square, 0) == lax.broadcasted_iota(jnp.int32, square, 1)
    prim_col = jnp.sum(jnp.where(eye, prim_v[...].astype(F32), 0.0), axis=1, keepdims=True)
    slot_col = jnp.sum(jnp.where(eye, slot_v[...].astype(F32), 0.0), axis=1, keepdims=True)
    corner_width = padded - 2 * width
    lane = lax.broadcasted_iota(jnp.int32, (primal, corner_width), 1).astype(F32)
    ordered = jnp.sum(jnp.where(slot_col == lane, prim_col + 1.0, 0.0), axis=0, keepdims=True) - 1.0
    ordering = jnp.where(lax.broadcasted_iota(jnp.int32, square, 0) == slot_v[...], 1.0, 0.0).astype(BF16)

    fh, fl = split(f_ref[...])
    fh_ref[...] = fh
    fl_ref[...] = fl

    def stream(first_tile, last_tile):
        @pl.loop(first_tile, last_tile)
        def _(c):
            k_copy(c).wait()
            rows = pl.ds(pl.multiple_of(c * tile, tile), tile)
            high, low = split(k_ref[rows, :])
            kh_ref[rows, :] = high
            kl_ref[rows, :] = low
            pre_ref[rows, :] = product_parts(high, low, fh_ref[...], fl_ref[...])

    half = 1
    stream(0, half)
    pl.semaphore_wait(barrier, len(greeted))
    for copy in cinv_copies:
        copy.start()
    stream(half, order // tile)

    used = 2 * width + primal

    def picked(to_ref, from_ref):
        def rows_of(start, size, row_at):
            @pl.loop(0, size // 8)
            def _(i):
                base = pl.multiple_of(i * 8, 8)
                for j in range(8):
                    to_ref[pl.ds(start + base + j, 1), :] = from_ref[pl.ds(row_at(base + j), 1), :]

        rows_of(0, width, lambda i: face_s[0, 1, i])
        rows_of(width, width, lambda i: face_s[0, 0, i])
        rows_of(2 * width, primal, lambda i: prim_s[0, i])

    def in_order(value):
        high, low = split(value)
        half_width = value.shape[1]
        both = jnp.dot(ordering, jnp.concatenate([high, low], axis=1), preferred_element_type=F32)
        return both[:, :half_width] + both[:, half_width:]

    picked(first_ref, pre_ref)
    empty = jnp.zeros((padded - used, columns), F32)
    first = jnp.concatenate([first_ref[:2 * width], in_order(first_ref[2 * width:used]), empty], axis=0)

    def one_hot_columns():
        right_ids, left_ids = face_v[0, 1:2, :], face_v[0, 0:1, :]
        ordered_ids = ordered.astype(jnp.int32)

        @pl.loop(0, order // tile)
        def _(c):
            rows = pl.ds(pl.multiple_of(c * tile, tile), tile)
            near = lax.broadcasted_iota(jnp.int32, (tile, width), 0) + c * tile
            e_ref[rows, :width] = jnp.where(near == right_ids, 1.0, 0.0).astype(BF16)
            e_ref[rows, width:2 * width] = jnp.where(near == left_ids, 1.0, 0.0).astype(BF16)
            near = lax.broadcasted_iota(jnp.int32, (tile, corner_width), 0) + c * tile
            e_ref[rows, 2 * width:] = jnp.where(near == ordered_ids, 1.0, 0.0).astype(BF16)

    def finish_a():
        one_hot_columns()
        if padded > used:
            ks_ref[used:, :] = jnp.zeros((padded - used, order), F32)
        picked(ks_ref, k_ref)
        high, low = split(ks_ref[...])
        parts = []
        for part, out in ((high, ah_ref), (low, al_ref)):
            found = jnp.dot(part, e_ref[...], preferred_element_type=F32)
            out[:2 * width, :] = found[:2 * width].astype(BF16)
            out[2 * width:used, :] = jnp.dot(
                ordering, found[2 * width:used].astype(BF16), preferred_element_type=F32
            ).astype(BF16)
            if padded > used:
                out[used:, :] = jnp.zeros((padded - used, padded), BF16)
            parts.append(found[:2 * width, 2 * width:])
        corner = parts[0] + parts[1]
        send_ar[...] = corner[:width]
        send_al[...] = corner[width:]

    def primal_columns():
        picks = e_ref[:, 2 * width:]

        @pl.loop(0, order // tile)
        def _(c):
            rows = pl.ds(pl.multiple_of(c * tile, tile), tile)
            kph_ref[rows, :] = jnp.dot(kh_ref[rows, :], picks, preferred_element_type=F32).astype(BF16)
            kpl_ref[rows, :] = jnp.dot(kl_ref[rows, :], picks, preferred_element_type=F32).astype(BF16)

    def uncorrected(changes):
        high, low = split(changes)
        spread = jnp.dot(e_ref[:, :2 * width], jnp.concatenate([high, low], axis=1), preferred_element_type=F32)
        loads = f_ref[...] + (spread[:, :columns] + spread[:, columns:])
        high, low = split(loads)
        fh_ref[...] = high
        fl_ref[...] = low

        @pl.loop(0, order // tile)
        def _(c):
            rows = pl.ds(pl.multiple_of(c * tile, tile), tile)
            pre_ref[rows, :] = product_parts(kh_ref[rows, :], kl_ref[rows, :], fh_ref[...], fl_ref[...])

    a_copies = [
        remote(send_al, got_al, a_send.at[0], a_recv.at[0], around(-1)),
        remote(send_ar, got_ar, a_send.at[1], a_recv.at[1], around(1)),
    ]

    lam = jnp.zeros((width, columns), F32)
    lam_before = jnp.zeros((width, columns), F32)
    values = first
    changes = None
    for step in range(ITERS):
        if step:
            changes = jnp.concatenate([-lam, lam_before], axis=0)
            values = first + product(ah_ref[:, :2 * width], al_ref[:, :2 * width], changes)
        gat = gat_ref.at[step]
        gat_ref[step, me] = values[2 * width:2 * width + primal]
        send_r[step] = values[:width]
        send_l[step] = values[width:2 * width]
        started = []

        def forward(block, peer, part):
            rows = gat.at[block, pl.ds(part * owned, owned)]
            copy = remote(rows, rows, send_sem.at[step, len(started)], block_sem.at[step, block, part], peer)
            copy.start()
            started.append(copy)

        def arrived(block, part):
            rows = gat.at[block, pl.ds(part * owned, owned)]
            remote(rows, rows, send_sem.at[step, 0], block_sem.at[step, block, part], partner).wait_recv()

        for part in range(2):
            for peer in reversed(outer_peers):
                forward(me, peer, part)
            for peer in inner_peers:
                forward(me, peer, part)
            forward(me, partner, part)
        faces = [
            remote(send_l.at[step], got_l.at[step], face_sem.at[0, step, 0], face_sem.at[1, step, 0], around(-1)),
            remote(send_r.at[step], got_r.at[step], face_sem.at[0, step, 1], face_sem.at[1, step, 1], around(1)),
        ]
        for copy in faces:
            copy.start()

        if step == 0:
            cinv_copies[1].wait_recv()
            passed_on.start()
            finish_a()
            for copy in a_copies:
                copy.start()
        if step == 1:
            primal_columns()
        if step == ITERS - 1:
            uncorrected(changes)

        for part in range(2):
            for source in outer_back:
                block = at(source, y, core)
                arrived(block, part)
                for peer in inner_peers:
                    forward(block, peer, part)
                forward(block, partner, part)
        if step == 0:
            cinv_copies[0].wait()
            cinv_copies[1].wait_send()
            passed_on.wait()
            for slot, part in enumerate((cols_ref.at[0], cinv_ref, cols_ref.at[1], cols_ref.at[2])):
                high, low = split(part[...])
                ch_ref[slot * owned:(slot + 1) * owned, :] = high
                cl_ref[slot * owned:(slot + 1) * owned, :] = low
        for part in range(2):
            for m in range(1, inner):
                for source in [z] + outer_back:
                    block = at(source, returned(y, m, inner), core)
                    arrived(block, part)
                    forward(block, partner, part)
        for part in range(2):
            for source in [z] + outer_back:
                for m in range(inner):
                    arrived(at(source, y if m == 0 else returned(y, m, inner), 1 - core), part)

        for s in range(count):
            r_ref[s * owned:(s + 1) * owned, :] = (
                gat_ref[step, s, :owned, :] + gat_ref[step, (s - 1) % count, owned:, :]
            )
        coarse = product(ch_ref[...], cl_ref[...], r_ref[...])
        fill = jnp.zeros((padded - 2 * width - primal, columns), F32)

        def steps_of(slot):
            return jnp.concatenate([coarse[slot * owned:(slot + 2) * owned], fill], axis=0)

        q_before, q_own, q_after = steps_of(0), steps_of(1), steps_of(2)
        own = product(ah_ref[:2 * width, 2 * width:], al_ref[:2 * width, 2 * width:], q_own)
        if step == 0:
            for copy in a_copies:
                copy.wait()
        for copy in faces:
            copy.wait()
        after = product(*split(got_al[...]), q_after)
        lam = lam + DAMPING * ((values[:width] - own[:width]) - (got_l[step] - after))
        if step + 1 < ITERS:
            before = product(*split(got_ar[...]), q_before)
            lam_before = lam_before + DAMPING * ((got_r[step] - before) - (values[width:2 * width] - own[width:]))
        else:
            lam_ref[...] = lam
            q_ref[...] = q_own
        for copy in started:
            copy.wait_send()


def finish(pre_ref, kph_ref, kpl_ref, q_ref, lam_ref, u_ref, lam_out):
    u_ref[...] = pre_ref[...] - product(kph_ref[...], kpl_ref[...], q_ref[...])
    lam_out[...] = lam_ref[...]


NT = (((1,), (1,)), ((), ()))
NN = (((1,), (0,)), ((), ()))


def tall(x, high, low, dims):
    x_high, x_low = split(x)
    count = x.shape[0]
    both = lax.dot_general(jnp.concatenate([x_high, x_low], axis=0), high, dims, preferred_element_type=F32)
    return both[:count] + both[count:] + lax.dot_general(x_high, low, dims, preferred_element_type=F32)


def lanes_of(count):
    return -(-count // LANES) * LANES


def plane_kernel(
    count, primal, width, face_hbm, prim_hbm, slot_hbm, k_hbm, f_hbm, cinv_hbm, u_ref, lam_ref,
    face_s, prim_s, face_v, prim_v, slot_v, f_ref, k_ref, kh_ref, kl_ref, kph_ref, kpl_ref, e_ref, fh_ref, fl_ref, ks_ref,
    own_c, own_b, c_in, b_in, cinv_ref, cqh_ref, cql_ref, ac_ref, ap_ref, ar_ref, edge_ref,
    ach_ref, acl_ref, aph_ref, apl_ref, arh_ref, arl_ref, r_ref, face_out, face_in, x_out, x_in, q_out, q_in, lam_out, lam_in,
    in_sem, k_sem, c_sem, b_sem, cinv_send, cinv_recv, ac_send, ac_recv, ap_send, ap_recv, ar_send, ar_recv,
    halo_send, halo_recv, edge_sem, r_sem, face_sem, x_sem, q_sem, lam_sem,
):
    outer, inner = grid_of(count)
    plane = 2 * inner
    order, columns = f_ref.shape
    owned = primal // 2
    total = cinv_ref.shape[-1]
    tiles = k_sem.shape[0]
    tile = order // tiles
    share = columns // plane
    both = 2 * width
    wide = lanes_of(primal)
    span = r_ref.shape[-1]
    me = lax.axis_index("sub")
    mine = lax.rem(me, plane)
    z = me // plane
    core = lax.rem(me, 2)

    def at(z_, mine_):
        return z_ * plane + mine_

    partner = at(z, mine + 1 - 2 * core)
    across = [lax.rem(mine + 2 * m, plane) for m in range(1, inner)]
    across_peers = [at(z, other) for other in across]
    others = [lax.rem(mine + m, plane) for m in range(1, plane)]
    mates = [at(z, other) for other in others]
    turned = lax.rem(z, 2) if outer % 2 == 0 else 0

    def swapped(index, turn):
        return index + turn * (1 - 2 * lax.rem(index, 2))

    portion = swapped(mine, turned)

    def kin(place):
        return at(place, swapped(portion, lax.rem(place, 2) if outer % 2 == 0 else 0))

    beyond = [kin(lax.rem(z + m, outer)) for m in range(1, outer)]
    next_kin, last_kin = beyond[0], beyond[-1]
    after, before = [at(lax.rem(z + m, outer), mine) for m in (1, outer - 1)]
    far_first = beyond[::-1]
    if outer == 4:
        end = lax.rem(z + 1, outer) < 2
        mirror, skip, twin = outer - 1 - z, lax.rem(z + 2, outer), z + 1 - 2 * lax.rem(z, 2)
        far_first = [kin(place) for place in (jnp.where(end, mirror, skip), jnp.where(end, skip, mirror), twin)]

    def remote(src, dst, ssem, rsem, peer):
        return pltpu.make_async_remote_copy(
            src_ref=src, dst_ref=dst, send_sem=ssem, recv_sem=rsem, device_id={"sub": peer}, device_id_type=MESH
        )

    def send(src, dst, ssem, rsem, peer):
        remote(src, dst, ssem, rsem, peer).start()

    def arrived(ref, rsem):
        remote(ref, ref, r_sem.at[0, 0], rsem, partner).wait_recv()

    def sent(ref, ssem):
        remote(ref, ref, ssem, r_sem.at[0, 1], partner).wait_send()

    ints = [
        pltpu.make_async_copy(src, dst, in_sem.at[i])
        for i, (src, dst) in enumerate((
            (face_hbm, face_s), (prim_hbm, prim_s), (face_hbm, face_v), (prim_hbm, prim_v), (slot_hbm, slot_v)
        ))
    ]
    cinv_copy = pltpu.make_async_copy(cinv_hbm, cinv_ref.at[mine + 1], in_sem.at[5])
    f_copy = pltpu.make_async_copy(f_hbm, f_ref, in_sem.at[6])

    def k_copy(c):
        rows = pl.ds(c * tile, tile)
        return pltpu.make_async_copy(k_hbm.at[rows, :], k_ref.at[rows, :], k_sem.at[c])

    for copy in ints + [cinv_copy, f_copy]:
        copy.start()
    for c in range(tiles):
        k_copy(c).start()

    barrier = pltpu.get_barrier_semaphore()
    greeted = mates + beyond + ([after, before] if outer % 2 == 0 else [])
    for peer in greeted:
        pl.semaphore_signal(barrier, inc=1, device_id={"sub": peer}, device_id_type=MESH)

    with jax.named_scope("P_ints"):
        for copy in ints:
            copy.wait()
    square = (primal, primal)
    eye = lax.broadcasted_iota(jnp.int32, square, 0) == lax.broadcasted_iota(jnp.int32, square, 1)
    prim_col = jnp.sum(jnp.where(eye, prim_v[...].astype(F32), 0.0), axis=1, keepdims=True)
    slot_col = jnp.sum(jnp.where(eye, slot_v[...].astype(F32), 0.0), axis=1, keepdims=True)
    lane = lax.broadcasted_iota(jnp.int32, (primal, wide), 1).astype(F32)
    ordered = jnp.sum(jnp.where(slot_col == lane, prim_col + 1.0, 0.0), axis=0, keepdims=True) - 1.0
    ordering = jnp.where(lax.broadcasted_iota(jnp.int32, (wide, primal), 0) == slot_v[...], 1.0, 0.0).astype(BF16)

    def in_order(value):
        high, low = split(value)
        size = value.shape[1]
        pair = jnp.dot(ordering, jnp.concatenate([high, low], axis=1), preferred_element_type=F32)
        return pair[:, :size] + pair[:, size:]

    def one_hot_columns():
        right_ids, left_ids = face_v[0, 1:2, :], face_v[0, 0:1, :]
        ordered_ids = ordered.astype(jnp.int32)

        @pl.loop(0, tiles)
        def _(c):
            rows = pl.ds(pl.multiple_of(c * tile, tile), tile)
            near = lax.broadcasted_iota(jnp.int32, (tile, width), 0) + c * tile
            e_ref[rows, :width] = jnp.where(near == right_ids, 1.0, 0.0).astype(BF16)
            e_ref[rows, width:both] = jnp.where(near == left_ids, 1.0, 0.0).astype(BF16)
            near = lax.broadcasted_iota(jnp.int32, (tile, wide), 0) + c * tile
            e_ref[rows, both:] = jnp.where(near == ordered_ids, 1.0, 0.0).astype(BF16)

    def spread(buf, ssem, rsem, own):
        for peer in across_peers + [partner]:
            send(buf.at[own], buf.at[own], ssem, rsem.at[own], peer)

    def relay(buf, ssem, rsem):
        for other in across:
            arrived(buf.at[other], rsem.at[other])
            send(buf.at[other], buf.at[other], ssem, rsem.at[other], partner)

    def settle(buf, rsem):
        for other in [mine] + across:
            block = other + 1 - 2 * core
            arrived(buf.at[block], rsem.at[block])

    with jax.named_scope("P_onehot"):
        one_hot_columns()
    with jax.named_scope("P_barrier"):
        pl.semaphore_wait(barrier, len(greeted))
        cinv_copy.wait()
    halves = owned // 2

    def piece(block, half):
        return cinv_ref.at[block, pl.ds(half * halves, halves)]

    def send_far(half):
        send(piece(1 + core, half), piece(plane + 1 + core, half), halo_send.at[0], halo_recv.at[0, half], before)

    def send_near(half):
        send(piece(plane, half), piece(0, half), halo_send.at[1], halo_recv.at[1, half], after)

    def spread_coarse(half):
        for peer in across_peers + [partner]:
            rows = piece(mine + 1, half)
            send(rows, rows, cinv_send, cinv_recv.at[mine + 1, half], peer)

    def relay_coarse(half):
        for other in across:
            rows = piece(other + 1, half)
            arrived(rows, cinv_recv.at[other + 1, half])
            send(rows, rows, cinv_send, cinv_recv.at[other + 1, half], partner)
        pl.when(mine >= 2)(functools.partial(send_far, half))
        pl.when(mine == 1)(functools.partial(send_near, half))

    def settle_coarse():
        for half in range(2):
            for other in [mine] + across:
                block = other + 2 - 2 * core
                arrived(piece(block, half), cinv_recv.at[block, half])

    def last_edge():
        send(ac_ref.at[plane - 1, :, pl.ds(0, width)], edge_ref.at[0], edge_sem.at[0], edge_sem.at[1], after)

    def first_edge():
        send(ac_ref.at[0, :, pl.ds(width, width)], edge_ref.at[1], edge_sem.at[0], edge_sem.at[1], before)

    spread_coarse(0)
    for half in range(2):
        pl.when(mine < 2)(functools.partial(send_far, half))
        pl.when(mine == plane - 1)(functools.partial(send_near, half))
    with jax.named_scope("P_f"):
        f_copy.wait()
        high, low = split(f_ref[...])
        fh_ref[...] = high
        fl_ref[...] = low

    def halve(first_tile, last_tile):
        @pl.loop(first_tile, last_tile)
        def _(c):
            rows = pl.ds(pl.multiple_of(c * tile, tile), tile)
            high, low = split(k_ref[rows, :])
            kh_ref[rows, :] = high
            kl_ref[rows, :] = low

    with jax.named_scope("P_kwait"):
        for c in range(tiles):
            k_copy(c).wait()

    def picked(start, size, row_at):
        @pl.loop(0, size // 8)
        def _(i):
            base = pl.multiple_of(i * 8, 8)
            for j in range(8):
                ks_ref[pl.ds(start + base + j, 1), :] = k_ref[pl.ds(row_at(base + j), 1), :]

    def first(rows):
        high, low = split(ks_ref[rows, :])
        return product_parts(high, low, fh_ref[...], fl_ref[...])

    def columns_of(rows, picks):
        high, low = split(ks_ref[rows, :])
        return jnp.dot(high, picks, preferred_element_type=F32) + jnp.dot(low, picks, preferred_element_type=F32)

    def give(out, into, sems):
        for other, peer in zip(others, mates):
            send(out.at[swapped(other, turned)], into.at[mine], sems.at[0], sems.at[1], peer)
        into[mine] = out[portion]

    def give_back(out, into, sems):
        for other, peer in zip(others, mates):
            send(out.at[other], into.at[portion], sems.at[0], sems.at[1], peer)
        into[portion] = out[mine]

    def taken(into, sems):
        arrived(into.at[pl.ds(0, plane - 1)], sems.at[1])

    def assembled(parts):
        sums = None
        for i, part in enumerate(parts):
            part = jnp.concatenate([part, jnp.zeros((share, span - wide), F32)], axis=1)
            part = pltpu.roll(part, owned * i, 1) if i else part
            sums = part if sums is None else sums + part
        return sums

    def publish(step, parts):
        r_ref[step, z] = assembled(parts)
        for peer in far_first:
            rows = r_ref.at[step, z]
            send(rows, rows, r_sem.at[step, 0], r_sem.at[step, 1], peer)

    def faces(step, last_right, first_left):
        face_out[step, 0] = first_left
        send(face_out.at[step, 0], face_in.at[step, 0], face_sem.at[step, 0], face_sem.at[step, 1], last_kin)
        if step + 1 < ITERS:
            face_out[step, 1] = last_right
            send(face_out.at[step, 1], face_in.at[step, 1], face_sem.at[step, 0], face_sem.at[step, 1], next_kin)

    def face_part(ref, step):
        return ref.at[step] if step + 1 < ITERS else ref.at[step, pl.ds(0, 1)]

    urgent = jnp.where(mine == 0, 1, 0)

    def spread_half(half):
        for peer in across_peers + [partner]:
            rows = ar_ref.at[mine, half]
            send(rows, rows, ar_send, ar_recv.at[mine, half], peer)

    def relay_half(flip):
        for other in across:
            half = jnp.where(other == 0, 1 - flip, flip)
            rows = ar_ref.at[other, half]
            arrived(rows, ar_recv.at[other, half])
            send(rows, rows, ar_send, ar_recv.at[other, half], partner)

    def settle_half(flip):
        for other in [mine] + across:
            block = other + 1 - 2 * core
            half = jnp.where(block == 0, 1 - flip, flip)
            arrived(ar_ref.at[block, half], ar_recv.at[block, half])

    with jax.named_scope("P_first"):
        picked(both, primal, lambda i: prim_s[0, i])
        own_c[...] = in_order(first(slice(both, both + primal))).T.reshape(own_c.shape)
        give(own_c, c_in, c_sem)
    spread_coarse(1)
    with jax.named_scope("P_pick"):
        picked(0, width, lambda i: face_s[0, 1, i])
        picked(width, width, lambda i: face_s[0, 0, i])
    with jax.named_scope("P_ac"):
        found = columns_of(slice(0, both), e_ref[:, both:])
        ac_ref[mine, :, :width] = found[:width].T[:primal]
        ac_ref[mine, :, width:] = found[width:].T[:primal]
        spread(ac_ref, ac_send, ac_recv, mine)
    with jax.named_scope("P_relayc0"):
        relay_coarse(0)
    with jax.named_scope("P_cwait"):
        taken(c_in, c_sem)
    publish(0, [c_in[i] for i in range(plane)])
    pl.when(mine == plane - 1)(last_edge)
    pl.when(mine == 0)(first_edge)
    with jax.named_scope("P_firstb"):
        loads = first(slice(0, both))
        own_b[:, :, :width] = loads[:width].T.reshape(plane, share, width)
        own_b[:, :, width:] = loads[width:].T.reshape(plane, share, width)
        give(own_b, b_in, b_sem)
    with jax.named_scope("P_relayc1"):
        relay_coarse(1)
    with jax.named_scope("P_ap"):
        ap_ref[mine] = in_order(columns_of(slice(both, both + primal), e_ref[:, :both]))[:primal]
        spread(ap_ref, ap_send, ap_recv, mine)
    with jax.named_scope("P_ar"):
        found = columns_of(slice(0, both), e_ref[:, :both])
        ar_ref[mine, 0] = found[:width]
        ar_ref[mine, 1] = found[width:]
        spread_half(urgent)
        spread_half(1 - urgent)
    with jax.named_scope("P_relayac"):
        relay(ac_ref, ac_send, ac_recv)
    pl.when(mine == 1)(last_edge)
    pl.when(mine == 2)(first_edge)
    with jax.named_scope("P_bwait"):
        taken(b_in, b_sem)
    faces(0, b_in[plane - 1, :, :width], b_in[0, :, width:])
    with jax.named_scope("P_halve"):
        halve(0, tiles)

    def primal_columns(first_tile, last_tile):
        picks = e_ref[:, both:]

        @pl.loop(first_tile, last_tile)
        def _(c):
            rows = pl.ds(pl.multiple_of(c * tile, tile), tile)
            kph_ref[rows, :] = jnp.dot(kh_ref[rows, :], picks, preferred_element_type=F32).astype(BF16)
            kpl_ref[rows, :] = jnp.dot(kl_ref[rows, :], picks, preferred_element_type=F32).astype(BF16)

    last_row = cqh_ref.shape[0]

    def coarse_rows(block, start):
        for ref, part in zip((cqh_ref, cql_ref), split(cinv_ref[block])):
            ref[start:start + owned, :] = part

    def halves_of(refs, src):
        for i in range(plane):
            for ref, part in zip(refs, split(src[i])):
                ref[i, :primal, :] = part
                ref[i, primal:, :] = jnp.zeros((wide - primal, both), BF16)

    early = tiles // 3
    sooner = jnp.where(mine < 2, early // 2, early)
    with jax.named_scope("P_halo"):
        settle_coarse()
        near = cinv_ref.at[0]
        for half in range(2):
            rows = piece(plane + 1 + core, half)
            arrived(rows, halo_recv.at[0, half])
            send(rows, rows, halo_send.at[0], halo_recv.at[3, half], partner)

        @pl.when(core == 1)
        def _():
            for half in range(2):
                arrived(piece(0, half), halo_recv.at[1, half])
            send(near, near, halo_send.at[1], halo_recv.at[2, 1], partner)

    with jax.named_scope("P_cq"):
        for ref in (cqh_ref, cql_ref):
            ref[plane * owned:, :] = jnp.zeros((last_row - plane * owned, total), BF16)
        for i in range(plane):
            coarse_rows(i + 1, i * owned)
    with jax.named_scope("P_settleac"):
        settle(ac_ref, ac_recv)
        halves_of((ach_ref, acl_ref), ac_ref)
    with jax.named_scope("P_edge0"):
        rows = edge_ref.at[1 - core]
        arrived(rows, edge_sem.at[1])
        send(rows, rows, edge_sem.at[3], edge_sem.at[2], partner)
    with jax.named_scope("P_relayap"):
        relay(ap_ref, ap_send, ap_recv)
    def coarse_halos():
        for half in range(2):
            arrived(piece(plane + 2 - core, half), halo_recv.at[3, half])

        @pl.when(core == 0)
        def _():
            arrived(near, halo_recv.at[2, 1])

        coarse_rows(plane + 1, plane * owned)
        coarse_rows(plane + 2, (plane + 1) * owned)
        coarse_rows(0, last_row - owned)

    def uncorrected(first_tile, last_tile):
        @pl.loop(first_tile, last_tile)
        def _(c):
            rows = pl.ds(pl.multiple_of(c * tile, tile), tile)
            u_ref[rows, :] = product_parts(kh_ref[rows, :], kl_ref[rows, :], fh_ref[...], fl_ref[...])

    def changed_loads():
        high, low = split(x_in[...].reshape(columns, both))
        moved = lax.dot_general(
            e_ref[:, :both], jnp.concatenate([high, low], axis=0), NT, preferred_element_type=F32
        )
        high, low = split(f_ref[...] + (moved[:, :columns] + moved[:, columns:]))
        fh_ref[...] = high
        fl_ref[...] = low

    def shifted(value, block):
        return (pltpu.roll(value, value.shape[1] - owned * block, 1) if block > 0 else pltpu.roll(
            value, owned, 1) if block else value)[:, :wide]

    def padded(value):
        return jnp.concatenate([value, jnp.zeros((wide - primal, value.shape[1]), F32)], axis=0)

    lam = [jnp.zeros((share, width), F32)] * (plane + 1)
    values = [b_in[i] for i in range(plane)]
    edges = None
    for step in range(ITERS):
        if step == ITERS - 1:
            with jax.named_scope("P_primcol1"):
                primal_columns(tiles - early, tiles)
            with jax.named_scope("P_xwait"):
                arrived(x_in.at[pl.ds(0, plane - 1)], x_sem.at[1])
                changed_loads()
            with jax.named_scope("P_uncorr0"):
                uncorrected(0, sooner)
        with jax.named_scope(f"P_rwait{step}"):
            arrived(r_ref.at[step, pl.ds(0, outer - 1)], r_sem.at[step, 1])
        with jax.named_scope(f"P_coarse{step}"):
            sums = None
            for i in range(outer):
                part = jnp.concatenate([r_ref[step, i], jnp.zeros((share, total - span), F32)], axis=1)
                part = pltpu.roll(part, plane * owned * i, 1) if i else part
                sums = part if sums is None else sums + part
            if step:
                coarse = tall(sums, cqh_ref[...], cql_ref[...], NT)
                moved = []
            else:
                own = tall(sums, cqh_ref[:lanes_of(plane * owned)], cql_ref[:lanes_of(plane * owned)], NT)
                moved = [values[i] - tall(shifted(own, i), ach_ref[i], acl_ref[i], NN) for i in range(plane - 1)]
                with jax.named_scope("P_halo2"):
                    coarse_halos()
                low_row = (plane - 1) * owned // LANES * LANES
                rest = tall(sums, cqh_ref[low_row:], cql_ref[low_row:], NT)
                coarse = jnp.concatenate([own[:, :low_row], rest], axis=1)
            steps = [shifted(coarse, i - 1) for i in range(plane + 2)]
            if step == ITERS - 1:
                for i in range(plane):
                    q_out[i] = steps[i + 1]
                give_back(q_out, q_in, q_sem)
        if edges is None:
            with jax.named_scope("P_edge"):
                arrived(edge_ref.at[core], edge_sem.at[2])
                edges = [split(padded(edge_ref[i])) for i in range(2)]
        with jax.named_scope(f"P_faces{step}"):
            arrived(face_part(face_in, step), face_sem.at[step, 1])
        with jax.named_scope(f"P_update{step}"):
            moved += [values[i] - tall(steps[i + 1], ach_ref[i], acl_ref[i], NN) for i in range(len(moved), plane)]
            right = [part[:, :width] for part in moved]
            left = [part[:, width:] for part in moved]
            left.append(face_in[step, 0] - tall(steps[plane + 1], *edges[1], NN))
            lam_next = [lam[i + 1] + DAMPING * (right[i] - left[i + 1]) for i in range(plane)]
            if step + 1 < ITERS:
                ahead = face_in[step, 1] - tall(steps[0], *edges[0], NN)
                lam_next = [lam[0] + DAMPING * (ahead - left[0])] + lam_next
            else:
                for i in range(plane):
                    lam_out[i] = lam_next[i]
                give_back(lam_out, lam_in, lam_sem)
                break
            lam = lam_next
            if step == 0:
                with jax.named_scope("P_settleap"):
                    settle(ap_ref, ap_recv)
                    halves_of((aph_ref, apl_ref), ap_ref)
            changes = [jnp.concatenate([-lam[i + 1], lam[i]], axis=1) for i in range(plane)]
            publish(step + 1, [
                c_in[i] + tall(changes[i], aph_ref[i], apl_ref[i], NT) for i in range(plane)
            ])
            if step == ITERS - 2:
                for i in range(plane):
                    x_out[i] = changes[i]
                give_back(x_out, x_in, x_sem)
        if step == 0:
            with jax.named_scope("P_relayr0"):
                relay_half(0)
                settle_half(0)
                for i, half in ((plane - 1, 0), (0, 1)):
                    rows = slice(half * width, (half + 1) * width)
                    for ref, part in zip((arh_ref, arl_ref), split(ar_ref[i, half])):
                        ref[i, rows] = part
            with jax.named_scope("P_facevalues"):
                last_right = tall(changes[-1], arh_ref[plane - 1, :width], arl_ref[plane - 1, :width], NT)
                first_left = tall(changes[0], arh_ref[0, width:], arl_ref[0, width:], NT)
                faces(1, b_in[plane - 1, :, :width] + last_right, b_in[0, :, width:] + first_left)
            with jax.named_scope("P_primcol0"):
                primal_columns(0, early)
            with jax.named_scope("P_relayr1"):
                relay_half(1)
            with jax.named_scope("P_primcol0"):
                primal_columns(early, tiles - early)
            with jax.named_scope("P_settler1"):
                settle_half(1)
                for i in range(plane):
                    for half in range(2):
                        if (i, half) not in ((plane - 1, 0), (0, 1)):
                            rows = slice(half * width, (half + 1) * width)
                            for ref, part in zip((arh_ref, arl_ref), split(ar_ref[i, half])):
                                ref[i, rows] = part
        with jax.named_scope(f"P_values{step}"):
            values = [b_in[i] + tall(changes[i], arh_ref[i], arl_ref[i], NT) for i in range(plane)]
            if step:
                faces(step + 1, values[plane - 1][:, :width], values[0][:, width:])

    with jax.named_scope("P_uncorr1"):
        uncorrected(sooner, tiles)
    with jax.named_scope("P_qwait"):
        arrived(q_in.at[pl.ds(0, plane - 1)], q_sem.at[1])
    with jax.named_scope("P_last"):
        high, low = split(q_in[...].reshape(columns, wide).T)
        pair = jnp.concatenate([high, low], axis=1)
        for c in range(tiles):
            rows = pl.ds(c * tile, tile)
            step = jnp.dot(kph_ref[rows, :], pair, preferred_element_type=F32)
            step = step[:, :columns] + step[:, columns:]
            u_ref[rows, :] = u_ref[rows, :] - (step + jnp.dot(kpl_ref[rows, :], high, preferred_element_type=F32))

    with jax.named_scope("P_lamwait"):
        arrived(lam_in.at[pl.ds(0, plane - 1)], lam_sem.at[1])
        lam_ref[...] = lam_in[...].reshape(columns, width).T
    with jax.named_scope("P_sent"):
        others_part = pl.ds(0, plane - 1)
        sent(own_c.at[others_part], c_sem.at[0])
        sent(own_b.at[others_part], b_sem.at[0])
        sent(cinv_ref.at[others_part], cinv_send)
        for ref, sem in ((ac_ref, ac_send), (ap_ref, ap_send), (ar_ref, ar_send)):
            sent(ref.at[others_part], sem)
        sent(cinv_ref.at[pl.ds(0, 2)], halo_send.at[0])

        @pl.when(core == 1)
        def _():
            sent(cinv_ref.at[pl.ds(0, 2)], halo_send.at[1])

        sent(edge_ref.at[0], edge_sem.at[0])
        sent(edge_ref.at[0], edge_sem.at[3])
        for step in range(ITERS):
            sent(r_ref.at[step, pl.ds(0, outer - 1)], r_sem.at[step, 0])
            sent(face_part(face_out, step), face_sem.at[step, 0])
        sent(x_out.at[others_part], x_sem.at[0])
        sent(q_out.at[others_part], q_sem.at[0])
        sent(lam_out.at[others_part], lam_sem.at[0])


def plane_finish(u_ref, lam_ref, u_hbm, lam_hbm, sem):
    copies = [pltpu.make_async_copy(u_ref, u_hbm, sem.at[0]), pltpu.make_async_copy(lam_ref, lam_hbm, sem.at[1])]
    for copy in copies:
        copy.start()
    for copy in copies:
        copy.wait()


def size_of(buffers):
    return sum((4 if kind == F32 else 2) * functools.reduce(lambda a, b: a * b, size) for size, kind in buffers)


def plane_scratch(count, order, columns, owned, total, width, primal):
    outer, inner = grid_of(count)
    plane = 2 * inner
    both = 2 * width
    wide = lanes_of(primal)
    span = lanes_of((plane + 1) * owned)
    share = columns // plane
    pairs = lanes_of((plane + 3) * owned)
    return plane, [
        ((order, columns), F32),
        ((order, order), F32),
        ((order, order), BF16),
        ((order, order), BF16),
        ((order, wide), BF16),
        ((order, wide), BF16),
        ((order, both + wide), BF16),
        ((order, columns), BF16),
        ((order, columns), BF16),
        ((both + primal, order), F32),
        ((plane, share, wide), F32),
        ((plane, share, both), F32),
        ((plane, share, wide), F32),
        ((plane, share, both), F32),
        ((plane + 3, owned, total), F32),
        ((pairs, total), BF16),
        ((pairs, total), BF16),
        ((plane, primal, both), F32),
        ((plane, primal, both), F32),
        ((plane, 2, width, both), F32),
        ((2, primal, width), F32),
        ((plane, wide, both), BF16),
        ((plane, wide, both), BF16),
        ((plane, wide, both), BF16),
        ((plane, wide, both), BF16),
        ((plane, both, both), BF16),
        ((plane, both, both), BF16),
        ((ITERS, outer, share, span), F32),
        ((ITERS, 2, share, width), F32),
        ((ITERS, 2, share, width), F32),
        ((plane, share, both), F32),
        ((plane, share, both), F32),
        ((plane, share, wide), F32),
        ((plane, share, wide), F32),
        ((plane, share, width), F32),
        ((plane, share, width), F32),
    ]


def planar(condensed, eigen_loads, coarse_inverse, face_rows, primal_rows, primal_slot):
    count = lax.axis_size("sub")
    order, columns = eigen_loads.shape
    owned, total = coarse_inverse.shape
    width = face_rows.shape[2]
    primal = primal_rows.shape[1]
    outer, inner = grid_of(count)
    tile = 256 if order % 256 == 0 else order
    tiles = order // tile
    plane, buffers = plane_scratch(count, order, columns, owned, total, width, primal)
    needed = size_of(buffers)
    wide = lanes_of(primal)
    dma = pltpu.SemaphoreType.DMA
    vmem = pl.BlockSpec(memory_space=pltpu.VMEM)
    shape = jax.ShapeDtypeStruct
    held = [
        pltpu.with_memory_space_constraint(value, pltpu.HBM)
        for value in (face_rows, primal_rows, primal_slot, condensed, eigen_loads, coarse_inverse)
    ]
    parts = pl.pallas_call(
        functools.partial(plane_kernel, count, primal, width),
        out_shape=(
            shape((order, columns), F32),
            shape((width, columns), F32),
        ),
        in_specs=[pl.BlockSpec(memory_space=pltpu.HBM)] * 6,
        out_specs=(vmem,) * 2,
        scratch_shapes=[
            pltpu.SMEM(face_rows.shape, jnp.int32),
            pltpu.SMEM(primal_rows.shape, jnp.int32),
            pltpu.VMEM(face_rows.shape, jnp.int32),
            pltpu.VMEM(primal_rows.shape, jnp.int32),
            pltpu.VMEM(primal_slot.shape, jnp.int32),
        ] + [pltpu.VMEM(size, kind) for size, kind in buffers] + [
            dma((7,)),
            dma((tiles,)),
            dma((2,)),
            dma((2,)),
            dma(()),
            dma((plane + 1, 2)),
            dma(()),
            dma((plane,)),
            dma(()),
            dma((plane,)),
            dma(()),
            dma((plane, 2)),
            dma((2,)),
            dma((4, 2)),
            dma((4,)),
            dma((ITERS, 2)),
            dma((ITERS, 2)),
            dma((2,)),
            dma((2,)),
            dma((2,)),
        ],
        compiler_params=pltpu.CompilerParams(
            collective_id=0, has_side_effects=True, vmem_limit_bytes=min(PLANE_LIMIT, needed + needed // 3)
        ),
    )(*held)
    return pl.pallas_call(
        plane_finish,
        out_shape=(shape((order, columns), F32), shape((width, columns), F32)),
        in_specs=[vmem] * 2,
        out_specs=(pl.BlockSpec(memory_space=pltpu.HBM),) * 2,
        scratch_shapes=[dma((2,))],
        compiler_params=pltpu.CompilerParams(vmem_limit_bytes=4 * order * columns * 4),
    )(*parts)


def fits_plane(condensed, eigen_loads, coarse_inverse, face_rows, primal_rows, primal_slot):
    count = lax.axis_size("sub")
    order, columns = eigen_loads.shape
    owned, total = coarse_inverse.shape
    width = face_rows.shape[2]
    primal = primal_rows.shape[1]
    outer, inner = grid_of(count)
    plane = 2 * inner
    if outer < 2 or inner != 2 or columns % (8 * plane) or total % LANES or width % LANES or owned % 16 or primal != 2 * owned:
        return False
    _, buffers = plane_scratch(count, order, columns, owned, total, width, primal)
    return size_of(buffers) <= PLANE_LIMIT * 3 // 4


def local(*values):
    return (planar if fits_plane(*values) else general)(*values)


def general(condensed, eigen_loads, coarse_inverse, face_rows, primal_rows, primal_slot):
    count = lax.axis_size("sub")
    order, columns = eigen_loads.shape
    owned, total = coarse_inverse.shape
    width = face_rows.shape[2]
    primal = primal_rows.shape[1]
    padded = 2 * width + -(-primal // LANES) * LANES
    outer, inner = grid_of(count)
    corner_width = padded - 2 * width
    tile = 256 if order % 256 == 0 else order
    sends = (outer - 1) + (inner - 1) * outer + outer * inner
    dma = pltpu.SemaphoreType.DMA
    vmem = pl.BlockSpec(memory_space=pltpu.VMEM)
    face = pltpu.VMEM((ITERS, width, columns), F32)
    corner = pltpu.VMEM((width, padded - 2 * width), F32)
    smem = pl.BlockSpec(memory_space=pltpu.SMEM)
    needed = 8 * order * (order + padded + 2 * columns) + 4 * padded * (order + columns + padded)
    needed += 4 * owned * total * 8 + 4 * columns * (ITERS * (count * primal + 4 * width) + total)
    needed += 4 * order * (columns + 2 * corner_width) + 4 * columns * (order + 8 * width)
    shape = jax.ShapeDtypeStruct
    held = [
        pltpu.with_memory_space_constraint(value, pltpu.HBM)
        for value in (face_rows, primal_rows, primal_slot, condensed, eigen_loads, coarse_inverse)
    ]
    parts = pl.pallas_call(
        functools.partial(kernel, count, primal, width),
        out_shape=(
            shape((order, columns), F32),
            shape((order, corner_width), BF16),
            shape((order, corner_width), BF16),
            shape((corner_width, columns), F32),
            shape((width, columns), F32),
        ),
        in_specs=[smem, smem] + [pl.BlockSpec(memory_space=pltpu.HBM)] * 6,
        out_specs=(vmem,) * 5,
        scratch_shapes=[
            pltpu.VMEM(face_rows.shape, jnp.int32),
            pltpu.VMEM(primal_rows.shape, jnp.int32),
            pltpu.VMEM(primal_slot.shape, jnp.int32),
            pltpu.VMEM((order, columns), F32),
            pltpu.VMEM((owned, total), F32),
            dma((5,)),
            pltpu.VMEM((order, order), F32),
            pltpu.VMEM((order, order), BF16),
            pltpu.VMEM((order, order), BF16),
            pltpu.VMEM((order, padded), BF16),
            pltpu.VMEM((order, columns), BF16),
            pltpu.VMEM((order, columns), BF16),
            pltpu.VMEM((padded, order), F32),
            pltpu.VMEM((padded, columns), F32),
            pltpu.VMEM((padded, padded), BF16),
            pltpu.VMEM((padded, padded), BF16),
            pltpu.VMEM((3, owned, total), F32),
            pltpu.VMEM((4 * owned, total), BF16),
            pltpu.VMEM((4 * owned, total), BF16),
            pltpu.VMEM((ITERS, count, primal, columns), F32),
            pltpu.VMEM((total, columns), F32),
            face, face, face, face,
            corner, corner, corner, corner,
            dma((order // tile,)),
            dma((ITERS, 2 * sends)),
            dma((ITERS, count, 2)),
            dma((2, ITERS, 2)),
            dma((3,)),
            dma((3,)),
            dma((2,)),
            dma((2,)),
        ],
        compiler_params=pltpu.CompilerParams(
            collective_id=0, has_side_effects=True, vmem_limit_bytes=min(VMEM_LIMIT, needed + needed // 4)
        ),
    )(face_rows, primal_rows, *held)
    return pl.pallas_call(
        finish,
        out_shape=(shape((order, columns), F32), shape((width, columns), F32)),
        in_specs=[vmem] * 5,
        out_specs=(vmem, vmem),
        compiler_params=pltpu.CompilerParams(vmem_limit_bytes=4 * order * columns * 8),
    )(*parts)


def solution(mesh):
    placed = (
        P(("rve", "sub"), None),
        P(("rve", "sub"), None),
        P(("rve", "sub"), None),
        P("sub", None, None),
        P("sub", None),
        P("sub", None),
    )
    return jax.shard_map(
        local,
        mesh=mesh,
        in_specs=placed,
        out_specs=(P(("rve", "sub"), None), P(("rve", "sub"), None)),
        check_vma=False,
    )
```

```python
import functools

import jax
import jax.numpy as jnp
from jax import lax
from jax.experimental import pallas as pl
from jax.experimental.pallas import tpu as pltpu
from jax.sharding import PartitionSpec as P

ITERS = 3
DAMPING = 0.5
VMEM_LIMIT = 67043328
MESH = pl.DeviceIdType.MESH
F32 = jnp.float32
BF16 = jnp.bfloat16
LANES = 128
PLANE_LIMIT = 60 * 1024 * 1024


def grid_of(count):
    chips = count // 2
    inner = 1
    while (2 * inner) ** 2 <= chips and chips % (2 * inner) == 0:
        inner *= 2
    return chips // inner, inner


def flipped(index, mask, count):
    if count & (count - 1):
        return lax.rem(index + count - mask, count)
    out = 0
    bit = 1
    while bit < count:
        own = lax.rem(index // bit, 2)
        out = out + bit * ((1 - own) if mask & bit else own)
        bit *= 2
    return out


def returned(index, mask, count):
    if count & (count - 1):
        return lax.rem(index + mask, count)
    return flipped(index, mask, count)


def split(value):
    high = value.astype(BF16)
    return high, (value - high.astype(F32)).astype(BF16)


def product(high, low, value):
    value_high, value_low = split(value)
    return product_parts(high, low, value_high, value_low)


def product_parts(high, low, value_high, value_low):
    width = value_high.shape[1]
    both = jnp.dot(high, jnp.concatenate([value_high, value_low], axis=1), preferred_element_type=F32)
    return both[:, :width] + both[:, width:] + jnp.dot(low, value_high, preferred_element_type=F32)


def kernel(
    count, primal, width, face_s, prim_s, face_hbm, prim_hbm, slot_hbm, k_hbm, f_hbm, cinv_hbm, pre_ref, kph_ref, kpl_ref, q_ref, lam_ref,
    face_v, prim_v, slot_v, f_ref, cinv_ref, in_sem, k_ref, kh_ref, kl_ref, e_ref, fh_ref, fl_ref, ks_ref, first_ref, ah_ref, al_ref, cols_ref, ch_ref, cl_ref,
    gat_ref, r_ref, send_r, send_l, got_r, got_l, send_ar, send_al, got_ar, got_al,
    k_sem, send_sem, block_sem, face_sem, cinv_send, cinv_recv, a_send, a_recv,
):
    outer, inner = grid_of(count)
    order, columns = f_ref.shape
    owned = primal // 2
    tile = order // k_sem.shape[0]
    padded = e_ref.shape[1]
    me = lax.axis_index("sub")
    core = lax.rem(me, 2)
    y = lax.rem(me // 2, inner)
    z = me // (2 * inner)

    def at(z_, y_, core_):
        return (z_ * inner + y_) * 2 + core_

    def around(steps):
        return lax.rem(me + (steps + count), count)

    def k_copy(c):
        rows = pl.ds(c * tile, tile)
        return pltpu.make_async_copy(k_hbm.at[rows, :], k_ref.at[rows, :], k_sem.at[c])

    held = [
        pltpu.make_async_copy(src, dst, in_sem.at[i])
        for i, (src, dst) in enumerate((
            (f_hbm, f_ref), (cinv_hbm, cinv_ref), (face_hbm, face_v), (prim_hbm, prim_v), (slot_hbm, slot_v)
        ))
    ]
    for copy in held:
        copy.start()
    for c in range(k_sem.shape[0]):
        k_copy(c).start()

    outer_peers = [at(flipped(z, m, outer), y, core) for m in range(1, outer)]
    outer_back = [returned(z, m, outer) for m in range(1, outer)]
    inner_peers = [at(z, flipped(y, m, inner), core) for m in range(1, inner)]
    partner = at(z, y, 1 - core)
    ring = [around(d) for d in (-1, 1)]

    barrier = pltpu.get_barrier_semaphore()
    greeted = outer_peers + inner_peers + [partner] + ring
    if outer & (outer - 1):
        greeted = greeted + [at(b, y, core) for b in outer_back]
    for peer in greeted:
        pl.semaphore_signal(barrier, inc=1, device_id={"sub": peer}, device_id_type=MESH)

    def remote(src, dst, ssem, rsem, peer):
        return pltpu.make_async_remote_copy(
            src_ref=src, dst_ref=dst, send_sem=ssem, recv_sem=rsem, device_id={"sub": peer}, device_id_type=MESH
        )

    cinv_copies = [
        remote(cinv_ref, cols_ref.at[slot], cinv_send.at[slot], cinv_recv.at[slot], around(d))
        for slot, d in ((0, 1), (1, -1))
    ]
    passed_on = remote(cols_ref.at[1], cols_ref.at[2], cinv_send.at[2], cinv_recv.at[2], around(-1))

    for copy in held:
        copy.wait()

    square = (primal, primal)
    eye = lax.broadcasted_iota(jnp.int32, square, 0) == lax.broadcasted_iota(jnp.int32, square, 1)
    prim_col = jnp.sum(jnp.where(eye, prim_v[...].astype(F32), 0.0), axis=1, keepdims=True)
    slot_col = jnp.sum(jnp.where(eye, slot_v[...].astype(F32), 0.0), axis=1, keepdims=True)
    corner_width = padded - 2 * width
    lane = lax.broadcasted_iota(jnp.int32, (primal, corner_width), 1).astype(F32)
    ordered = jnp.sum(jnp.where(slot_col == lane, prim_col + 1.0, 0.0), axis=0, keepdims=True) - 1.0
    ordering = jnp.where(lax.broadcasted_iota(jnp.int32, square, 0) == slot_v[...], 1.0, 0.0).astype(BF16)

    fh, fl = split(f_ref[...])
    fh_ref[...] = fh
    fl_ref[...] = fl

    def stream(first_tile, last_tile):
        @pl.loop(first_tile, last_tile)
        def _(c):
            k_copy(c).wait()
            rows = pl.ds(pl.multiple_of(c * tile, tile), tile)
            high, low = split(k_ref[rows, :])
            kh_ref[rows, :] = high
            kl_ref[rows, :] = low
            pre_ref[rows, :] = product_parts(high, low, fh_ref[...], fl_ref[...])

    half = 1
    stream(0, half)
    pl.semaphore_wait(barrier, len(greeted))
    for copy in cinv_copies:
        copy.start()
    stream(half, order // tile)

    used = 2 * width + primal

    def picked(to_ref, from_ref):
        def rows_of(start, size, row_at):
            @pl.loop(0, size // 8)
            def _(i):
                base = pl.multiple_of(i * 8, 8)
                for j in range(8):
                    to_ref[pl.ds(start + base + j, 1), :] = from_ref[pl.ds(row_at(base + j), 1), :]

        rows_of(0, width, lambda i: face_s[0, 1, i])
        rows_of(width, width, lambda i: face_s[0, 0, i])
        rows_of(2 * width, primal, lambda i: prim_s[0, i])

    def in_order(value):
        high, low = split(value)
        half_width = value.shape[1]
        both = jnp.dot(ordering, jnp.concatenate([high, low], axis=1), preferred_element_type=F32)
        return both[:, :half_width] + both[:, half_width:]

    picked(first_ref, pre_ref)
    empty = jnp.zeros((padded - used, columns), F32)
    first = jnp.concatenate([first_ref[:2 * width], in_order(first_ref[2 * width:used]), empty], axis=0)

    def one_hot_columns():
        right_ids, left_ids = face_v[0, 1:2, :], face_v[0, 0:1, :]
        ordered_ids = ordered.astype(jnp.int32)

        @pl.loop(0, order // tile)
        def _(c):
            rows = pl.ds(pl.multiple_of(c * tile, tile), tile)
            near = lax.broadcasted_iota(jnp.int32, (tile, width), 0) + c * tile
            e_ref[rows, :width] = jnp.where(near == right_ids, 1.0, 0.0).astype(BF16)
            e_ref[rows, width:2 * width] = jnp.where(near == left_ids, 1.0, 0.0).astype(BF16)
            near = lax.broadcasted_iota(jnp.int32, (tile, corner_width), 0) + c * tile
            e_ref[rows, 2 * width:] = jnp.where(near == ordered_ids, 1.0, 0.0).astype(BF16)

    def finish_a():
        one_hot_columns()
        if padded > used:
            ks_ref[used:, :] = jnp.zeros((padded - used, order), F32)
        picked(ks_ref, k_ref)
        high, low = split(ks_ref[...])
        parts = []
        for part, out in ((high, ah_ref), (low, al_ref)):
            found = jnp.dot(part, e_ref[...], preferred_element_type=F32)
            out[:2 * width, :] = found[:2 * width].astype(BF16)
            out[2 * width:used, :] = jnp.dot(
                ordering, found[2 * width:used].astype(BF16), preferred_element_type=F32
            ).astype(BF16)
            if padded > used:
                out[used:, :] = jnp.zeros((padded - used, padded), BF16)
            parts.append(found[:2 * width, 2 * width:])
        corner = parts[0] + parts[1]
        send_ar[...] = corner[:width]
        send_al[...] = corner[width:]

    def primal_columns():
        picks = e_ref[:, 2 * width:]

        @pl.loop(0, order // tile)
        def _(c):
            rows = pl.ds(pl.multiple_of(c * tile, tile), tile)
            kph_ref[rows, :] = jnp.dot(kh_ref[rows, :], picks, preferred_element_type=F32).astype(BF16)
            kpl_ref[rows, :] = jnp.dot(kl_ref[rows, :], picks, preferred_element_type=F32).astype(BF16)

    def uncorrected(changes):
        high, low = split(changes)
        spread = jnp.dot(e_ref[:, :2 * width], jnp.concatenate([high, low], axis=1), preferred_element_type=F32)
        loads = f_ref[...] + (spread[:, :columns] + spread[:, columns:])
        high, low = split(loads)
        fh_ref[...] = high
        fl_ref[...] = low

        @pl.loop(0, order // tile)
        def _(c):
            rows = pl.ds(pl.multiple_of(c * tile, tile), tile)
            pre_ref[rows, :] = product_parts(kh_ref[rows, :], kl_ref[rows, :], fh_ref[...], fl_ref[...])

    a_copies = [
        remote(send_al, got_al, a_send.at[0], a_recv.at[0], around(-1)),
        remote(send_ar, got_ar, a_send.at[1], a_recv.at[1], around(1)),
    ]

    lam = jnp.zeros((width, columns), F32)
    lam_before = jnp.zeros((width, columns), F32)
    values = first
    changes = None
    for step in range(ITERS):
        if step:
            changes = jnp.concatenate([-lam, lam_before], axis=0)
            values = first + product(ah_ref[:, :2 * width], al_ref[:, :2 * width], changes)
        gat = gat_ref.at[step]
        gat_ref[step, me] = values[2 * width:2 * width + primal]
        send_r[step] = values[:width]
        send_l[step] = values[width:2 * width]
        started = []

        def forward(block, peer, part):
            rows = gat.at[block, pl.ds(part * owned, owned)]
            copy = remote(rows, rows, send_sem.at[step, len(started)], block_sem.at[step, block, part], peer)
            copy.start()
            started.append(copy)

        def arrived(block, part):
            rows = gat.at[block, pl.ds(part * owned, owned)]
            remote(rows, rows, send_sem.at[step, 0], block_sem.at[step, block, part], partner).wait_recv()

        for part in range(2):
            for peer in reversed(outer_peers):
                forward(me, peer, part)
            for peer in inner_peers:
                forward(me, peer, part)
            forward(me, partner, part)
        faces = [
            remote(send_l.at[step], got_l.at[step], face_sem.at[0, step, 0], face_sem.at[1, step, 0], around(-1)),
            remote(send_r.at[step], got_r.at[step], face_sem.at[0, step, 1], face_sem.at[1, step, 1], around(1)),
        ]
        for copy in faces:
            copy.start()

        if step == 0:
            cinv_copies[1].wait_recv()
            passed_on.start()
            finish_a()
            for copy in a_copies:
                copy.start()
        if step == 1:
            primal_columns()
        if step == ITERS - 1:
            uncorrected(changes)

        for part in range(2):
            for source in outer_back:
                block = at(source, y, core)
                arrived(block, part)
                for peer in inner_peers:
                    forward(block, peer, part)
                forward(block, partner, part)
        if step == 0:
            cinv_copies[0].wait()
            cinv_copies[1].wait_send()
            passed_on.wait()
            for slot, part in enumerate((cols_ref.at[0], cinv_ref, cols_ref.at[1], cols_ref.at[2])):
                high, low = split(part[...])
                ch_ref[slot * owned:(slot + 1) * owned, :] = high
                cl_ref[slot * owned:(slot + 1) * owned, :] = low
        for part in range(2):
            for m in range(1, inner):
                for source in [z] + outer_back:
                    block = at(source, returned(y, m, inner), core)
                    arrived(block, part)
                    forward(block, partner, part)
        for part in range(2):
            for source in [z] + outer_back:
                for m in range(inner):
                    arrived(at(source, y if m == 0 else returned(y, m, inner), 1 - core), part)

        for s in range(count):
            r_ref[s * owned:(s + 1) * owned, :] = (
                gat_ref[step, s, :owned, :] + gat_ref[step, (s - 1) % count, owned:, :]
            )
        coarse = product(ch_ref[...], cl_ref[...], r_ref[...])
        fill = jnp.zeros((padded - 2 * width - primal, columns), F32)

        def steps_of(slot):
            return jnp.concatenate([coarse[slot * owned:(slot + 2) * owned], fill], axis=0)

        q_before, q_own, q_after = steps_of(0), steps_of(1), steps_of(2)
        own = product(ah_ref[:2 * width, 2 * width:], al_ref[:2 * width, 2 * width:], q_own)
        if step == 0:
            for copy in a_copies:
                copy.wait()
        for copy in faces:
            copy.wait()
        after = product(*split(got_al[...]), q_after)
        lam = lam + DAMPING * ((values[:width] - own[:width]) - (got_l[step] - after))
        if step + 1 < ITERS:
            before = product(*split(got_ar[...]), q_before)
            lam_before = lam_before + DAMPING * ((got_r[step] - before) - (values[width:2 * width] - own[width:]))
        else:
            lam_ref[...] = lam
            q_ref[...] = q_own
        for copy in started:
            copy.wait_send()


def finish(pre_ref, kph_ref, kpl_ref, q_ref, lam_ref, u_ref, lam_out):
    u_ref[...] = pre_ref[...] - product(kph_ref[...], kpl_ref[...], q_ref[...])
    lam_out[...] = lam_ref[...]


NT = (((1,), (1,)), ((), ()))
NN = (((1,), (0,)), ((), ()))


def tall(x, high, low, dims):
    x_high, x_low = split(x)
    count = x.shape[0]
    both = lax.dot_general(jnp.concatenate([x_high, x_low], axis=0), high, dims, preferred_element_type=F32)
    return both[:count] + both[count:] + lax.dot_general(x_high, low, dims, preferred_element_type=F32)


def lanes_of(count):
    return -(-count // LANES) * LANES


def plane_kernel(
    count, primal, width, face_hbm, prim_hbm, slot_hbm, k_hbm, f_hbm, cinv_hbm, u_ref, lam_ref,
    face_s, prim_s, face_v, prim_v, slot_v, f_ref, k_ref, kh_ref, kl_ref, kph_ref, kpl_ref, e_ref, fh_ref, fl_ref, ks_ref,
    own_c, own_b, c_in, b_in, cinv_ref, cqh_ref, cql_ref, ac_ref, ap_ref, ar_ref, edge_ref,
    ach_ref, acl_ref, aph_ref, apl_ref, arh_ref, arl_ref, r_ref, face_out, face_in, x_out, x_in, q_out, q_in, lam_out, lam_in,
    in_sem, k_sem, c_sem, b_sem, cinv_send, cinv_recv, ac_send, ac_recv, ap_send, ap_recv, ar_send, ar_recv,
    halo_send, halo_recv, edge_sem, r_sem, face_sem, x_sem, q_sem, lam_sem,
):
    outer, inner = grid_of(count)
    plane = 2 * inner
    order, columns = f_ref.shape
    owned = primal // 2
    total = cinv_ref.shape[-1]
    tiles = k_sem.shape[0]
    tile = order // tiles
    share = columns // plane
    both = 2 * width
    wide = lanes_of(primal)
    span = r_ref.shape[-1]
    me = lax.axis_index("sub")
    mine = lax.rem(me, plane)
    z = me // plane
    core = lax.rem(me, 2)

    def at(z_, mine_):
        return z_ * plane + mine_

    partner = at(z, mine + 1 - 2 * core)
    across = [lax.rem(mine + 2 * m, plane) for m in range(1, inner)]
    across_peers = [at(z, other) for other in across]
    others = [lax.rem(mine + m, plane) for m in range(1, plane)]
    mates = [at(z, other) for other in others]
    turned = lax.rem(z, 2) if outer % 2 == 0 else 0

    def swapped(index, turn):
        return index + turn * (1 - 2 * lax.rem(index, 2))

    portion = swapped(mine, turned)

    def kin(place):
        return at(place, swapped(portion, lax.rem(place, 2) if outer % 2 == 0 else 0))

    beyond = [kin(lax.rem(z + m, outer)) for m in range(1, outer)]
    next_kin, last_kin = beyond[0], beyond[-1]
    after, before = [at(lax.rem(z + m, outer), mine) for m in (1, outer - 1)]
    far_first = beyond[::-1]
    if outer == 4:
        end = lax.rem(z + 1, outer) < 2
        mirror, skip, twin = outer - 1 - z, lax.rem(z + 2, outer), z + 1 - 2 * lax.rem(z, 2)
        far_first = [kin(place) for place in (jnp.where(end, mirror, skip), jnp.where(end, skip, mirror), twin)]

    def remote(src, dst, ssem, rsem, peer):
        return pltpu.make_async_remote_copy(
            src_ref=src, dst_ref=dst, send_sem=ssem, recv_sem=rsem, device_id={"sub": peer}, device_id_type=MESH
        )

    def send(src, dst, ssem, rsem, peer):
        remote(src, dst, ssem, rsem, peer).start()

    def arrived(ref, rsem):
        remote(ref, ref, r_sem.at[0, 0], rsem, partner).wait_recv()

    def sent(ref, ssem):
        remote(ref, ref, ssem, r_sem.at[0, 1], partner).wait_send()

    ints = [
        pltpu.make_async_copy(src, dst, in_sem.at[i])
        for i, (src, dst) in enumerate((
            (face_hbm, face_s), (prim_hbm, prim_s), (face_hbm, face_v), (prim_hbm, prim_v), (slot_hbm, slot_v)
        ))
    ]
    cinv_copy = pltpu.make_async_copy(cinv_hbm, cinv_ref.at[mine + 1], in_sem.at[5])
    f_copy = pltpu.make_async_copy(f_hbm, f_ref, in_sem.at[6])

    def k_copy(c):
        rows = pl.ds(c * tile, tile)
        return pltpu.make_async_copy(k_hbm.at[rows, :], k_ref.at[rows, :], k_sem.at[c])

    for copy in ints + [cinv_copy, f_copy]:
        copy.start()
    for c in range(tiles):
        k_copy(c).start()

    barrier = pltpu.get_barrier_semaphore()
    greeted = mates + beyond + ([after, before] if outer % 2 == 0 else [])
    for peer in greeted:
        pl.semaphore_signal(barrier, inc=1, device_id={"sub": peer}, device_id_type=MESH)

    with jax.named_scope("P_ints"):
        for copy in ints:
            copy.wait()
    square = (primal, primal)
    eye = lax.broadcasted_iota(jnp.int32, square, 0) == lax.broadcasted_iota(jnp.int32, square, 1)
    prim_col = jnp.sum(jnp.where(eye, prim_v[...].astype(F32), 0.0), axis=1, keepdims=True)
    slot_col = jnp.sum(jnp.where(eye, slot_v[...].astype(F32), 0.0), axis=1, keepdims=True)
    lane = lax.broadcasted_iota(jnp.int32, (primal, wide), 1).astype(F32)
    ordered = jnp.sum(jnp.where(slot_col == lane, prim_col + 1.0, 0.0), axis=0, keepdims=True) - 1.0
    ordering = jnp.where(lax.broadcasted_iota(jnp.int32, (wide, primal), 0) == slot_v[...], 1.0, 0.0).astype(BF16)

    def in_order(value):
        high, low = split(value)
        size = value.shape[1]
        pair = jnp.dot(ordering, jnp.concatenate([high, low], axis=1), preferred_element_type=F32)
        return pair[:, :size] + pair[:, size:]

    def one_hot_columns():
        right_ids, left_ids = face_v[0, 1:2, :], face_v[0, 0:1, :]
        ordered_ids = ordered.astype(jnp.int32)

        @pl.loop(0, tiles)
        def _(c):
            rows = pl.ds(pl.multiple_of(c * tile, tile), tile)
            near = lax.broadcasted_iota(jnp.int32, (tile, width), 0) + c * tile
            e_ref[rows, :width] = jnp.where(near == right_ids, 1.0, 0.0).astype(BF16)
            e_ref[rows, width:both] = jnp.where(near == left_ids, 1.0, 0.0).astype(BF16)
            near = lax.broadcasted_iota(jnp.int32, (tile, wide), 0) + c * tile
            e_ref[rows, both:] = jnp.where(near == ordered_ids, 1.0, 0.0).astype(BF16)

    def spread(buf, ssem, rsem, own):
        for peer in across_peers + [partner]:
            send(buf.at[own], buf.at[own], ssem, rsem.at[own], peer)

    def relay(buf, ssem, rsem):
        for other in across:
            arrived(buf.at[other], rsem.at[other])
            send(buf.at[other], buf.at[other], ssem, rsem.at[other], partner)

    def settle(buf, rsem):
        for other in [mine] + across:
            block = other + 1 - 2 * core
            arrived(buf.at[block], rsem.at[block])

    with jax.named_scope("P_onehot"):
        one_hot_columns()
    with jax.named_scope("P_barrier"):
        pl.semaphore_wait(barrier, len(greeted))
        cinv_copy.wait()
    halves = owned // 2

    def piece(block, half):
        return cinv_ref.at[block, pl.ds(half * halves, halves)]

    def send_far(half):
        send(piece(1 + core, half), piece(plane + 1 + core, half), halo_send.at[0], halo_recv.at[0, half], before)

    def send_near(half):
        send(piece(plane, half), piece(0, half), halo_send.at[1], halo_recv.at[1, half], after)

    def spread_coarse(half):
        for peer in across_peers + [partner]:
            rows = piece(mine + 1, half)
            send(rows, rows, cinv_send, cinv_recv.at[mine + 1, half], peer)

    def relay_coarse(half):
        for other in across:
            rows = piece(other + 1, half)
            arrived(rows, cinv_recv.at[other + 1, half])
            send(rows, rows, cinv_send, cinv_recv.at[other + 1, half], partner)
        pl.when(mine >= 2)(functools.partial(send_far, half))
        pl.when(mine == 1)(functools.partial(send_near, half))

    def settle_coarse():
        for half in range(2):
            for other in [mine] + across:
                block = other + 2 - 2 * core
                arrived(piece(block, half), cinv_recv.at[block, half])

    def last_edge():
        send(ac_ref.at[plane - 1, :, pl.ds(0, width)], edge_ref.at[0], edge_sem.at[0], edge_sem.at[1], after)

    def first_edge():
        send(ac_ref.at[0, :, pl.ds(width, width)], edge_ref.at[1], edge_sem.at[0], edge_sem.at[1], before)

    spread_coarse(0)
    for half in range(2):
        pl.when(mine < 2)(functools.partial(send_far, half))
        pl.when(mine == plane - 1)(functools.partial(send_near, half))
    with jax.named_scope("P_f"):
        f_copy.wait()
        high, low = split(f_ref[...])
        fh_ref[...] = high
        fl_ref[...] = low

    def halve(first_tile, last_tile):
        @pl.loop(first_tile, last_tile)
        def _(c):
            rows = pl.ds(pl.multiple_of(c * tile, tile), tile)
            high, low = split(k_ref[rows, :])
            kh_ref[rows, :] = high
            kl_ref[rows, :] = low

    with jax.named_scope("P_kwait"):
        for c in range(tiles):
            k_copy(c).wait()

    def picked(start, size, row_at):
        @pl.loop(0, size // 8)
        def _(i):
            base = pl.multiple_of(i * 8, 8)
            for j in range(8):
                ks_ref[pl.ds(start + base + j, 1), :] = k_ref[pl.ds(row_at(base + j), 1), :]

    def first(rows):
        high, low = split(ks_ref[rows, :])
        return product_parts(high, low, fh_ref[...], fl_ref[...])

    def columns_of(rows, picks):
        high, low = split(ks_ref[rows, :])
        return jnp.dot(high, picks, preferred_element_type=F32) + jnp.dot(low, picks, preferred_element_type=F32)

    def give(out, into, sems):
        for other, peer in zip(others, mates):
            send(out.at[swapped(other, turned)], into.at[mine], sems.at[0], sems.at[1], peer)
        into[mine] = out[portion]

    def give_back(out, into, sems):
        for other, peer in zip(others, mates):
            send(out.at[other], into.at[portion], sems.at[0], sems.at[1], peer)
        into[portion] = out[mine]

    def taken(into, sems):
        arrived(into.at[pl.ds(0, plane - 1)], sems.at[1])

    def assembled(parts):
        sums = None
        for i, part in enumerate(parts):
            part = jnp.concatenate([part, jnp.zeros((share, span - wide), F32)], axis=1)
            part = pltpu.roll(part, owned * i, 1) if i else part
            sums = part if sums is None else sums + part
        return sums

    def publish(step, parts):
        r_ref[step, z] = assembled(parts)
        for peer in far_first:
            rows = r_ref.at[step, z]
            send(rows, rows, r_sem.at[step, 0], r_sem.at[step, 1], peer)

    def faces(step, last_right, first_left):
        face_out[step, 0] = first_left
        send(face_out.at[step, 0], face_in.at[step, 0], face_sem.at[step, 0], face_sem.at[step, 1], last_kin)
        if step + 1 < ITERS:
            face_out[step, 1] = last_right
            send(face_out.at[step, 1], face_in.at[step, 1], face_sem.at[step, 0], face_sem.at[step, 1], next_kin)

    def face_part(ref, step):
        return ref.at[step] if step + 1 < ITERS else ref.at[step, pl.ds(0, 1)]

    rim = (mine == 0) | (mine == plane - 1)

    def urgent_half(block):
        return jnp.where(block == 0, 1, 0)

    def spread_half(half):
        for peer in across_peers + [partner]:
            rows = ar_ref.at[mine, half]
            send(rows, rows, ar_send, ar_recv.at[mine, half], peer)

    def relay_half(block, half):
        rows = ar_ref.at[block, half]
        arrived(rows, ar_recv.at[block, half])
        send(rows, rows, ar_send, ar_recv.at[block, half], partner)

    def spread_rows():
        half = urgent_half(mine)
        spread_half(half)
        spread_half(1 - half)

    def relay_urgent():
        relay_half(across[0], urgent_half(across[0]))

    def relay_whole():
        relay_half(across[0], 0)
        relay_half(across[0], 1)

    def relay_second():
        relay_half(across[0], 1 - urgent_half(across[0]))

    first_block = jnp.where(core == 0, plane - 1, 0)
    second_block = mine + across[0] + 2 - 4 * core - first_block

    def settle_half(block, half):
        arrived(ar_ref.at[block, half], ar_recv.at[block, half])

    with jax.named_scope("P_first"):
        picked(both, primal, lambda i: prim_s[0, i])
        own_c[...] = in_order(first(slice(both, both + primal))).T.reshape(own_c.shape)
        give(own_c, c_in, c_sem)
    spread_coarse(1)
    with jax.named_scope("P_pick"):
        picked(0, width, lambda i: face_s[0, 1, i])
        picked(width, width, lambda i: face_s[0, 0, i])
    with jax.named_scope("P_ac"):
        found = columns_of(slice(0, both), e_ref[:, both:])
        ac_ref[mine, :, :width] = found[:width].T[:primal]
        ac_ref[mine, :, width:] = found[width:].T[:primal]
        spread(ac_ref, ac_send, ac_recv, mine)
    with jax.named_scope("P_relayc0"):
        relay_coarse(0)
    with jax.named_scope("P_cwait"):
        taken(c_in, c_sem)
    publish(0, [c_in[i] for i in range(plane)])
    pl.when(mine == plane - 1)(last_edge)
    pl.when(mine == 0)(first_edge)
    with jax.named_scope("P_firstb"):
        loads = first(slice(0, both))
        own_b[:, :, :width] = loads[:width].T.reshape(plane, share, width)
        own_b[:, :, width:] = loads[width:].T.reshape(plane, share, width)
        give(own_b, b_in, b_sem)
    with jax.named_scope("P_relayc1"):
        relay_coarse(1)
    with jax.named_scope("P_ap"):
        ap_ref[mine] = in_order(columns_of(slice(both, both + primal), e_ref[:, :both]))[:primal]
        spread(ap_ref, ap_send, ap_recv, mine)
    with jax.named_scope("P_ar"):
        found = columns_of(slice(0, both), e_ref[:, :both])
        ar_ref[mine, 0] = found[:width]
        ar_ref[mine, 1] = found[width:]
        pl.when(rim)(spread_rows)
    with jax.named_scope("P_relayac"):
        relay(ac_ref, ac_send, ac_recv)
    pl.when(mine == 1)(last_edge)
    pl.when(mine == 2)(first_edge)
    with jax.named_scope("P_bwait"):
        taken(b_in, b_sem)
    faces(0, b_in[plane - 1, :, :width], b_in[0, :, width:])
    with jax.named_scope("P_halve"):
        halve(0, tiles)
    pl.when(jnp.logical_not(rim))(spread_rows)

    def primal_columns(first_tile, last_tile):
        picks = e_ref[:, both:]

        @pl.loop(first_tile, last_tile)
        def _(c):
            rows = pl.ds(pl.multiple_of(c * tile, tile), tile)
            kph_ref[rows, :] = jnp.dot(kh_ref[rows, :], picks, preferred_element_type=F32).astype(BF16)
            kpl_ref[rows, :] = jnp.dot(kl_ref[rows, :], picks, preferred_element_type=F32).astype(BF16)

    last_row = cqh_ref.shape[0]

    def coarse_rows(block, start):
        for ref, part in zip((cqh_ref, cql_ref), split(cinv_ref[block])):
            ref[start:start + owned, :] = part

    def halves_of(refs, src):
        for i in range(plane):
            for ref, part in zip(refs, split(src[i])):
                ref[i, :primal, :] = part
                ref[i, primal:, :] = jnp.zeros((wide - primal, both), BF16)

    early = tiles // 3
    sooner = jnp.where(mine == 1, early // 2, early)
    with jax.named_scope("P_halo"):
        settle_coarse()
        near = cinv_ref.at[0]
        for half in range(2):
            rows = piece(plane + 1 + core, half)
            arrived(rows, halo_recv.at[0, half])
            send(rows, rows, halo_send.at[0], halo_recv.at[3, half], partner)

        @pl.when(core == 1)
        def _():
            for half in range(2):
                arrived(piece(0, half), halo_recv.at[1, half])
            send(near, near, halo_send.at[1], halo_recv.at[2, 1], partner)

    with jax.named_scope("P_cq"):
        for ref in (cqh_ref, cql_ref):
            ref[plane * owned:, :] = jnp.zeros((last_row - plane * owned, total), BF16)
        for i in range(plane):
            coarse_rows(i + 1, i * owned)
    with jax.named_scope("P_settleac"):
        settle(ac_ref, ac_recv)
        halves_of((ach_ref, acl_ref), ac_ref)
    with jax.named_scope("P_edge0"):
        rows = edge_ref.at[1 - core]
        arrived(rows, edge_sem.at[1])
        send(rows, rows, edge_sem.at[3], edge_sem.at[2], partner)
    with jax.named_scope("P_relayap"):
        relay(ap_ref, ap_send, ap_recv)
    def coarse_halos():
        for half in range(2):
            arrived(piece(plane + 2 - core, half), halo_recv.at[3, half])

        @pl.when(core == 0)
        def _():
            arrived(near, halo_recv.at[2, 1])

        coarse_rows(plane + 1, plane * owned)
        coarse_rows(plane + 2, (plane + 1) * owned)
        coarse_rows(0, last_row - owned)

    def uncorrected(first_tile, last_tile):
        @pl.loop(first_tile, last_tile)
        def _(c):
            rows = pl.ds(pl.multiple_of(c * tile, tile), tile)
            u_ref[rows, :] = product_parts(kh_ref[rows, :], kl_ref[rows, :], fh_ref[...], fl_ref[...])

    def changed_loads():
        high, low = split(x_in[...].reshape(columns, both))
        moved = lax.dot_general(
            e_ref[:, :both], jnp.concatenate([high, low], axis=0), NT, preferred_element_type=F32
        )
        high, low = split(f_ref[...] + (moved[:, :columns] + moved[:, columns:]))
        fh_ref[...] = high
        fl_ref[...] = low

    def shifted(value, block):
        return (pltpu.roll(value, value.shape[1] - owned * block, 1) if block > 0 else pltpu.roll(
            value, owned, 1) if block else value)[:, :wide]

    def padded(value):
        return jnp.concatenate([value, jnp.zeros((wide - primal, value.shape[1]), F32)], axis=0)

    lam = [jnp.zeros((share, width), F32)] * (plane + 1)
    values = [b_in[i] for i in range(plane)]
    edges = None
    for step in range(ITERS):
        if step == ITERS - 1:
            with jax.named_scope("P_primcol1"):
                primal_columns(tiles - early, tiles)
            with jax.named_scope("P_xwait"):
                arrived(x_in.at[pl.ds(0, plane - 1)], x_sem.at[1])
                changed_loads()
            with jax.named_scope("P_uncorr0"):
                uncorrected(0, sooner)
        with jax.named_scope(f"P_rwait{step}"):
            arrived(r_ref.at[step, pl.ds(0, outer - 1)], r_sem.at[step, 1])
        with jax.named_scope(f"P_coarse{step}"):
            sums = None
            for i in range(outer):
                part = jnp.concatenate([r_ref[step, i], jnp.zeros((share, total - span), F32)], axis=1)
                part = pltpu.roll(part, plane * owned * i, 1) if i else part
                sums = part if sums is None else sums + part
            if step:
                coarse = tall(sums, cqh_ref[...], cql_ref[...], NT)
                moved = []
            else:
                own = tall(sums, cqh_ref[:lanes_of(plane * owned)], cql_ref[:lanes_of(plane * owned)], NT)
                moved = [values[i] - tall(shifted(own, i), ach_ref[i], acl_ref[i], NN) for i in range(plane - 1)]
                with jax.named_scope("P_halo2"):
                    coarse_halos()
                low_row = (plane - 1) * owned // LANES * LANES
                rest = tall(sums, cqh_ref[low_row:], cql_ref[low_row:], NT)
                coarse = jnp.concatenate([own[:, :low_row], rest], axis=1)
            steps = [shifted(coarse, i - 1) for i in range(plane + 2)]
            if step == ITERS - 1:
                for i in range(plane):
                    q_out[i] = steps[i + 1]
                give_back(q_out, q_in, q_sem)
        if edges is None:
            with jax.named_scope("P_edge"):
                arrived(edge_ref.at[core], edge_sem.at[2])
                edges = [split(padded(edge_ref[i])) for i in range(2)]
        with jax.named_scope(f"P_faces{step}"):
            arrived(face_part(face_in, step), face_sem.at[step, 1])
        with jax.named_scope(f"P_update{step}"):
            moved += [values[i] - tall(steps[i + 1], ach_ref[i], acl_ref[i], NN) for i in range(len(moved), plane)]
            right = [part[:, :width] for part in moved]
            left = [part[:, width:] for part in moved]
            left.append(face_in[step, 0] - tall(steps[plane + 1], *edges[1], NN))
            lam_next = [lam[i + 1] + DAMPING * (right[i] - left[i + 1]) for i in range(plane)]
            if step + 1 < ITERS:
                ahead = face_in[step, 1] - tall(steps[0], *edges[0], NN)
                lam_next = [lam[0] + DAMPING * (ahead - left[0])] + lam_next
            else:
                for i in range(plane):
                    lam_out[i] = lam_next[i]
                give_back(lam_out, lam_in, lam_sem)
                break
            lam = lam_next
            if step == 0:
                with jax.named_scope("P_settleap"):
                    settle(ap_ref, ap_recv)
                    halves_of((aph_ref, apl_ref), ap_ref)
            changes = [jnp.concatenate([-lam[i + 1], lam[i]], axis=1) for i in range(plane)]
            if step == ITERS - 2:
                for i in range(plane):
                    x_out[i] = changes[i]
                give_back(x_out, x_in, x_sem)
            publish(step + 1, [
                c_in[i] + tall(changes[i], aph_ref[i], apl_ref[i], NT) for i in range(plane)
            ])
        if step == 0:
            with jax.named_scope("P_relayr0"):
                pl.when(jnp.logical_not(rim))(relay_urgent)
                settle_half(first_block, urgent_half(first_block))
                for i, half in ((plane - 1, 0), (0, 1)):
                    rows = slice(half * width, (half + 1) * width)
                    for ref, part in zip((arh_ref, arl_ref), split(ar_ref[i, half])):
                        ref[i, rows] = part
            with jax.named_scope("P_facevalues"):
                last_right = tall(changes[-1], arh_ref[plane - 1, :width], arl_ref[plane - 1, :width], NT)
                first_left = tall(changes[0], arh_ref[0, width:], arl_ref[0, width:], NT)
                faces(1, b_in[plane - 1, :, :width] + last_right, b_in[0, :, width:] + first_left)
            with jax.named_scope("P_primcol0"):
                primal_columns(0, early)
            with jax.named_scope("P_relayr1"):
                pl.when(rim)(relay_whole)
                pl.when(jnp.logical_not(rim))(relay_second)
            with jax.named_scope("P_primcol0"):
                primal_columns(early, tiles - early)
            with jax.named_scope("P_settler1"):
                settle_half(first_block, 1 - urgent_half(first_block))
                settle_half(second_block, 0)
                settle_half(second_block, 1)
                for i in range(plane):
                    for half in range(2):
                        if (i, half) not in ((plane - 1, 0), (0, 1)):
                            rows = slice(half * width, (half + 1) * width)
                            for ref, part in zip((arh_ref, arl_ref), split(ar_ref[i, half])):
                                ref[i, rows] = part
        with jax.named_scope(f"P_values{step}"):
            values = [b_in[i] + tall(changes[i], arh_ref[i], arl_ref[i], NT) for i in range(plane)]
            if step:
                faces(step + 1, values[plane - 1][:, :width], values[0][:, width:])

    with jax.named_scope("P_uncorr1"):
        uncorrected(sooner, tiles)
    with jax.named_scope("P_qwait"):
        arrived(q_in.at[pl.ds(0, plane - 1)], q_sem.at[1])
    with jax.named_scope("P_last"):
        high, low = split(q_in[...].reshape(columns, wide).T)
        pair = jnp.concatenate([high, low], axis=1)
        for c in range(tiles):
            rows = pl.ds(c * tile, tile)
            step = jnp.dot(kph_ref[rows, :], pair, preferred_element_type=F32)
            step = step[:, :columns] + step[:, columns:]
            u_ref[rows, :] = u_ref[rows, :] - (step + jnp.dot(kpl_ref[rows, :], high, preferred_element_type=F32))

    with jax.named_scope("P_lamwait"):
        arrived(lam_in.at[pl.ds(0, plane - 1)], lam_sem.at[1])
        lam_ref[...] = lam_in[...].reshape(columns, width).T
    with jax.named_scope("P_sent"):
        others_part = pl.ds(0, plane - 1)
        sent(own_c.at[others_part], c_sem.at[0])
        sent(own_b.at[others_part], b_sem.at[0])
        sent(cinv_ref.at[others_part], cinv_send)
        for ref, sem in ((ac_ref, ac_send), (ap_ref, ap_send), (ar_ref, ar_send)):
            sent(ref.at[others_part], sem)
        sent(cinv_ref.at[pl.ds(0, 2)], halo_send.at[0])

        @pl.when(core == 1)
        def _():
            sent(cinv_ref.at[pl.ds(0, 2)], halo_send.at[1])

        sent(edge_ref.at[0], edge_sem.at[0])
        sent(edge_ref.at[0], edge_sem.at[3])
        for step in range(ITERS):
            sent(r_ref.at[step, pl.ds(0, outer - 1)], r_sem.at[step, 0])
            sent(face_part(face_out, step), face_sem.at[step, 0])
        sent(x_out.at[others_part], x_sem.at[0])
        sent(q_out.at[others_part], q_sem.at[0])
        sent(lam_out.at[others_part], lam_sem.at[0])


def plane_finish(u_ref, lam_ref, u_hbm, lam_hbm, sem):
    copies = [pltpu.make_async_copy(u_ref, u_hbm, sem.at[0]), pltpu.make_async_copy(lam_ref, lam_hbm, sem.at[1])]
    for copy in copies:
        copy.start()
    for copy in copies:
        copy.wait()


def size_of(buffers):
    return sum((4 if kind == F32 else 2) * functools.reduce(lambda a, b: a * b, size) for size, kind in buffers)


def plane_scratch(count, order, columns, owned, total, width, primal):
    outer, inner = grid_of(count)
    plane = 2 * inner
    both = 2 * width
    wide = lanes_of(primal)
    span = lanes_of((plane + 1) * owned)
    share = columns // plane
    pairs = lanes_of((plane + 3) * owned)
    return plane, [
        ((order, columns), F32),
        ((order, order), F32),
        ((order, order), BF16),
        ((order, order), BF16),
        ((order, wide), BF16),
        ((order, wide), BF16),
        ((order, both + wide), BF16),
        ((order, columns), BF16),
        ((order, columns), BF16),
        ((both + primal, order), F32),
        ((plane, share, wide), F32),
        ((plane, share, both), F32),
        ((plane, share, wide), F32),
        ((plane, share, both), F32),
        ((plane + 3, owned, total), F32),
        ((pairs, total), BF16),
        ((pairs, total), BF16),
        ((plane, primal, both), F32),
        ((plane, primal, both), F32),
        ((plane, 2, width, both), F32),
        ((2, primal, width), F32),
        ((plane, wide, both), BF16),
        ((plane, wide, both), BF16),
        ((plane, wide, both), BF16),
        ((plane, wide, both), BF16),
        ((plane, both, both), BF16),
        ((plane, both, both), BF16),
        ((ITERS, outer, share, span), F32),
        ((ITERS, 2, share, width), F32),
        ((ITERS, 2, share, width), F32),
        ((plane, share, both), F32),
        ((plane, share, both), F32),
        ((plane, share, wide), F32),
        ((plane, share, wide), F32),
        ((plane, share, width), F32),
        ((plane, share, width), F32),
    ]


def planar(condensed, eigen_loads, coarse_inverse, face_rows, primal_rows, primal_slot):
    count = lax.axis_size("sub")
    order, columns = eigen_loads.shape
    owned, total = coarse_inverse.shape
    width = face_rows.shape[2]
    primal = primal_rows.shape[1]
    outer, inner = grid_of(count)
    tile = 256 if order % 256 == 0 else order
    tiles = order // tile
    plane, buffers = plane_scratch(count, order, columns, owned, total, width, primal)
    needed = size_of(buffers)
    wide = lanes_of(primal)
    dma = pltpu.SemaphoreType.DMA
    vmem = pl.BlockSpec(memory_space=pltpu.VMEM)
    shape = jax.ShapeDtypeStruct
    held = [
        pltpu.with_memory_space_constraint(value, pltpu.HBM)
        for value in (face_rows, primal_rows, primal_slot, condensed, eigen_loads, coarse_inverse)
    ]
    parts = pl.pallas_call(
        functools.partial(plane_kernel, count, primal, width),
        out_shape=(
            shape((order, columns), F32),
            shape((width, columns), F32),
        ),
        in_specs=[pl.BlockSpec(memory_space=pltpu.HBM)] * 6,
        out_specs=(vmem,) * 2,
        scratch_shapes=[
            pltpu.SMEM(face_rows.shape, jnp.int32),
            pltpu.SMEM(primal_rows.shape, jnp.int32),
            pltpu.VMEM(face_rows.shape, jnp.int32),
            pltpu.VMEM(primal_rows.shape, jnp.int32),
            pltpu.VMEM(primal_slot.shape, jnp.int32),
        ] + [pltpu.VMEM(size, kind) for size, kind in buffers] + [
            dma((7,)),
            dma((tiles,)),
            dma((2,)),
            dma((2,)),
            dma(()),
            dma((plane + 1, 2)),
            dma(()),
            dma((plane,)),
            dma(()),
            dma((plane,)),
            dma(()),
            dma((plane, 2)),
            dma((2,)),
            dma((4, 2)),
            dma((4,)),
            dma((ITERS, 2)),
            dma((ITERS, 2)),
            dma((2,)),
            dma((2,)),
            dma((2,)),
        ],
        compiler_params=pltpu.CompilerParams(
            collective_id=0, has_side_effects=True, vmem_limit_bytes=min(PLANE_LIMIT, needed + needed // 3)
        ),
    )(*held)
    return pl.pallas_call(
        plane_finish,
        out_shape=(shape((order, columns), F32), shape((width, columns), F32)),
        in_specs=[vmem] * 2,
        out_specs=(pl.BlockSpec(memory_space=pltpu.HBM),) * 2,
        scratch_shapes=[dma((2,))],
        compiler_params=pltpu.CompilerParams(vmem_limit_bytes=4 * order * columns * 4),
    )(*parts)


def fits_plane(condensed, eigen_loads, coarse_inverse, face_rows, primal_rows, primal_slot):
    count = lax.axis_size("sub")
    order, columns = eigen_loads.shape
    owned, total = coarse_inverse.shape
    width = face_rows.shape[2]
    primal = primal_rows.shape[1]
    outer, inner = grid_of(count)
    plane = 2 * inner
    if outer < 2 or inner != 2 or columns % (8 * plane) or total % LANES or width % LANES or owned % 16 or primal != 2 * owned:
        return False
    _, buffers = plane_scratch(count, order, columns, owned, total, width, primal)
    return size_of(buffers) <= PLANE_LIMIT * 3 // 4


def local(*values):
    return (planar if fits_plane(*values) else general)(*values)


def general(condensed, eigen_loads, coarse_inverse, face_rows, primal_rows, primal_slot):
    count = lax.axis_size("sub")
    order, columns = eigen_loads.shape
    owned, total = coarse_inverse.shape
    width = face_rows.shape[2]
    primal = primal_rows.shape[1]
    padded = 2 * width + -(-primal // LANES) * LANES
    outer, inner = grid_of(count)
    corner_width = padded - 2 * width
    tile = 256 if order % 256 == 0 else order
    sends = (outer - 1) + (inner - 1) * outer + outer * inner
    dma = pltpu.SemaphoreType.DMA
    vmem = pl.BlockSpec(memory_space=pltpu.VMEM)
    face = pltpu.VMEM((ITERS, width, columns), F32)
    corner = pltpu.VMEM((width, padded - 2 * width), F32)
    smem = pl.BlockSpec(memory_space=pltpu.SMEM)
    needed = 8 * order * (order + padded + 2 * columns) + 4 * padded * (order + columns + padded)
    needed += 4 * owned * total * 8 + 4 * columns * (ITERS * (count * primal + 4 * width) + total)
    needed += 4 * order * (columns + 2 * corner_width) + 4 * columns * (order + 8 * width)
    shape = jax.ShapeDtypeStruct
    held = [
        pltpu.with_memory_space_constraint(value, pltpu.HBM)
        for value in (face_rows, primal_rows, primal_slot, condensed, eigen_loads, coarse_inverse)
    ]
    parts = pl.pallas_call(
        functools.partial(kernel, count, primal, width),
        out_shape=(
            shape((order, columns), F32),
            shape((order, corner_width), BF16),
            shape((order, corner_width), BF16),
            shape((corner_width, columns), F32),
            shape((width, columns), F32),
        ),
        in_specs=[smem, smem] + [pl.BlockSpec(memory_space=pltpu.HBM)] * 6,
        out_specs=(vmem,) * 5,
        scratch_shapes=[
            pltpu.VMEM(face_rows.shape, jnp.int32),
            pltpu.VMEM(primal_rows.shape, jnp.int32),
            pltpu.VMEM(primal_slot.shape, jnp.int32),
            pltpu.VMEM((order, columns), F32),
            pltpu.VMEM((owned, total), F32),
            dma((5,)),
            pltpu.VMEM((order, order), F32),
            pltpu.VMEM((order, order), BF16),
            pltpu.VMEM((order, order), BF16),
            pltpu.VMEM((order, padded), BF16),
            pltpu.VMEM((order, columns), BF16),
            pltpu.VMEM((order, columns), BF16),
            pltpu.VMEM((padded, order), F32),
            pltpu.VMEM((padded, columns), F32),
            pltpu.VMEM((padded, padded), BF16),
            pltpu.VMEM((padded, padded), BF16),
            pltpu.VMEM((3, owned, total), F32),
            pltpu.VMEM((4 * owned, total), BF16),
            pltpu.VMEM((4 * owned, total), BF16),
            pltpu.VMEM((ITERS, count, primal, columns), F32),
            pltpu.VMEM((total, columns), F32),
            face, face, face, face,
            corner, corner, corner, corner,
            dma((order // tile,)),
            dma((ITERS, 2 * sends)),
            dma((ITERS, count, 2)),
            dma((2, ITERS, 2)),
            dma((3,)),
            dma((3,)),
            dma((2,)),
            dma((2,)),
        ],
        compiler_params=pltpu.CompilerParams(
            collective_id=0, has_side_effects=True, vmem_limit_bytes=min(VMEM_LIMIT, needed + needed // 4)
        ),
    )(face_rows, primal_rows, *held)
    return pl.pallas_call(
        finish,
        out_shape=(shape((order, columns), F32), shape((width, columns), F32)),
        in_specs=[vmem] * 5,
        out_specs=(vmem, vmem),
        compiler_params=pltpu.CompilerParams(vmem_limit_bytes=4 * order * columns * 8),
    )(*parts)


def solution(mesh):
    placed = (
        P(("rve", "sub"), None),
        P(("rve", "sub"), None),
        P(("rve", "sub"), None),
        P("sub", None, None),
        P("sub", None),
        P("sub", None),
    )
    return jax.shard_map(
        local,
        mesh=mesh,
        in_specs=placed,
        out_specs=(P(("rve", "sub"), None), P(("rve", "sub"), None)),
        check_vma=False,
    )
```

```python
import functools

import jax
import jax.numpy as jnp
from jax import lax
from jax.experimental import pallas as pl
from jax.experimental.pallas import tpu as pltpu
from jax.sharding import PartitionSpec as P

ITERS = 3
DAMPING = 0.5
VMEM_LIMIT = 67043328
MESH = pl.DeviceIdType.MESH
F32 = jnp.float32
BF16 = jnp.bfloat16
LANES = 128
PLANE_LIMIT = 60 * 1024 * 1024


def grid_of(count):
    chips = count // 2
    inner = 1
    while (2 * inner) ** 2 <= chips and chips % (2 * inner) == 0:
        inner *= 2
    return chips // inner, inner


def flipped(index, mask, count):
    if count & (count - 1):
        return lax.rem(index + count - mask, count)
    out = 0
    bit = 1
    while bit < count:
        own = lax.rem(index // bit, 2)
        out = out + bit * ((1 - own) if mask & bit else own)
        bit *= 2
    return out


def returned(index, mask, count):
    if count & (count - 1):
        return lax.rem(index + mask, count)
    return flipped(index, mask, count)


def split(value):
    high = value.astype(BF16)
    return high, (value - high.astype(F32)).astype(BF16)


def product(high, low, value):
    value_high, value_low = split(value)
    return product_parts(high, low, value_high, value_low)


def product_parts(high, low, value_high, value_low):
    width = value_high.shape[1]
    both = jnp.dot(high, jnp.concatenate([value_high, value_low], axis=1), preferred_element_type=F32)
    return both[:, :width] + both[:, width:] + jnp.dot(low, value_high, preferred_element_type=F32)


def kernel(
    count, primal, width, face_s, prim_s, face_hbm, prim_hbm, slot_hbm, k_hbm, f_hbm, cinv_hbm, pre_ref, kph_ref, kpl_ref, q_ref, lam_ref,
    face_v, prim_v, slot_v, f_ref, cinv_ref, in_sem, k_ref, kh_ref, kl_ref, e_ref, fh_ref, fl_ref, ks_ref, first_ref, ah_ref, al_ref, cols_ref, ch_ref, cl_ref,
    gat_ref, r_ref, send_r, send_l, got_r, got_l, send_ar, send_al, got_ar, got_al,
    k_sem, send_sem, block_sem, face_sem, cinv_send, cinv_recv, a_send, a_recv,
):
    outer, inner = grid_of(count)
    order, columns = f_ref.shape
    owned = primal // 2
    tile = order // k_sem.shape[0]
    padded = e_ref.shape[1]
    me = lax.axis_index("sub")
    core = lax.rem(me, 2)
    y = lax.rem(me // 2, inner)
    z = me // (2 * inner)

    def at(z_, y_, core_):
        return (z_ * inner + y_) * 2 + core_

    def around(steps):
        return lax.rem(me + (steps + count), count)

    def k_copy(c):
        rows = pl.ds(c * tile, tile)
        return pltpu.make_async_copy(k_hbm.at[rows, :], k_ref.at[rows, :], k_sem.at[c])

    held = [
        pltpu.make_async_copy(src, dst, in_sem.at[i])
        for i, (src, dst) in enumerate((
            (f_hbm, f_ref), (cinv_hbm, cinv_ref), (face_hbm, face_v), (prim_hbm, prim_v), (slot_hbm, slot_v)
        ))
    ]
    for copy in held:
        copy.start()
    for c in range(k_sem.shape[0]):
        k_copy(c).start()

    outer_peers = [at(flipped(z, m, outer), y, core) for m in range(1, outer)]
    outer_back = [returned(z, m, outer) for m in range(1, outer)]
    inner_peers = [at(z, flipped(y, m, inner), core) for m in range(1, inner)]
    partner = at(z, y, 1 - core)
    ring = [around(d) for d in (-1, 1)]

    barrier = pltpu.get_barrier_semaphore()
    greeted = outer_peers + inner_peers + [partner] + ring
    if outer & (outer - 1):
        greeted = greeted + [at(b, y, core) for b in outer_back]
    for peer in greeted:
        pl.semaphore_signal(barrier, inc=1, device_id={"sub": peer}, device_id_type=MESH)

    def remote(src, dst, ssem, rsem, peer):
        return pltpu.make_async_remote_copy(
            src_ref=src, dst_ref=dst, send_sem=ssem, recv_sem=rsem, device_id={"sub": peer}, device_id_type=MESH
        )

    cinv_copies = [
        remote(cinv_ref, cols_ref.at[slot], cinv_send.at[slot], cinv_recv.at[slot], around(d))
        for slot, d in ((0, 1), (1, -1))
    ]
    passed_on = remote(cols_ref.at[1], cols_ref.at[2], cinv_send.at[2], cinv_recv.at[2], around(-1))

    for copy in held:
        copy.wait()

    square = (primal, primal)
    eye = lax.broadcasted_iota(jnp.int32, square, 0) == lax.broadcasted_iota(jnp.int32, square, 1)
    prim_col = jnp.sum(jnp.where(eye, prim_v[...].astype(F32), 0.0), axis=1, keepdims=True)
    slot_col = jnp.sum(jnp.where(eye, slot_v[...].astype(F32), 0.0), axis=1, keepdims=True)
    corner_width = padded - 2 * width
    lane = lax.broadcasted_iota(jnp.int32, (primal, corner_width), 1).astype(F32)
    ordered = jnp.sum(jnp.where(slot_col == lane, prim_col + 1.0, 0.0), axis=0, keepdims=True) - 1.0
    ordering = jnp.where(lax.broadcasted_iota(jnp.int32, square, 0) == slot_v[...], 1.0, 0.0).astype(BF16)

    fh, fl = split(f_ref[...])
    fh_ref[...] = fh
    fl_ref[...] = fl

    def stream(first_tile, last_tile):
        @pl.loop(first_tile, last_tile)
        def _(c):
            k_copy(c).wait()
            rows = pl.ds(pl.multiple_of(c * tile, tile), tile)
            high, low = split(k_ref[rows, :])
            kh_ref[rows, :] = high
            kl_ref[rows, :] = low
            pre_ref[rows, :] = product_parts(high, low, fh_ref[...], fl_ref[...])

    half = 1
    stream(0, half)
    pl.semaphore_wait(barrier, len(greeted))
    for copy in cinv_copies:
        copy.start()
    stream(half, order // tile)

    used = 2 * width + primal

    def picked(to_ref, from_ref):
        def rows_of(start, size, row_at):
            @pl.loop(0, size // 8)
            def _(i):
                base = pl.multiple_of(i * 8, 8)
                for j in range(8):
                    to_ref[pl.ds(start + base + j, 1), :] = from_ref[pl.ds(row_at(base + j), 1), :]

        rows_of(0, width, lambda i: face_s[0, 1, i])
        rows_of(width, width, lambda i: face_s[0, 0, i])
        rows_of(2 * width, primal, lambda i: prim_s[0, i])

    def in_order(value):
        high, low = split(value)
        half_width = value.shape[1]
        both = jnp.dot(ordering, jnp.concatenate([high, low], axis=1), preferred_element_type=F32)
        return both[:, :half_width] + both[:, half_width:]

    picked(first_ref, pre_ref)
    empty = jnp.zeros((padded - used, columns), F32)
    first = jnp.concatenate([first_ref[:2 * width], in_order(first_ref[2 * width:used]), empty], axis=0)

    def one_hot_columns():
        right_ids, left_ids = face_v[0, 1:2, :], face_v[0, 0:1, :]
        ordered_ids = ordered.astype(jnp.int32)

        @pl.loop(0, order // tile)
        def _(c):
            rows = pl.ds(pl.multiple_of(c * tile, tile), tile)
            near = lax.broadcasted_iota(jnp.int32, (tile, width), 0) + c * tile
            e_ref[rows, :width] = jnp.where(near == right_ids, 1.0, 0.0).astype(BF16)
            e_ref[rows, width:2 * width] = jnp.where(near == left_ids, 1.0, 0.0).astype(BF16)
            near = lax.broadcasted_iota(jnp.int32, (tile, corner_width), 0) + c * tile
            e_ref[rows, 2 * width:] = jnp.where(near == ordered_ids, 1.0, 0.0).astype(BF16)

    def finish_a():
        one_hot_columns()
        if padded > used:
            ks_ref[used:, :] = jnp.zeros((padded - used, order), F32)
        picked(ks_ref, k_ref)
        high, low = split(ks_ref[...])
        parts = []
        for part, out in ((high, ah_ref), (low, al_ref)):
            found = jnp.dot(part, e_ref[...], preferred_element_type=F32)
            out[:2 * width, :] = found[:2 * width].astype(BF16)
            out[2 * width:used, :] = jnp.dot(
                ordering, found[2 * width:used].astype(BF16), preferred_element_type=F32
            ).astype(BF16)
            if padded > used:
                out[used:, :] = jnp.zeros((padded - used, padded), BF16)
            parts.append(found[:2 * width, 2 * width:])
        corner = parts[0] + parts[1]
        send_ar[...] = corner[:width]
        send_al[...] = corner[width:]

    def primal_columns():
        picks = e_ref[:, 2 * width:]

        @pl.loop(0, order // tile)
        def _(c):
            rows = pl.ds(pl.multiple_of(c * tile, tile), tile)
            kph_ref[rows, :] = jnp.dot(kh_ref[rows, :], picks, preferred_element_type=F32).astype(BF16)
            kpl_ref[rows, :] = jnp.dot(kl_ref[rows, :], picks, preferred_element_type=F32).astype(BF16)

    def uncorrected(changes):
        high, low = split(changes)
        spread = jnp.dot(e_ref[:, :2 * width], jnp.concatenate([high, low], axis=1), preferred_element_type=F32)
        loads = f_ref[...] + (spread[:, :columns] + spread[:, columns:])
        high, low = split(loads)
        fh_ref[...] = high
        fl_ref[...] = low

        @pl.loop(0, order // tile)
        def _(c):
            rows = pl.ds(pl.multiple_of(c * tile, tile), tile)
            pre_ref[rows, :] = product_parts(kh_ref[rows, :], kl_ref[rows, :], fh_ref[...], fl_ref[...])

    a_copies = [
        remote(send_al, got_al, a_send.at[0], a_recv.at[0], around(-1)),
        remote(send_ar, got_ar, a_send.at[1], a_recv.at[1], around(1)),
    ]

    lam = jnp.zeros((width, columns), F32)
    lam_before = jnp.zeros((width, columns), F32)
    values = first
    changes = None
    for step in range(ITERS):
        if step:
            changes = jnp.concatenate([-lam, lam_before], axis=0)
            values = first + product(ah_ref[:, :2 * width], al_ref[:, :2 * width], changes)
        gat = gat_ref.at[step]
        gat_ref[step, me] = values[2 * width:2 * width + primal]
        send_r[step] = values[:width]
        send_l[step] = values[width:2 * width]
        started = []

        def forward(block, peer, part):
            rows = gat.at[block, pl.ds(part * owned, owned)]
            copy = remote(rows, rows, send_sem.at[step, len(started)], block_sem.at[step, block, part], peer)
            copy.start()
            started.append(copy)

        def arrived(block, part):
            rows = gat.at[block, pl.ds(part * owned, owned)]
            remote(rows, rows, send_sem.at[step, 0], block_sem.at[step, block, part], partner).wait_recv()

        for part in range(2):
            for peer in reversed(outer_peers):
                forward(me, peer, part)
            for peer in inner_peers:
                forward(me, peer, part)
            forward(me, partner, part)
        faces = [
            remote(send_l.at[step], got_l.at[step], face_sem.at[0, step, 0], face_sem.at[1, step, 0], around(-1)),
            remote(send_r.at[step], got_r.at[step], face_sem.at[0, step, 1], face_sem.at[1, step, 1], around(1)),
        ]
        for copy in faces:
            copy.start()

        if step == 0:
            cinv_copies[1].wait_recv()
            passed_on.start()
            finish_a()
            for copy in a_copies:
                copy.start()
        if step == 1:
            primal_columns()
        if step == ITERS - 1:
            uncorrected(changes)

        for part in range(2):
            for source in outer_back:
                block = at(source, y, core)
                arrived(block, part)
                for peer in inner_peers:
                    forward(block, peer, part)
                forward(block, partner, part)
        if step == 0:
            cinv_copies[0].wait()
            cinv_copies[1].wait_send()
            passed_on.wait()
            for slot, part in enumerate((cols_ref.at[0], cinv_ref, cols_ref.at[1], cols_ref.at[2])):
                high, low = split(part[...])
                ch_ref[slot * owned:(slot + 1) * owned, :] = high
                cl_ref[slot * owned:(slot + 1) * owned, :] = low
        for part in range(2):
            for m in range(1, inner):
                for source in [z] + outer_back:
                    block = at(source, returned(y, m, inner), core)
                    arrived(block, part)
                    forward(block, partner, part)
        for part in range(2):
            for source in [z] + outer_back:
                for m in range(inner):
                    arrived(at(source, y if m == 0 else returned(y, m, inner), 1 - core), part)

        for s in range(count):
            r_ref[s * owned:(s + 1) * owned, :] = (
                gat_ref[step, s, :owned, :] + gat_ref[step, (s - 1) % count, owned:, :]
            )
        coarse = product(ch_ref[...], cl_ref[...], r_ref[...])
        fill = jnp.zeros((padded - 2 * width - primal, columns), F32)

        def steps_of(slot):
            return jnp.concatenate([coarse[slot * owned:(slot + 2) * owned], fill], axis=0)

        q_before, q_own, q_after = steps_of(0), steps_of(1), steps_of(2)
        own = product(ah_ref[:2 * width, 2 * width:], al_ref[:2 * width, 2 * width:], q_own)
        if step == 0:
            for copy in a_copies:
                copy.wait()
        for copy in faces:
            copy.wait()
        after = product(*split(got_al[...]), q_after)
        lam = lam + DAMPING * ((values[:width] - own[:width]) - (got_l[step] - after))
        if step + 1 < ITERS:
            before = product(*split(got_ar[...]), q_before)
            lam_before = lam_before + DAMPING * ((got_r[step] - before) - (values[width:2 * width] - own[width:]))
        else:
            lam_ref[...] = lam
            q_ref[...] = q_own
        for copy in started:
            copy.wait_send()


def finish(pre_ref, kph_ref, kpl_ref, q_ref, lam_ref, u_ref, lam_out):
    u_ref[...] = pre_ref[...] - product(kph_ref[...], kpl_ref[...], q_ref[...])
    lam_out[...] = lam_ref[...]


NT = (((1,), (1,)), ((), ()))
NN = (((1,), (0,)), ((), ()))


def tall(x, high, low, dims):
    x_high, x_low = split(x)
    count = x.shape[0]
    both = lax.dot_general(jnp.concatenate([x_high, x_low], axis=0), high, dims, preferred_element_type=F32)
    return both[:count] + both[count:] + lax.dot_general(x_high, low, dims, preferred_element_type=F32)


def lanes_of(count):
    return -(-count // LANES) * LANES


def plane_kernel(
    count, primal, width, face_hbm, prim_hbm, slot_hbm, k_hbm, f_hbm, cinv_hbm, u_ref, lam_ref,
    face_s, prim_s, face_v, prim_v, slot_v, f_ref, k_ref, kh_ref, kl_ref, kph_ref, kpl_ref, e_ref, fh_ref, fl_ref, ks_ref,
    own_c, own_b, c_in, b_in, cinv_ref, cqh_ref, cql_ref, ac_ref, ap_ref, ar_ref, edge_ref,
    ach_ref, acl_ref, aph_ref, apl_ref, arh_ref, arl_ref, r_ref, face_out, face_in, x_out, x_in, q_out, q_in, lam_out, lam_in,
    in_sem, k_sem, c_sem, b_sem, cinv_send, cinv_recv, ac_send, ac_recv, ap_send, ap_recv, ar_send, ar_recv,
    halo_send, halo_recv, edge_sem, r_sem, face_sem, x_sem, q_sem, lam_sem,
):
    outer, inner = grid_of(count)
    plane = 2 * inner
    order, columns = f_ref.shape
    owned = primal // 2
    total = cinv_ref.shape[-1]
    tile = 256 if order % 256 == 0 else order
    tiles = order // tile
    share = columns // plane
    both = 2 * width
    wide = lanes_of(primal)
    span = r_ref.shape[-1]
    me = lax.axis_index("sub")
    mine = lax.rem(me, plane)
    z = me // plane
    core = lax.rem(me, 2)

    def at(z_, mine_):
        return z_ * plane + mine_

    partner = at(z, mine + 1 - 2 * core)
    across = [lax.rem(mine + 2 * m, plane) for m in range(1, inner)]
    across_peers = [at(z, other) for other in across]
    others = [lax.rem(mine + m, plane) for m in range(1, plane)]
    mates = [at(z, other) for other in others]
    turned = lax.rem(z, 2) if outer % 2 == 0 else 0

    def swapped(index, turn):
        return index + turn * (1 - 2 * lax.rem(index, 2))

    portion = swapped(mine, turned)

    def kin(place):
        return at(place, swapped(portion, lax.rem(place, 2) if outer % 2 == 0 else 0))

    beyond = [kin(lax.rem(z + m, outer)) for m in range(1, outer)]
    next_kin, last_kin = beyond[0], beyond[-1]
    after, before = [at(lax.rem(z + m, outer), mine) for m in (1, outer - 1)]
    far_first = beyond[::-1]
    if outer == 4:
        end = lax.rem(z + 1, outer) < 2
        mirror, skip, twin = outer - 1 - z, lax.rem(z + 2, outer), z + 1 - 2 * lax.rem(z, 2)
        far_first = [kin(place) for place in (jnp.where(end, mirror, skip), jnp.where(end, skip, mirror), twin)]

    def remote(src, dst, ssem, rsem, peer):
        return pltpu.make_async_remote_copy(
            src_ref=src, dst_ref=dst, send_sem=ssem, recv_sem=rsem, device_id={"sub": peer}, device_id_type=MESH
        )

    def send(src, dst, ssem, rsem, peer):
        remote(src, dst, ssem, rsem, peer).start()

    def arrived(ref, rsem):
        remote(ref, ref, r_sem.at[0, 0], rsem, partner).wait_recv()

    def sent(ref, ssem):
        remote(ref, ref, ssem, r_sem.at[0, 1], partner).wait_send()

    barrier = pltpu.get_barrier_semaphore()
    greeted = mates + beyond + ([after, before] if outer % 2 == 0 else [])
    for peer in greeted:
        pl.semaphore_signal(barrier, inc=1, device_id={"sub": peer}, device_id_type=MESH)

    ints = [
        pltpu.make_async_copy(src, dst, in_sem.at[i])
        for i, (src, dst) in enumerate((
            (face_hbm, face_s), (prim_hbm, prim_s), (face_hbm, face_v), (prim_hbm, prim_v), (slot_hbm, slot_v)
        ))
    ]
    cinv_copy = pltpu.make_async_copy(cinv_hbm, cinv_ref.at[mine + 1], in_sem.at[5])
    f_copy = pltpu.make_async_copy(f_hbm, f_ref, in_sem.at[6])

    def k_copy(c):
        rows = pl.ds(c * tile, tile)
        return pltpu.make_async_copy(k_hbm.at[rows, :], k_ref.at[rows, :], k_sem)

    for copy in ints + [cinv_copy, f_copy]:
        copy.start()
    for c in range(tiles):
        k_copy(c).start()

    with jax.named_scope("P_ints"):
        for copy in ints:
            copy.wait()
    square = (primal, primal)
    eye = lax.broadcasted_iota(jnp.int32, square, 0) == lax.broadcasted_iota(jnp.int32, square, 1)
    prim_col = jnp.sum(jnp.where(eye, prim_v[...].astype(F32), 0.0), axis=1, keepdims=True)
    slot_col = jnp.sum(jnp.where(eye, slot_v[...].astype(F32), 0.0), axis=1, keepdims=True)
    lane = lax.broadcasted_iota(jnp.int32, (primal, wide), 1).astype(F32)
    ordered = jnp.sum(jnp.where(slot_col == lane, prim_col + 1.0, 0.0), axis=0, keepdims=True) - 1.0
    ordering = jnp.where(lax.broadcasted_iota(jnp.int32, (wide, primal), 0) == slot_v[...], 1.0, 0.0).astype(BF16)

    def in_order(value):
        high, low = split(value)
        size = value.shape[1]
        pair = jnp.dot(ordering, jnp.concatenate([high, low], axis=1), preferred_element_type=F32)
        return pair[:, :size] + pair[:, size:]

    def one_hot_columns():
        right_ids, left_ids = face_v[0, 1:2, :], face_v[0, 0:1, :]
        ordered_ids = ordered.astype(jnp.int32)

        @pl.loop(0, tiles)
        def _(c):
            rows = pl.ds(pl.multiple_of(c * tile, tile), tile)
            near = lax.broadcasted_iota(jnp.int32, (tile, width), 0) + c * tile
            e_ref[rows, :width] = jnp.where(near == right_ids, 1.0, 0.0).astype(BF16)
            e_ref[rows, width:both] = jnp.where(near == left_ids, 1.0, 0.0).astype(BF16)
            near = lax.broadcasted_iota(jnp.int32, (tile, wide), 0) + c * tile
            e_ref[rows, both:] = jnp.where(near == ordered_ids, 1.0, 0.0).astype(BF16)

    def spread(buf, ssem, rsem, own):
        for peer in across_peers + [partner]:
            send(buf.at[own], buf.at[own], ssem, rsem.at[own], peer)

    def relay(buf, ssem, rsem):
        for other in across:
            arrived(buf.at[other], rsem.at[other])
            send(buf.at[other], buf.at[other], ssem, rsem.at[other], partner)

    def settle(buf, rsem):
        for other in [mine] + across:
            block = other + 1 - 2 * core
            arrived(buf.at[block], rsem.at[block])

    with jax.named_scope("P_onehot"):
        one_hot_columns()
    with jax.named_scope("P_barrier"):
        pl.semaphore_wait(barrier, len(greeted))
        cinv_copy.wait()
    halves = owned // 2

    def piece(block, half):
        return cinv_ref.at[block, pl.ds(half * halves, halves)]

    def send_far(half):
        send(piece(1 + core, half), piece(plane + 1 + core, half), halo_send.at[0], halo_recv.at[0, half], before)

    def send_near(half):
        send(piece(plane, half), piece(0, half), halo_send.at[1], halo_recv.at[1, half], after)

    def spread_coarse(half):
        for peer in across_peers + [partner]:
            rows = piece(mine + 1, half)
            send(rows, rows, cinv_send, cinv_recv.at[mine + 1, half], peer)

    def relay_coarse(half):
        for other in across:
            rows = piece(other + 1, half)
            arrived(rows, cinv_recv.at[other + 1, half])
            send(rows, rows, cinv_send, cinv_recv.at[other + 1, half], partner)
        pl.when(mine >= 2)(functools.partial(send_far, half))
        pl.when(mine == 1)(functools.partial(send_near, half))

    def settle_coarse():
        for half in range(2):
            for other in [mine] + across:
                block = other + 2 - 2 * core
                arrived(piece(block, half), cinv_recv.at[block, half])

    def last_edge():
        send(ac_ref.at[plane - 1, :, pl.ds(0, width)], edge_ref.at[0], edge_sem.at[0], edge_sem.at[1], after)

    def first_edge():
        send(ac_ref.at[0, :, pl.ds(width, width)], edge_ref.at[1], edge_sem.at[0], edge_sem.at[1], before)

    spread_coarse(0)
    for half in range(2):
        pl.when(mine < 2)(functools.partial(send_far, half))
        pl.when(mine == plane - 1)(functools.partial(send_near, half))
    with jax.named_scope("P_f"):
        f_copy.wait()
        high, low = split(f_ref[...])
        fh_ref[...] = high
        fl_ref[...] = low

    def halve(first_tile, last_tile):
        @pl.loop(first_tile, last_tile)
        def _(c):
            rows = pl.ds(pl.multiple_of(c * tile, tile), tile)
            high, low = split(k_ref[rows, :])
            kh_ref[rows, :] = high
            kl_ref[rows, :] = low

    with jax.named_scope("P_kwait"):
        pltpu.make_async_copy(k_hbm, k_ref, k_sem).wait()

    def picked(start, size, row_at):
        @pl.loop(0, size // 8)
        def _(i):
            base = pl.multiple_of(i * 8, 8)
            for j in range(8):
                ks_ref[pl.ds(start + base + j, 1), :] = k_ref[pl.ds(row_at(base + j), 1), :]

    def first(rows):
        high, low = split(ks_ref[rows, :])
        return product_parts(high, low, fh_ref[...], fl_ref[...])

    def columns_of(rows, picks):
        high, low = split(ks_ref[rows, :])
        return jnp.dot(high, picks, preferred_element_type=F32) + jnp.dot(low, picks, preferred_element_type=F32)

    def give(out, into, sems):
        for other, peer in zip(others, mates):
            send(out.at[swapped(other, turned)], into.at[mine], sems.at[0], sems.at[1], peer)
        into[mine] = out[portion]

    def give_back(out, into, sems):
        for other, peer in zip(others, mates):
            send(out.at[other], into.at[portion], sems.at[0], sems.at[1], peer)
        into[portion] = out[mine]

    def taken(into, sems):
        arrived(into.at[pl.ds(0, plane - 1)], sems.at[1])

    def assembled(parts):
        sums = None
        for i, part in enumerate(parts):
            part = jnp.concatenate([part, jnp.zeros((share, span - wide), F32)], axis=1)
            part = pltpu.roll(part, owned * i, 1) if i else part
            sums = part if sums is None else sums + part
        return sums

    def publish(step, parts):
        r_ref[step, z] = assembled(parts)
        for peer in far_first:
            rows = r_ref.at[step, z]
            send(rows, rows, r_sem.at[step, 0], r_sem.at[step, 1], peer)

    def faces(step, last_right, first_left):
        face_out[step, 0] = first_left
        send(face_out.at[step, 0], face_in.at[step, 0], face_sem.at[step, 0], face_sem.at[step, 1], last_kin)
        if step + 1 < ITERS:
            face_out[step, 1] = last_right
            send(face_out.at[step, 1], face_in.at[step, 1], face_sem.at[step, 0], face_sem.at[step, 1], next_kin)

    def face_part(ref, step):
        return ref.at[step] if step + 1 < ITERS else ref.at[step, pl.ds(0, 1)]

    rim = (mine == 0) | (mine == plane - 1)

    def urgent_half(block):
        return jnp.where(block == 0, 1, 0)

    def spread_half(half):
        for peer in across_peers + [partner]:
            rows = ar_ref.at[mine, half]
            send(rows, rows, ar_send, ar_recv.at[mine, half], peer)

    def relay_half(block, half):
        rows = ar_ref.at[block, half]
        arrived(rows, ar_recv.at[block, half])
        send(rows, rows, ar_send, ar_recv.at[block, half], partner)

    def spread_rows():
        half = urgent_half(mine)
        spread_half(half)
        spread_half(1 - half)

    def relay_urgent():
        relay_half(across[0], urgent_half(across[0]))

    def relay_whole():
        relay_half(across[0], 0)
        relay_half(across[0], 1)

    def relay_second():
        relay_half(across[0], 1 - urgent_half(across[0]))

    first_block = jnp.where(core == 0, plane - 1, 0)
    second_block = mine + across[0] + 2 - 4 * core - first_block

    def settle_half(block, half):
        arrived(ar_ref.at[block, half], ar_recv.at[block, half])

    with jax.named_scope("P_first"):
        picked(both, primal, lambda i: prim_s[0, i])
        own_c[...] = in_order(first(slice(both, both + primal))).T.reshape(own_c.shape)
        give(own_c, c_in, c_sem)
    spread_coarse(1)
    with jax.named_scope("P_pick"):
        picked(0, width, lambda i: face_s[0, 1, i])
        picked(width, width, lambda i: face_s[0, 0, i])
    with jax.named_scope("P_ac"):
        found = columns_of(slice(0, both), e_ref[:, both:])
        ac_ref[mine, :, :width] = found[:width].T[:primal]
        ac_ref[mine, :, width:] = found[width:].T[:primal]
        spread(ac_ref, ac_send, ac_recv, mine)
    with jax.named_scope("P_relayc0"):
        relay_coarse(0)
    with jax.named_scope("P_cwait"):
        taken(c_in, c_sem)
    publish(0, [c_in[i] for i in range(plane)])
    pl.when(mine == plane - 1)(last_edge)
    pl.when(mine == 0)(first_edge)
    with jax.named_scope("P_firstb"):
        loads = first(slice(0, both))
        own_b[:, :, :width] = loads[:width].T.reshape(plane, share, width)
        own_b[:, :, width:] = loads[width:].T.reshape(plane, share, width)
        give(own_b, b_in, b_sem)
    with jax.named_scope("P_relayc1"):
        relay_coarse(1)
    with jax.named_scope("P_ap"):
        ap_ref[mine] = in_order(columns_of(slice(both, both + primal), e_ref[:, :both]))[:primal]
        spread(ap_ref, ap_send, ap_recv, mine)
    with jax.named_scope("P_ar"):
        found = columns_of(slice(0, both), e_ref[:, :both])
        ar_ref[mine, 0] = found[:width]
        ar_ref[mine, 1] = found[width:]
        pl.when(rim)(spread_rows)
    with jax.named_scope("P_relayac"):
        relay(ac_ref, ac_send, ac_recv)
    pl.when(mine == 1)(last_edge)
    pl.when(mine == 2)(first_edge)
    with jax.named_scope("P_bwait"):
        taken(b_in, b_sem)
    faces(0, b_in[plane - 1, :, :width], b_in[0, :, width:])
    with jax.named_scope("P_halve"):
        halve(0, tiles)
    pl.when(jnp.logical_not(rim))(spread_rows)

    def primal_columns(first_tile, last_tile):
        picks = e_ref[:, both:]

        @pl.loop(first_tile, last_tile)
        def _(c):
            rows = pl.ds(pl.multiple_of(c * tile, tile), tile)
            kph_ref[rows, :] = jnp.dot(kh_ref[rows, :], picks, preferred_element_type=F32).astype(BF16)
            kpl_ref[rows, :] = jnp.dot(kl_ref[rows, :], picks, preferred_element_type=F32).astype(BF16)

    last_row = cqh_ref.shape[0]

    def coarse_rows(block, start):
        for ref, part in zip((cqh_ref, cql_ref), split(cinv_ref[block])):
            ref[start:start + owned, :] = part

    def halves_of(refs, src):
        for i in range(plane):
            for ref, part in zip(refs, split(src[i])):
                ref[i, :primal, :] = part
                ref[i, primal:, :] = jnp.zeros((wide - primal, both), BF16)

    early = tiles // 3
    sooner = jnp.where(mine == 1, early // 2, early)
    with jax.named_scope("P_halo"):
        settle_coarse()
        near = cinv_ref.at[0]
        for half in range(2):
            rows = piece(plane + 1 + core, half)
            arrived(rows, halo_recv.at[0, half])
            send(rows, rows, halo_send.at[0], halo_recv.at[3, half], partner)

        @pl.when(core == 1)
        def _():
            for half in range(2):
                arrived(piece(0, half), halo_recv.at[1, half])
            send(near, near, halo_send.at[1], halo_recv.at[2, 1], partner)

    with jax.named_scope("P_cq"):
        for ref in (cqh_ref, cql_ref):
            ref[plane * owned:, :] = jnp.zeros((last_row - plane * owned, total), BF16)
        for i in range(plane):
            coarse_rows(i + 1, i * owned)
    with jax.named_scope("P_settleac"):
        settle(ac_ref, ac_recv)
        halves_of((ach_ref, acl_ref), ac_ref)
    with jax.named_scope("P_edge0"):
        rows = edge_ref.at[1 - core]
        arrived(rows, edge_sem.at[1])
        send(rows, rows, edge_sem.at[3], edge_sem.at[2], partner)
    with jax.named_scope("P_relayap"):
        relay(ap_ref, ap_send, ap_recv)
    def coarse_halos():
        for half in range(2):
            arrived(piece(plane + 2 - core, half), halo_recv.at[3, half])

        @pl.when(core == 0)
        def _():
            arrived(near, halo_recv.at[2, 1])

        coarse_rows(plane + 1, plane * owned)
        coarse_rows(plane + 2, (plane + 1) * owned)
        coarse_rows(0, last_row - owned)

    def uncorrected(first_tile, last_tile):
        @pl.loop(first_tile, last_tile)
        def _(c):
            rows = pl.ds(pl.multiple_of(c * tile, tile), tile)
            u_ref[rows, :] = product_parts(kh_ref[rows, :], kl_ref[rows, :], fh_ref[...], fl_ref[...])

    def changed_loads():
        high, low = split(x_in[...].reshape(columns, both))
        moved = lax.dot_general(
            e_ref[:, :both], jnp.concatenate([high, low], axis=0), NT, preferred_element_type=F32
        )
        high, low = split(f_ref[...] + (moved[:, :columns] + moved[:, columns:]))
        fh_ref[...] = high
        fl_ref[...] = low

    def shifted(value, block):
        return (pltpu.roll(value, value.shape[1] - owned * block, 1) if block > 0 else pltpu.roll(
            value, owned, 1) if block else value)[:, :wide]

    def padded(value):
        return jnp.concatenate([value, jnp.zeros((wide - primal, value.shape[1]), F32)], axis=0)

    lam = [jnp.zeros((share, width), F32)] * (plane + 1)
    values = [b_in[i] for i in range(plane)]
    edges = None
    for step in range(ITERS):
        if step == ITERS - 1:
            with jax.named_scope("P_primcol1"):
                primal_columns(tiles - early, tiles)
            with jax.named_scope("P_xwait"):
                arrived(x_in.at[pl.ds(0, plane - 1)], x_sem.at[1])
                changed_loads()
            with jax.named_scope("P_uncorr0"):
                uncorrected(0, sooner)
        with jax.named_scope(f"P_rwait{step}"):
            arrived(r_ref.at[step, pl.ds(0, outer - 1)], r_sem.at[step, 1])
        with jax.named_scope(f"P_coarse{step}"):
            sums = None
            for i in range(outer):
                part = jnp.concatenate([r_ref[step, i], jnp.zeros((share, total - span), F32)], axis=1)
                part = pltpu.roll(part, plane * owned * i, 1) if i else part
                sums = part if sums is None else sums + part
            if step:
                coarse = tall(sums, cqh_ref[...], cql_ref[...], NT)
                moved = []
            else:
                own = tall(sums, cqh_ref[:lanes_of(plane * owned)], cql_ref[:lanes_of(plane * owned)], NT)
                moved = [values[i] - tall(shifted(own, i), ach_ref[i], acl_ref[i], NN) for i in range(plane - 1)]
                with jax.named_scope("P_halo2"):
                    coarse_halos()
                low_row = (plane - 1) * owned // LANES * LANES
                rest = tall(sums, cqh_ref[low_row:], cql_ref[low_row:], NT)
                coarse = jnp.concatenate([own[:, :low_row], rest], axis=1)
            steps = [shifted(coarse, i - 1) for i in range(plane + 2)]
            if step == ITERS - 1:
                for i in range(plane):
                    q_out[i] = steps[i + 1]
                give_back(q_out, q_in, q_sem)
        if edges is None:
            with jax.named_scope("P_edge"):
                arrived(edge_ref.at[core], edge_sem.at[2])
                edges = [split(padded(edge_ref[i])) for i in range(2)]
        with jax.named_scope(f"P_faces{step}"):
            arrived(face_part(face_in, step), face_sem.at[step, 1])
        with jax.named_scope(f"P_update{step}"):
            moved += [values[i] - tall(steps[i + 1], ach_ref[i], acl_ref[i], NN) for i in range(len(moved), plane)]
            right = [part[:, :width] for part in moved]
            left = [part[:, width:] for part in moved]
            left.append(face_in[step, 0] - tall(steps[plane + 1], *edges[1], NN))
            lam_next = [lam[i + 1] + DAMPING * (right[i] - left[i + 1]) for i in range(plane)]
            if step + 1 < ITERS:
                ahead = face_in[step, 1] - tall(steps[0], *edges[0], NN)
                lam_next = [lam[0] + DAMPING * (ahead - left[0])] + lam_next
            else:
                for i in range(plane):
                    lam_out[i] = lam_next[i]
                give_back(lam_out, lam_in, lam_sem)
                break
            lam = lam_next
            if step == 0:
                with jax.named_scope("P_settleap"):
                    settle(ap_ref, ap_recv)
                    halves_of((aph_ref, apl_ref), ap_ref)
            changes = [jnp.concatenate([-lam[i + 1], lam[i]], axis=1) for i in range(plane)]
            if step == ITERS - 2:
                for i in range(plane):
                    x_out[i] = changes[i]
                give_back(x_out, x_in, x_sem)
            publish(step + 1, [
                c_in[i] + tall(changes[i], aph_ref[i], apl_ref[i], NT) for i in range(plane)
            ])
        if step == 0:
            with jax.named_scope("P_relayr0"):
                pl.when(jnp.logical_not(rim))(relay_urgent)
                settle_half(first_block, urgent_half(first_block))
                for i, half in ((plane - 1, 0), (0, 1)):
                    rows = slice(half * width, (half + 1) * width)
                    for ref, part in zip((arh_ref, arl_ref), split(ar_ref[i, half])):
                        ref[i, rows] = part
            with jax.named_scope("P_facevalues"):
                last_right = tall(changes[-1], arh_ref[plane - 1, :width], arl_ref[plane - 1, :width], NT)
                first_left = tall(changes[0], arh_ref[0, width:], arl_ref[0, width:], NT)
                faces(1, b_in[plane - 1, :, :width] + last_right, b_in[0, :, width:] + first_left)
            with jax.named_scope("P_primcol0"):
                primal_columns(0, early)
            with jax.named_scope("P_relayr1"):
                pl.when(rim)(relay_whole)
                pl.when(jnp.logical_not(rim))(relay_second)
            with jax.named_scope("P_primcol0"):
                primal_columns(early, tiles - early)
            with jax.named_scope("P_settler1"):
                settle_half(first_block, 1 - urgent_half(first_block))
                settle_half(second_block, 0)
                settle_half(second_block, 1)
                for i in range(plane):
                    for half in range(2):
                        if (i, half) not in ((plane - 1, 0), (0, 1)):
                            rows = slice(half * width, (half + 1) * width)
                            for ref, part in zip((arh_ref, arl_ref), split(ar_ref[i, half])):
                                ref[i, rows] = part
        with jax.named_scope(f"P_values{step}"):
            values = [b_in[i] + tall(changes[i], arh_ref[i], arl_ref[i], NT) for i in range(plane)]
            if step:
                faces(step + 1, values[plane - 1][:, :width], values[0][:, width:])

    with jax.named_scope("P_uncorr1"):
        uncorrected(sooner, tiles)
    with jax.named_scope("P_qwait"):
        arrived(q_in.at[pl.ds(0, plane - 1)], q_sem.at[1])
    with jax.named_scope("P_last"):
        high, low = split(q_in[...].reshape(columns, wide).T)
        pair = jnp.concatenate([high, low], axis=1)
        for c in range(tiles):
            rows = pl.ds(c * tile, tile)
            step = jnp.dot(kph_ref[rows, :], pair, preferred_element_type=F32)
            step = step[:, :columns] + step[:, columns:]
            u_ref[rows, :] = u_ref[rows, :] - (step + jnp.dot(kpl_ref[rows, :], high, preferred_element_type=F32))

    with jax.named_scope("P_lamwait"):
        arrived(lam_in.at[pl.ds(0, plane - 1)], lam_sem.at[1])
        lam_ref[...] = lam_in[...].reshape(columns, width).T
    with jax.named_scope("P_sent"):
        others_part = pl.ds(0, plane - 1)
        sent(own_c.at[others_part], c_sem.at[0])
        sent(own_b.at[others_part], b_sem.at[0])
        sent(cinv_ref.at[others_part], cinv_send)
        for ref, sem in ((ac_ref, ac_send), (ap_ref, ap_send), (ar_ref, ar_send)):
            sent(ref.at[others_part], sem)
        sent(cinv_ref.at[pl.ds(0, 2)], halo_send.at[0])

        @pl.when(core == 1)
        def _():
            sent(cinv_ref.at[pl.ds(0, 2)], halo_send.at[1])

        sent(edge_ref.at[0], edge_sem.at[0])
        sent(edge_ref.at[0], edge_sem.at[3])
        for step in range(ITERS):
            sent(r_ref.at[step, pl.ds(0, outer - 1)], r_sem.at[step, 0])
            sent(face_part(face_out, step), face_sem.at[step, 0])
        sent(x_out.at[others_part], x_sem.at[0])
        sent(q_out.at[others_part], q_sem.at[0])
        sent(lam_out.at[others_part], lam_sem.at[0])


def plane_finish(u_ref, lam_ref, u_hbm, lam_hbm, sem):
    copies = [pltpu.make_async_copy(u_ref, u_hbm, sem.at[0]), pltpu.make_async_copy(lam_ref, lam_hbm, sem.at[1])]
    for copy in copies:
        copy.start()
    for copy in copies:
        copy.wait()


def size_of(buffers):
    return sum((4 if kind == F32 else 2) * functools.reduce(lambda a, b: a * b, size) for size, kind in buffers)


def plane_scratch(count, order, columns, owned, total, width, primal):
    outer, inner = grid_of(count)
    plane = 2 * inner
    both = 2 * width
    wide = lanes_of(primal)
    span = lanes_of((plane + 1) * owned)
    share = columns // plane
    pairs = lanes_of((plane + 3) * owned)
    return plane, [
        ((order, columns), F32),
        ((order, order), F32),
        ((order, order), BF16),
        ((order, order), BF16),
        ((order, wide), BF16),
        ((order, wide), BF16),
        ((order, both + wide), BF16),
        ((order, columns), BF16),
        ((order, columns), BF16),
        ((both + primal, order), F32),
        ((plane, share, wide), F32),
        ((plane, share, both), F32),
        ((plane, share, wide), F32),
        ((plane, share, both), F32),
        ((plane + 3, owned, total), F32),
        ((pairs, total), BF16),
        ((pairs, total), BF16),
        ((plane, primal, both), F32),
        ((plane, primal, both), F32),
        ((plane, 2, width, both), F32),
        ((2, primal, width), F32),
        ((plane, wide, both), BF16),
        ((plane, wide, both), BF16),
        ((plane, wide, both), BF16),
        ((plane, wide, both), BF16),
        ((plane, both, both), BF16),
        ((plane, both, both), BF16),
        ((ITERS, outer, share, span), F32),
        ((ITERS, 2, share, width), F32),
        ((ITERS, 2, share, width), F32),
        ((plane, share, both), F32),
        ((plane, share, both), F32),
        ((plane, share, wide), F32),
        ((plane, share, wide), F32),
        ((plane, share, width), F32),
        ((plane, share, width), F32),
    ]


def planar(condensed, eigen_loads, coarse_inverse, face_rows, primal_rows, primal_slot):
    count = lax.axis_size("sub")
    order, columns = eigen_loads.shape
    owned, total = coarse_inverse.shape
    width = face_rows.shape[2]
    primal = primal_rows.shape[1]
    outer, inner = grid_of(count)
    tile = 256 if order % 256 == 0 else order
    tiles = order // tile
    plane, buffers = plane_scratch(count, order, columns, owned, total, width, primal)
    needed = size_of(buffers)
    wide = lanes_of(primal)
    dma = pltpu.SemaphoreType.DMA
    vmem = pl.BlockSpec(memory_space=pltpu.VMEM)
    shape = jax.ShapeDtypeStruct
    held = [
        pltpu.with_memory_space_constraint(value, pltpu.HBM)
        for value in (face_rows, primal_rows, primal_slot, condensed, eigen_loads, coarse_inverse)
    ]
    parts = pl.pallas_call(
        functools.partial(plane_kernel, count, primal, width),
        out_shape=(
            shape((order, columns), F32),
            shape((width, columns), F32),
        ),
        in_specs=[pl.BlockSpec(memory_space=pltpu.HBM)] * 6,
        out_specs=(vmem,) * 2,
        scratch_shapes=[
            pltpu.SMEM(face_rows.shape, jnp.int32),
            pltpu.SMEM(primal_rows.shape, jnp.int32),
            pltpu.VMEM(face_rows.shape, jnp.int32),
            pltpu.VMEM(primal_rows.shape, jnp.int32),
            pltpu.VMEM(primal_slot.shape, jnp.int32),
        ] + [pltpu.VMEM(size, kind) for size, kind in buffers] + [
            dma((7,)),
            dma(()),
            dma((2,)),
            dma((2,)),
            dma(()),
            dma((plane + 1, 2)),
            dma(()),
            dma((plane,)),
            dma(()),
            dma((plane,)),
            dma(()),
            dma((plane, 2)),
            dma((2,)),
            dma((4, 2)),
            dma((4,)),
            dma((ITERS, 2)),
            dma((ITERS, 2)),
            dma((2,)),
            dma((2,)),
            dma((2,)),
        ],
        compiler_params=pltpu.CompilerParams(
            collective_id=0, has_side_effects=True, vmem_limit_bytes=min(PLANE_LIMIT, needed + needed // 3)
        ),
    )(*held)
    return pl.pallas_call(
        plane_finish,
        out_shape=(shape((order, columns), F32), shape((width, columns), F32)),
        in_specs=[vmem] * 2,
        out_specs=(pl.BlockSpec(memory_space=pltpu.HBM),) * 2,
        scratch_shapes=[dma((2,))],
        compiler_params=pltpu.CompilerParams(vmem_limit_bytes=4 * order * columns * 4),
    )(*parts)


def fits_plane(condensed, eigen_loads, coarse_inverse, face_rows, primal_rows, primal_slot):
    count = lax.axis_size("sub")
    order, columns = eigen_loads.shape
    owned, total = coarse_inverse.shape
    width = face_rows.shape[2]
    primal = primal_rows.shape[1]
    outer, inner = grid_of(count)
    plane = 2 * inner
    if outer < 2 or inner != 2 or columns % (8 * plane) or total % LANES or width % LANES or owned % 16 or primal != 2 * owned:
        return False
    _, buffers = plane_scratch(count, order, columns, owned, total, width, primal)
    return size_of(buffers) <= PLANE_LIMIT * 3 // 4


def local(*values):
    return (planar if fits_plane(*values) else general)(*values)


def general(condensed, eigen_loads, coarse_inverse, face_rows, primal_rows, primal_slot):
    count = lax.axis_size("sub")
    order, columns = eigen_loads.shape
    owned, total = coarse_inverse.shape
    width = face_rows.shape[2]
    primal = primal_rows.shape[1]
    padded = 2 * width + -(-primal // LANES) * LANES
    outer, inner = grid_of(count)
    corner_width = padded - 2 * width
    tile = 256 if order % 256 == 0 else order
    sends = (outer - 1) + (inner - 1) * outer + outer * inner
    dma = pltpu.SemaphoreType.DMA
    vmem = pl.BlockSpec(memory_space=pltpu.VMEM)
    face = pltpu.VMEM((ITERS, width, columns), F32)
    corner = pltpu.VMEM((width, padded - 2 * width), F32)
    smem = pl.BlockSpec(memory_space=pltpu.SMEM)
    needed = 8 * order * (order + padded + 2 * columns) + 4 * padded * (order + columns + padded)
    needed += 4 * owned * total * 8 + 4 * columns * (ITERS * (count * primal + 4 * width) + total)
    needed += 4 * order * (columns + 2 * corner_width) + 4 * columns * (order + 8 * width)
    shape = jax.ShapeDtypeStruct
    held = [
        pltpu.with_memory_space_constraint(value, pltpu.HBM)
        for value in (face_rows, primal_rows, primal_slot, condensed, eigen_loads, coarse_inverse)
    ]
    parts = pl.pallas_call(
        functools.partial(kernel, count, primal, width),
        out_shape=(
            shape((order, columns), F32),
            shape((order, corner_width), BF16),
            shape((order, corner_width), BF16),
            shape((corner_width, columns), F32),
            shape((width, columns), F32),
        ),
        in_specs=[smem, smem] + [pl.BlockSpec(memory_space=pltpu.HBM)] * 6,
        out_specs=(vmem,) * 5,
        scratch_shapes=[
            pltpu.VMEM(face_rows.shape, jnp.int32),
            pltpu.VMEM(primal_rows.shape, jnp.int32),
            pltpu.VMEM(primal_slot.shape, jnp.int32),
            pltpu.VMEM((order, columns), F32),
            pltpu.VMEM((owned, total), F32),
            dma((5,)),
            pltpu.VMEM((order, order), F32),
            pltpu.VMEM((order, order), BF16),
            pltpu.VMEM((order, order), BF16),
            pltpu.VMEM((order, padded), BF16),
            pltpu.VMEM((order, columns), BF16),
            pltpu.VMEM((order, columns), BF16),
            pltpu.VMEM((padded, order), F32),
            pltpu.VMEM((padded, columns), F32),
            pltpu.VMEM((padded, padded), BF16),
            pltpu.VMEM((padded, padded), BF16),
            pltpu.VMEM((3, owned, total), F32),
            pltpu.VMEM((4 * owned, total), BF16),
            pltpu.VMEM((4 * owned, total), BF16),
            pltpu.VMEM((ITERS, count, primal, columns), F32),
            pltpu.VMEM((total, columns), F32),
            face, face, face, face,
            corner, corner, corner, corner,
            dma((order // tile,)),
            dma((ITERS, 2 * sends)),
            dma((ITERS, count, 2)),
            dma((2, ITERS, 2)),
            dma((3,)),
            dma((3,)),
            dma((2,)),
            dma((2,)),
        ],
        compiler_params=pltpu.CompilerParams(
            collective_id=0, has_side_effects=True, vmem_limit_bytes=min(VMEM_LIMIT, needed + needed // 4)
        ),
    )(face_rows, primal_rows, *held)
    return pl.pallas_call(
        finish,
        out_shape=(shape((order, columns), F32), shape((width, columns), F32)),
        in_specs=[vmem] * 5,
        out_specs=(vmem, vmem),
        compiler_params=pltpu.CompilerParams(vmem_limit_bytes=4 * order * columns * 8),
    )(*parts)


def solution(mesh):
    placed = (
        P(("rve", "sub"), None),
        P(("rve", "sub"), None),
        P(("rve", "sub"), None),
        P("sub", None, None),
        P("sub", None),
        P("sub", None),
    )
    return jax.shard_map(
        local,
        mesh=mesh,
        in_specs=placed,
        out_specs=(P(("rve", "sub"), None), P(("rve", "sub"), None)),
        check_vma=False,
    )
```
